32 devices in a mesh: dp: 8 (over z, core), mp: 4 (over y, x).
Axes of the slice: x: 2, y: 2, z: 4, core: 2. Of those that a mesh axis runs over, the one named last changes fastest.
Arguments:
- tokens: bfloat16 [65536, 1024], P('dp'), may hold values from -7 to 7
- segments: int32 [64, 1024], P('dp'), may hold values from 0 to 3, never falling along the last dimension, each value on 1 to 512 neighbouring positions
- routes: int32 [64, 128], P('dp'), may hold values from 0 to 1023, as said below
- cotangent: bfloat16 [65536, 1024], P('dp'), may hold values from -6 to 6
- gain_attn: bfloat16 [1024], replicated, may hold values from 0.5 to 1.5
- gain_mlp: bfloat16 [1024], replicated, may hold values from 0.5 to 1.5
- w_router: bfloat16 [1024], replicated, may hold values from -1 to 1
- w_qkv: bfloat16 [1024, 3072], P(None, 'mp'), may hold values from -0.1875 to 0.1875
- w_out: bfloat16 [1024, 1024], P('mp'), may hold values from -0.75 to 0.75
- w_up: bfloat16 [1024, 4096], P(None, 'mp'), may hold values from -0.1875 to 0.1875
- w_down: bfloat16 [4096, 1024], P('mp'), may hold values from -0.09375 to 0.09375
Outputs:
- output: bfloat16 [65536, 1024], P('dp')
- grad_tokens: bfloat16 [65536, 1024], P('dp')
- grad_gain_attn: float32 [1024], replicated
- grad_gain_mlp: float32 [1024], replicated
- grad_router: float32 [1024], replicated
- grad_qkv: float32 [1024, 3072], P(None, 'mp')
- grad_out: float32 [1024, 1024], P('mp')
- grad_up: float32 [1024, 4096], P(None, 'mp')
- grad_down: float32 [4096, 1024], P('mp')
- routed_share: float32 [], replicated
- mean_score: float32 [], replicated
The draws below stay inside these ranges and needn't reach their ends.
Inputs may be any that keep to these rules, and one draw needn't show every extreme that they name: `routes`: each row holds 128 different positions of its sequence in ascending order, the first 0 and the last 1023. The segment numbers of one sequence never fall; each of the 4 segments has 1 to 512 positions, one exactly 512.
All inputs are finite; a program needn't handle non-finite values.
Results may differ from the reference program's by a relative error of at most 0.012.
Values may be sent and summed in bfloat16 or wider, within the bound.
No kernel may reach another device: no remote copies, remote signals or barrier semaphores. Data moves between devices by JAX's collectives and lax.ppermute only.
A program may use at most 256 MiB of HBM per device.

```python
import math
import jax
import jax.numpy as jnp
import numpy as np
from jax import lax

D = 1024
H = 16
HD = 64
FF = 4096
LEN = 1024
SEGS = 4
ROUTED = 128
SEQS = 64
TOKENS = 65536


def draw_routes(key, part):
    seq_keys = jax.random.split(key, SEQS)

    def one_row(row_key):
        shuffled = jax.random.permutation(row_key, LEN - 2) + 1
        return shuffled[:ROUTED - 2]
    chosen = jax.vmap(one_row)(seq_keys).astype(jnp.int32)
    starts = jnp.zeros((SEQS, 1), jnp.int32)
    combined = jnp.concatenate([starts, chosen, starts + (LEN - 1)], axis=1)
    return jnp.sort(combined, axis=1).astype(jnp.int32)


def router_direction(key):
    return jnp.clip(jax.random.normal(jax.random.fold_in(key, 7), (D,), jnp.float32), -4.0, 4.0)


def draw_w_router(key, part):
    return (router_direction(key) / D ** 0.5).astype(jnp.bfloat16)


def draw_tokens(key, part):
    direction = router_direction(key)
    base_key = jax.random.fold_in(key, 11)
    base = jnp.clip(jax.random.normal(base_key, (TOKENS, D), jnp.float32), -6.0, 6.0)
    amp = 3.0
    seq_pos = (lax_rows(TOKENS) // LEN).astype(jnp.float32) / max(SEQS - 1, 1)
    coeff = amp * (seq_pos - 0.5) / D ** 0.5
    return (base + coeff[:, None] * direction[None, :]).astype(jnp.bfloat16)


def lax_rows(count):
    return jnp.arange(count, dtype=jnp.int32)


def levels(rng, dims, shards, smallest, top_value):
    gain = 1.0
    for axis_at, shards_of in shards:
        heights = jax.random.uniform(jax.random.fold_in(jax.random.fold_in(rng, 6), axis_at), (shards_of,), jnp.float32, smallest / len(shards), top_value / len(shards))
        gain = gain * jnp.repeat(jnp.exp(heights), dims[axis_at] // shards_of).reshape((-1,) + (1,) * (len(dims) - 1 - axis_at))
    return gain


def length_profile(count, total, bound, slope):
    loads = [(1 << 20) // math.isqrt(grade ** slope) + 1 for grade in range(2, count + 1)]
    spare, holding = total - bound - (count - 1), [1] * (count - 1)
    while spare > 0:
        candidates = [i for i in range(count - 1) if holding[i] < bound]
        whole, left = sum([loads[i] for i in candidates]), spare
        for i in candidates:
            more = min(bound - holding[i], max(1, left * loads[i] // whole), spare)
            holding[i] = holding[i] + more
            spare = spare - more
    return np.array([bound] + holding)


def ragged(stream_key, amount, total, reach, lean):
    if amount == 2:
        one = jax.random.randint(stream_key, (), max(1, total - reach), min(reach, total - 1) + 1)
        return jnp.stack([one, total - one])
    sizes = jnp.asarray(length_profile(amount, total, reach, lean), jnp.int32)
    twos = (amount - 1) // 2
    donor, taker = sizes[1:1 + 2 * twos:2], sizes[2:2 + 2 * twos:2]
    slack = jnp.minimum(donor - 1, reach - taker)
    passed = jax.random.randint(jax.random.fold_in(stream_key, 1), (twos,), 0, 1 << 20) % (slack + 1)
    sizes = sizes.at[1:1 + 2 * twos:2].set(donor - passed).at[2:2 + 2 * twos:2].set(taker + passed)
    return sizes[jax.random.permutation(jax.random.fold_in(stream_key, 2), amount)]


def gaussian(own_key, extent, deviation, reach, pieces=(), kind=jnp.bfloat16):
    entries = jax.random.normal(own_key, extent, jnp.float32) * deviation
    if len(pieces) > 0:
        entries = levels(own_key, extent, pieces, -0.22, 0.18) * entries
    return jnp.clip(entries, min=-reach, max=reach).astype(kind)


def setup_inputs(seed: int = 0) -> dict:
    splits = jax.random.split(jax.random.key(seed), 12)
    return {
        "tokens": draw_tokens(jax.random.fold_in(splits[11], 71), 0),
        "segments": jax.vmap(lambda own: jnp.searchsorted(jnp.cumsum(ragged(own, SEGS, LEN, LEN // 2, 0)), jnp.arange(LEN), side="right"))(jax.random.split(splits[1], SEQS)).reshape((SEQS, LEN)).astype(jnp.int32),
        "routes": draw_routes(jax.random.fold_in(splits[11], 71), 0),
        "cotangent": gaussian(splits[3], (TOKENS, D), 1.0, 6.0, ((0, 8),)),
        "gain_attn": jnp.clip(1.0 + 0.1 * jax.random.normal(splits[4], (D,), jnp.float32), 0.5, 1.5).astype(jnp.bfloat16),
        "gain_mlp": jnp.clip(1.0 + 0.1 * jax.random.normal(splits[5], (D,), jnp.float32), 0.5, 1.5).astype(jnp.bfloat16),
        "w_router": draw_w_router(jax.random.fold_in(splits[11], 71), 0),
        "w_qkv": gaussian(splits[7], (D, 3 * H * HD), D ** -0.5, 0.1875, ((1, 4),)),
        "w_out": gaussian(splits[8], (H * HD, D), (H * HD // 16) ** -0.5, 0.75, ((0, 4),)),
        "w_up": gaussian(splits[9], (D, FF), D ** -0.5, 0.1875, ((1, 4),)),
        "w_down": gaussian(splits[10], (FF, D), FF ** -0.5, 0.09375, ((0, 4),)),
    }


@jax.custom_vjp
def low(v):
    return lax.optimization_barrier(v.astype(jnp.bfloat16)).astype(jnp.float32)

@jax.custom_vjp
def low_back(v):
    return v

def low_keep(v):
    return (low(v), None)

def low_pass(kept, grad):
    return (grad,)

def back_keep(v):
    return (v, None)

def back_low(kept, grad):
    return (low(grad),)
low.defvjp(low_keep, low_pass)
low_back.defvjp(back_keep, back_low)

def rms_scale(inputs, gain_vec):
    inverse = lax.rsqrt(lax.optimization_barrier(jnp.mean(inputs * inputs, axis=-1, keepdims=True)) + 1e-06)
    return inputs * inverse * gain_vec

def forward(frames, gain_attn, gain_mlp, w_router, w_qkv, w_out, w_up, w_down, segments, routes):
    highest = lax.Precision.HIGHEST
    seq_count = frames.shape[0]
    logits = jnp.einsum('std,d->st', frames, w_router, precision=highest)
    scores = jax.nn.sigmoid(logits)
    rows_routed = jnp.take_along_axis(frames, routes[:, :, None], axis=1)
    rate_routed = jnp.take_along_axis(scores, routes, axis=1)
    seg_routed = jnp.take_along_axis(segments, routes, axis=1)
    normed_one = low(rms_scale(rows_routed, gain_attn))
    joint_qkv = low(low_back(jnp.einsum('skd,dc->skc', normed_one, w_qkv, precision=highest)))
    joint_qkv = joint_qkv.reshape(seq_count, ROUTED, H, 3, HD)
    queries = joint_qkv[:, :, :, 0]
    key_rows = joint_qkv[:, :, :, 1]
    values = joint_qkv[:, :, :, 2]
    raw_scores = jnp.einsum('sqhe,skhe->shqk', queries, key_rows, precision=highest) * HD ** (-0.5)
    causal = lax.broadcasted_iota(jnp.int32, (ROUTED, ROUTED), 0) >= lax.broadcasted_iota(jnp.int32, (ROUTED, ROUTED), 1)
    allowed = causal[None, None] & (seg_routed[:, None, :, None] == seg_routed[:, None, None, :])
    masked = jnp.where(allowed, low_back(raw_scores), -1e+30)
    weights_low = low(jax.nn.softmax(masked, axis=-1))
    mixed = jnp.einsum('shqk,skhe->sqhe', weights_low, values, precision=highest).reshape(seq_count, ROUTED, H * HD)
    heads_out = low(low_back(mixed))
    attended = low_back(jnp.einsum('skc,cd->skd', heads_out, w_out, precision=highest))
    middle = rows_routed + attended
    normed_two = low(rms_scale(middle, gain_mlp))
    pre_act = low_back(jnp.einsum('skd,df->skf', normed_two, w_up, precision=highest))
    hidden = low(jax.nn.gelu(pre_act))
    mlp_out = low_back(jnp.einsum('skf,fd->skd', hidden, w_down, precision=highest))
    updated = rows_routed + rate_routed[:, :, None] * (attended + mlp_out)
    seq_index = jnp.arange(seq_count)[:, None]
    result = frames.at[seq_index, routes].set(updated)
    return (result, scores)

def reference(tokens, segments, routes, cotangent, gain_attn, gain_mlp, w_router, w_qkv, w_out, w_up, w_down):
    frames = tokens.astype(jnp.float32).reshape(SEQS, LEN, D)
    params = [weight_in.astype(jnp.float32) for weight_in in (gain_attn, gain_mlp, w_router, w_qkv, w_out, w_up, w_down)]

    def wrapped(*arrays):
        return forward(*arrays, segments, routes)
    result, pullback, scores = jax.vjp(wrapped, frames, *params, has_aux=True)
    gradients = pullback(cotangent.astype(jnp.float32).reshape(SEQS, LEN, D))
    picked = jnp.take_along_axis(scores, routes, axis=1)
    routed_share = jnp.sum(picked) / jnp.sum(scores)
    mean_score = jnp.mean(scores)
    return (result.reshape(TOKENS, D).astype(jnp.bfloat16), gradients[0].reshape(TOKENS, D).astype(jnp.bfloat16), gradients[1], gradients[2], gradients[3], gradients[4], gradients[5], gradients[6], gradients[7], routed_share, mean_score)
```

```python
import functools

import jax
import jax.numpy as jnp
from jax import lax
from jax.experimental import pallas as pl
from jax.experimental.pallas import tpu as pltpu
from jax.sharding import PartitionSpec as P

HD = 64
EPS = 1e-06
SCALE = HD ** (-0.5)
GELU_C = (2.0 / 3.141592653589793) ** 0.5
GELU_A = 0.044715
F32 = jnp.float32
BF16 = jnp.bfloat16


def dot(left, right, on=((1,), (0,))):
    return lax.dot_general(left, right, (on, ((), ())), preferred_element_type=F32)


NT = ((1,), (1,))
TN = ((0,), (0,))


def iota(shape, axis):
    return lax.broadcasted_iota(jnp.int32, shape, axis)


def sigmoid(value):
    return 1.0 / (1.0 + jnp.exp(-value))


def call(body, grid, in_specs, out_specs, out_shape, flops, nbytes, name, scratch=(), alias=None):
    return pl.pallas_call(
        body,
        grid_spec=pltpu.PrefetchScalarGridSpec(
            num_scalar_prefetch=1,
            grid=grid,
            in_specs=in_specs,
            out_specs=out_specs,
            scratch_shapes=list(scratch),
        ),
        out_shape=out_shape,
        cost_estimate=pl.CostEstimate(
            flops=int(flops), bytes_accessed=int(nbytes), transcendentals=0
        ),
        input_output_aliases=alias or {},
        name=name,
    )


def whole(shape):
    zeros = (0,) * len(shape)
    return pl.BlockSpec(shape, lambda *_: zeros)


def one_hot_rows(routes_row, length):
    routed = routes_row.shape[1]
    eye = iota((routed, routed), 0) == iota((routed, routed), 1)
    column = jnp.sum(jnp.where(eye, routes_row.astype(F32), 0.0), axis=1, keepdims=True)
    return iota((routed, length), 1) == column.astype(jnp.int32), eye


def head_mask(hot, eye, seg_line):
    seg_col = jnp.sum(jnp.where(hot, seg_line, 0.0), axis=1, keepdims=True)
    seg_row = jnp.sum(jnp.where(eye, seg_col, 0.0), axis=0, keepdims=True)
    routed = eye.shape[0]
    causal = iota((routed, routed), 0) >= iota((routed, routed), 1)
    return causal & (seg_col == seg_row)


def softmax_head(query, key, allowed):
    logits = jnp.where(allowed, dot(query, key, NT) * SCALE, -1e30)
    expon = jnp.exp(logits - jnp.max(logits, axis=1, keepdims=True))
    return expon / jnp.sum(expon, axis=1, keepdims=True)


def front_body(
    heads, slice_rows, where, tokens, routes, segments, gain, router, w_qkv,
    xr_out, a1_out, qkv_out, mask_out, mixed_out, score_out,
):
    step = pl.program_id(0)
    length = tokens.shape[0]
    hot, eye = one_hot_rows(routes[pl.ds(step, 1), :], length)
    seg_line = segments[pl.ds(step, 1), :].astype(F32)
    allowed = head_mask(hot, eye, seg_line)
    mask_out[...] = jnp.where(allowed, 1.0, 0.0).astype(BF16)
    rows = dot(jnp.where(hot, 1.0, 0.0).astype(BF16), tokens[...])
    xr_out[...] = rows.astype(BF16)
    vec = router[...].astype(F32)
    start = pl.multiple_of(where[0] * slice_rows, slice_rows)
    part = tokens[pl.ds(start, slice_rows), :].astype(F32)
    total = jnp.sum(sigmoid(jnp.sum(part * vec, axis=1, keepdims=True)), axis=0, keepdims=True)
    chosen = jnp.sum(sigmoid(jnp.sum(rows * vec, axis=1, keepdims=True)), axis=0, keepdims=True)

    @pl.when(step == 0)
    def _():
        score_out[...] = jnp.zeros_like(score_out)

    which = iota(score_out.shape, 0)
    score_out[...] += jnp.where(which == 0, total, jnp.where(which == 1, chosen, 0.0))
    inverse = lax.rsqrt(jnp.mean(rows * rows, axis=1, keepdims=True) + EPS)
    normed = (rows * inverse * gain[...].astype(F32)).astype(BF16)
    a1_out[...] = normed
    joint = dot(normed, w_qkv[...]).astype(BF16)
    qkv_out[...] = joint
    for head in range(heads):
        base = head * 3 * HD
        query = joint[:, base : base + HD]
        key = joint[:, base + HD : base + 2 * HD]
        value = joint[:, base + 2 * HD : base + 3 * HD]
        probs = softmax_head(query, key, allowed).astype(BF16)
        mixed_out[:, head * HD : (head + 1) * HD] = dot(probs, value).astype(BF16)


def cot_body(where, cotangent, routes, xr, router, w_down, dyr_out, gm_out, dh_out):
    step = pl.program_id(0)
    hot, _ = one_hot_rows(routes[pl.ds(step, 1), :], cotangent.shape[0])
    rows = dot(jnp.where(hot, 1.0, 0.0).astype(BF16), cotangent[...])
    dyr_out[...] = rows.astype(BF16)
    vec = router[...].astype(F32)
    rate = sigmoid(jnp.sum(xr[...].astype(F32) * vec, axis=1, keepdims=True))
    low = (rate * rows).astype(BF16)
    gm_out[...] = low
    dh_out[...] = dot(low, w_down[...], NT)


def middle_body(parts, table, *refs):
    mixed = refs[:parts]
    w_out, xr, dh, gain, w_up = refs[parts : parts + 5]
    attn_out, a2_out, hid_out, du_out, da2_out, gain_out = refs[parts + 5 :]
    attn = dot(mixed[0][...], w_out[0])
    for part in range(1, parts):
        attn = attn + dot(mixed[part][...], w_out[part])
    attn_out[...] = attn
    y = xr[...].astype(F32) + attn
    scaled = y * lax.rsqrt(jnp.mean(y * y, axis=1, keepdims=True) + EPS)
    a2 = (scaled * gain[...].astype(F32)).astype(BF16)
    a2_out[...] = a2
    u = dot(a2, w_up[...])
    square = u * u
    t = jnp.tanh(GELU_C * (u + GELU_A * (u * square)))
    hid_out[...] = (0.5 * u * (1.0 + t)).astype(BF16)
    slope = 0.5 * (1.0 + t) + (0.5 * GELU_C) * u * (1.0 - t * t) * (1.0 + 3.0 * GELU_A * square)
    du = (dh[...] * slope).astype(BF16)
    du_out[...] = du
    da2 = dot(du, w_up[...], NT)
    da2_out[0] = da2.astype(BF16)

    @pl.when(pl.program_id(0) == 0)
    def _():
        gain_out[...] = jnp.zeros_like(gain_out)

    gain_out[...] += jnp.sum((da2 * scaled).reshape(-1, 8, da2.shape[1]), axis=0)


def rows_body(parts, where, *refs):
    pieces = refs[:parts]
    attn, xr, dyr, gain, router, w_out = refs[parts : parts + 6]
    dyn_out, ga_out, do_out = refs[parts + 6 :]
    da2 = pieces[0][...].astype(F32)
    for piece in pieces[1:]:
        da2 = da2 + piece[...].astype(F32)
    rows = xr[...].astype(F32)
    y = rows + attn[...]
    inverse = lax.rsqrt(jnp.mean(y * y, axis=1, keepdims=True) + EPS)
    t = gain[...].astype(F32) * da2
    scaled = y * inverse
    dyn = inverse * (t - scaled * jnp.mean(t * scaled, axis=1, keepdims=True))
    dyn_out[...] = dyn
    rate = sigmoid(jnp.sum(rows * router[...].astype(F32), axis=1, keepdims=True))
    ga = (rate * dyr[...].astype(F32) + dyn).astype(BF16)
    ga_out[...] = ga
    for part in range(parts):
        do_out[part] = dot(ga, w_out[part], NT).astype(BF16)


def delta_body(parts, where, *refs):
    pieces = refs[:parts]
    attn, xr, dyr, dyn, router = refs[parts : parts + 5]
    upd_out, base_out, grad_router_out = refs[parts + 5 :]
    delta = attn[...]
    for piece in pieces:
        delta = delta + piece[...].astype(F32)
    rows = xr[...].astype(F32)
    grads = dyr[...].astype(F32)
    vec = router[...].astype(F32)
    rate = sigmoid(jnp.sum(rows * vec, axis=1, keepdims=True))
    upd_out[...] = (rows + rate * delta).astype(BF16)
    dlogit = jnp.sum(grads * delta, axis=1, keepdims=True) * rate * (1.0 - rate)
    base_out[...] = grads + dyn[...] + dlogit * vec

    @pl.when(pl.program_id(0) == 0)
    def _():
        grad_router_out[...] = jnp.zeros_like(grad_router_out)

    grad_router_out[...] += jnp.sum((dlogit * rows).reshape(-1, 8, rows.shape[1]), axis=0)


def back_body(heads, where, qkv, mask, dmixed, xr, gain, w_qkv, dqkv_out, da1_out, gain_out):
    joint = qkv[...]
    allowed = mask[...].astype(F32) > 0.5
    grads = dmixed[0]
    pieces = []
    for head in range(heads):
        base = head * 3 * HD
        query = joint[:, base : base + HD]
        key = joint[:, base + HD : base + 2 * HD]
        value = joint[:, base + 2 * HD : base + 3 * HD]
        dmix = grads[:, head * HD : (head + 1) * HD]
        probs = softmax_head(query, key, allowed)
        dprobs = dot(dmix, value, NT)
        spread = jnp.sum(probs * dprobs, axis=1, keepdims=True)
        dlog = (probs * (dprobs - spread)).astype(BF16)
        dquery = dot(dlog, key) * SCALE
        dkey = dot(dlog, query, TN) * SCALE
        dvalue = dot(probs.astype(BF16), dmix, TN)
        pieces += [dquery.astype(BF16), dkey.astype(BF16), dvalue.astype(BF16)]
    for at, piece in enumerate(pieces):
        dqkv_out[:, at * HD : (at + 1) * HD] = piece
    da1 = dot(dqkv_out[...], w_qkv[...], NT)
    da1_out[0] = da1.astype(BF16)
    rows = xr[...].astype(F32)
    scaled = rows * lax.rsqrt(jnp.mean(rows * rows, axis=1, keepdims=True) + EPS)

    @pl.when(pl.program_id(0) == 0)
    def _():
        gain_out[...] = jnp.zeros_like(gain_out)

    gain_out[...] += jnp.sum((da1 * scaled).reshape(-1, 8, da1.shape[1]), axis=0)


def last_body(parts, where, *refs):
    pieces = refs[:parts]
    xr, base, gain = refs[parts : parts + 3]
    (out,) = refs[parts + 3 :]
    da1 = pieces[0][...].astype(F32)
    for piece in pieces[1:]:
        da1 = da1 + piece[...].astype(F32)
    rows = xr[...].astype(F32)
    inverse = lax.rsqrt(jnp.mean(rows * rows, axis=1, keepdims=True) + EPS)
    t = gain[...].astype(F32) * da1
    scaled = rows * inverse
    dxn = inverse * (t - scaled * jnp.mean(t * scaled, axis=1, keepdims=True))
    out[...] = (base[...] + dxn).astype(BF16)


def put_body(where, source, routes, rows, *refs):
    out = refs[-1]
    length = source.shape[0]
    at = where[pl.program_id(0)]
    line = routes[pl.ds(at, 1), :]
    hot = iota((length, line.shape[1]), 0) == line
    picked = jnp.where(hot, 1.0, 0.0)
    taken = jnp.sum(picked, axis=1, keepdims=True) > 0.5
    moved = dot(picked.astype(BF16), rows[...])
    out[...] = jnp.where(taken, moved, source[...].astype(F32)).astype(BF16)


def put_rows(source, routes, rows, order, target, name):
    seqs, routed = routes.shape
    length = source.shape[0] // seqs
    width = source.shape[1]
    count = rows.shape[0] // routed
    in_specs = [
        pl.BlockSpec((length, width), lambda i, w: (w[i], 0)),
        whole(routes.shape),
        pl.BlockSpec((routed, width), lambda i, w: (i, 0)),
    ]
    args = [order, source, routes, rows]
    alias = None
    if target is not None:
        in_specs.append(pl.BlockSpec(memory_space=pl.ANY))
        args.append(target)
        alias = {4: 0}
    return call(
        put_body,
        (count,),
        in_specs,
        pl.BlockSpec((length, width), lambda i, w: (w[i], 0)),
        jax.ShapeDtypeStruct(source.shape, BF16),
        2 * count * length * routed * width,
        count * length * width * 4,
        name,
        alias=alias,
    )(*args)


def swap(value, axis, offset):
    size = lax.axis_size(axis)
    return lax.ppermute(value, axis, [(i, i ^ offset) for i in range(size)])


def block_of(value, index, rows):
    return lax.dynamic_slice_in_dim(value, index * rows, rows, 0)


def in_core_order(core, mine, other):
    return jnp.where(
        core == 0,
        jnp.concatenate([mine, other], axis=0),
        jnp.concatenate([other, mine], axis=0),
    )


def line_sum(value, depth):
    at = lax.axis_index("dp") // 2
    half = depth // 2

    def shift(array, pairs):
        return lax.ppermute(
            array, "dp", [(2 * a + c, 2 * b + c) for a, b in pairs for c in range(2)]
        )

    def mirrored(a, b):
        return [(a, b), (depth - 1 - a, depth - 1 - b)]

    for step in range(half - 1):
        got = shift(value, mirrored(step, step + 1))
        value = (value.astype(F32) + got.astype(F32)).astype(BF16)
    if depth > 1:
        got = shift(value, mirrored(half - 1, half))
        value = (value.astype(F32) + got.astype(F32)).astype(BF16)
    for step in reversed(range(half - 1)):
        got = shift(value, mirrored(step + 1, step))
        here = (at == step) | (at == depth - 1 - step)
        value = jnp.where(here, got, value)
    return value


def core_half(value, core):
    half = value.shape[0] // 2
    keep = block_of(value, core, half)
    give = block_of(value, 1 - core, half)
    got = swap(give.astype(BF16), "dp", 1)
    return (keep.astype(F32) + got.astype(F32)).astype(BF16)


def core_join(value, core):
    return in_core_order(core, value, swap(value, "dp", 1)).astype(F32)


def shards(
    tokens, segments, routes, cotangent, gain_attn, gain_mlp, w_router, w_qkv, w_out, w_up, w_down
):
    seqs, length = segments.shape
    routed = routes.shape[1]
    width = tokens.shape[1]
    total = seqs * routed
    wide = w_out.shape[0]
    heads = wide // HD
    joint = w_qkv.shape[1]
    hidden = w_up.shape[1]
    parts = lax.axis_size("mp")
    depth = lax.axis_size("dp") // 2
    own = total // parts
    rank = lax.axis_index("mp")
    core = lax.axis_index("dp") % 2
    aligned = own % routed == 0
    per = own // routed if aligned else 1
    where = rank.reshape(1).astype(jnp.int32)
    gain_one = gain_attn.reshape(1, width)
    gain_two = gain_mlp.reshape(1, width)
    router = w_router.reshape(1, width)
    partners = list(range(1, parts))
    sds = jax.ShapeDtypeStruct

    share = block_of(w_out, core, wide // 2)
    mine = jnp.stack([swap(share, "mp", j) for j in partners])
    other = swap(mine, "dp", 1)
    w_all = jnp.where(
        core == 0,
        jnp.concatenate([mine, other], axis=1),
        jnp.concatenate([other, mine], axis=1),
    )
    w_all = jnp.concatenate([w_out[None], w_all], axis=0)

    xr, a1, qkv, mask, mixed, score = call(
        functools.partial(front_body, heads, length // parts),
        (seqs,),
        [
            pl.BlockSpec((length, width), lambda i, w: (i, 0)),
            whole(routes.shape),
            whole(segments.shape),
            whole((1, width)),
            whole((1, width)),
            whole(w_qkv.shape),
        ],
        [
            pl.BlockSpec((routed, width), lambda i, w: (i, 0)),
            pl.BlockSpec((routed, width), lambda i, w: (i, 0)),
            pl.BlockSpec((routed, joint), lambda i, w: (i, 0)),
            pl.BlockSpec((routed, routed), lambda i, w: (i, 0)),
            pl.BlockSpec((routed, wide), lambda i, w: (i, 0)),
            whole((8, 128)),
        ],
        [
            sds((total, width), BF16),
            sds((total, width), BF16),
            sds((total, joint), BF16),
            sds((total, routed), BF16),
            sds((total, wide), BF16),
            sds((8, 128), F32),
        ],
        2 * total * width * (length + joint) * 1.3,
        2 * seqs * length * width + 8 * total * width,
        "front",
    )(where, tokens, routes, segments, gain_one, router, w_qkv)

    mixed_all = [mixed] + [swap(mixed, "mp", j) for j in partners]

    dyr, gm, dh = call(
        cot_body,
        (seqs,),
        [
            pl.BlockSpec((length, width), lambda i, w: (i, 0)),
            whole(routes.shape),
            pl.BlockSpec((routed, width), lambda i, w: (i, 0)),
            whole((1, width)),
            whole(w_down.shape),
        ],
        [
            pl.BlockSpec((routed, width), lambda i, w: (i, 0)),
            pl.BlockSpec((routed, width), lambda i, w: (i, 0)),
            pl.BlockSpec((routed, hidden), lambda i, w: (i, 0)),
        ],
        [sds((total, width), BF16), sds((total, width), BF16), sds((total, hidden), F32)],
        2 * total * width * (length + hidden),
        2 * seqs * length * width + 6 * total * width + 4 * total * hidden,
        "cot",
    )(where, cotangent, routes, xr, router, w_down)

    order = partners[::-1] + [0]
    tile = min(own, 128)
    tiles = own // tile
    blocks = jnp.stack([rank ^ j for j in order])
    table = (blocks[:, None] * tiles + jnp.arange(tiles)[None, :]).reshape(-1).astype(jnp.int32)

    def by_row(i, t):
        return (t[i], 0)

    steps = parts * tiles
    attn, a2, hid, du, da2, gain_two_part = call(
        functools.partial(middle_body, parts),
        (steps,),
        [pl.BlockSpec((tile, wide), by_row)] * parts
        + [
            whole(w_all.shape),
            pl.BlockSpec((tile, width), by_row),
            pl.BlockSpec((tile, hidden), by_row),
            whole((1, width)),
            whole(w_up.shape),
        ],
        [
            pl.BlockSpec((tile, width), lambda i, t: (jnp.maximum(i - (steps - tiles), 0), 0)),
            pl.BlockSpec((tile, width), by_row),
            pl.BlockSpec((tile, hidden), by_row),
            pl.BlockSpec((tile, hidden), by_row),
            pl.BlockSpec((1, tile, width), lambda i, t: (i // tiles, i % tiles, 0)),
            whole((8, width)),
        ],
        [
            sds((own, width), F32),
            sds((total, width), BF16),
            sds((total, hidden), BF16),
            sds((total, hidden), BF16),
            sds((parts, own, width), BF16),
            sds((8, width), F32),
        ],
        2 * total * width * (parts * wide + 2 * hidden),
        total * (10 * width + 8 * hidden) + 2 * width * (hidden + parts * wide),
        "middle",
    )(table, *mixed_all, w_all, xr, dh, gain_two, w_up)

    da2_all = [da2[-1]] + [swap(da2[at], "mp", j) for at, j in enumerate(order[:-1])]

    mlp = dot(hid, w_down).astype(BF16)
    grad_up = dot(a2, du, TN).astype(BF16)
    grad_down = dot(hid, gm, TN).astype(BF16)
    mlp_all = [block_of(mlp, rank, own)] + [
        swap(block_of(mlp, rank ^ j, own), "mp", j) for j in partners
    ]

    own_tiles = lambda i, w: (w[0] * tiles + i, 0)
    flat = lambda i, w: (i, 0)
    row_block = pl.BlockSpec((tile, width), flat)
    own_block = pl.BlockSpec((tile, width), own_tiles)
    dyn, ga, dmix = call(
        functools.partial(rows_body, parts),
        (tiles,),
        [row_block] * parts
        + [row_block, own_block, own_block, whole((1, width)), whole((1, width)), whole(w_all.shape)],
        [row_block, row_block, pl.BlockSpec((parts, tile, wide), lambda i, w: (0, i, 0))],
        [sds((own, width), F32), sds((own, width), BF16), sds((parts, own, wide), BF16)],
        2 * own * width * parts * wide,
        own * width * 24 + 2 * width * width,
        "rows",
    )(where, *da2_all, attn, xr, dyr, gain_two, router, w_all)

    dmix_all = jnp.stack([dmix[0]] + [swap(dmix[j], "mp", j) for j in partners])

    upd, base, router_part = call(
        functools.partial(delta_body, parts),
        (tiles,),
        [row_block] * parts + [row_block, own_block, own_block, row_block, whole((1, width))],
        [row_block, row_block, whole((8, width))],
        [sds((own, width), BF16), sds((own, width), F32), sds((8, width), F32)],
        own * width * 20,
        own * width * 24,
        "delta",
    )(where, *mlp_all, attn, xr, dyr, dyn, router)
    upd_all = [upd] + [swap(upd, "mp", j) for j in partners]

    if aligned:
        by_owner = lambda i, w: ((i // per) ^ w[0], i % per, 0)
        da1_shape = (parts, own, width)
    else:
        dmix_all = dmix_all[jnp.arange(parts) ^ rank].reshape(1, total, wide)
        by_owner = lambda i, w: (0, i, 0)
        da1_shape = (1, total, width)
    dqkv, da1, gain_one_part = call(
        functools.partial(back_body, heads),
        (seqs,),
        [
            pl.BlockSpec((routed, joint), flat),
            pl.BlockSpec((routed, routed), flat),
            pl.BlockSpec((1, routed, wide), by_owner),
            pl.BlockSpec((routed, width), flat),
            whole((1, width)),
            whole(w_qkv.shape),
        ],
        [
            pl.BlockSpec((routed, joint), flat),
            pl.BlockSpec((1, routed, width), by_owner),
            whole((8, width)),
        ],
        [sds((total, joint), BF16), sds(da1_shape, BF16), sds((8, width), F32)],
        2 * total * width * joint * 1.5,
        total * (4 * joint + 6 * width) + 2 * width * joint,
        "back",
    )(where, qkv, mask, dmix_all, xr, gain_one, w_qkv)

    if aligned:
        da1_blocks = [da1[j] for j in range(parts)]
    else:
        da1_blocks = [block_of(da1[0], rank ^ j, own) for j in range(parts)]
    da1_all = [da1_blocks[0]] + [swap(da1_blocks[j], "mp", j) for j in partners]

    grad_qkv = dot(a1, dqkv, TN).astype(BF16)

    last = call(
        functools.partial(last_body, parts),
        (tiles,),
        [row_block] * parts + [own_block, row_block, whole((1, width))],
        row_block,
        sds((own, width), BF16),
        own * width * 20,
        own * width * 18,
        "last",
    )(where, *da1_all, xr, base, gain_one)
    last_all = [last] + [swap(last, "mp", j) for j in partners]

    def spread(source, rows_all, name):
        if not aligned:
            rows = jnp.stack(rows_all)[jnp.arange(parts) ^ rank].reshape(total, width)
            return put_rows(source, routes, rows, jnp.arange(seqs, dtype=jnp.int32), None, name)
        target = None
        for j, rows in enumerate(rows_all):
            seq = ((rank ^ j) * per + jnp.arange(per)).astype(jnp.int32)
            target = put_rows(source, routes, rows, seq, target, name)
        return target

    output = spread(tokens, upd_all, "put_out")
    grad_tokens = spread(cotangent, last_all, "put_grad")

    grad_up = core_join(line_sum(core_half(grad_up, core), depth), core)
    grad_down = core_join(line_sum(core_half(grad_down, core), depth), core)
    grad_qkv = core_join(line_sum(core_half(grad_qkv, core), depth), core)

    def out_part(j):
        rows = block_of(mixed_all[j], rank, own)
        return dot(rows, ga, TN).astype(BF16)

    outs = jnp.stack([out_part(j) for j in range(parts)], axis=1)
    outs = core_half(outs, core)
    half = outs[:, 0].astype(F32)
    for j in partners:
        half = half + swap(outs[:, j], "mp", j).astype(F32)
    grad_out = core_join(line_sum(half.astype(BF16), depth), core)

    lines = jnp.sum(
        jnp.stack([gain_one_part, gain_two_part, router_part]), axis=1
    )
    scores = jnp.concatenate(
        [score[0:1] / 1.0, score[1:2] / parts, jnp.zeros((6, 128), F32)], axis=0
    ).reshape(1, -1)
    scores = jnp.pad(scores, ((0, 0), (0, width - 1024))) if width > 1024 else scores[:, :width]
    small = jnp.concatenate([lines, scores, jnp.zeros((4, width), F32)], axis=0)
    bit = 1
    while bit < 2 * depth:
        small = small + swap(small, "dp", bit)
        bit *= 2
    bit = 1
    while bit < parts:
        small = small + swap(small, "mp", bit)
        bit *= 2
    score_total = small[3, 0]
    routed_total = small[3, 128]
    token_count = seqs * length * lax.axis_size("dp")
    return (
        output,
        grad_tokens,
        small[0],
        small[1],
        small[2],
        grad_qkv,
        grad_out,
        grad_up,
        grad_down,
        routed_total / score_total,
        score_total / token_count,
    )


def solution(mesh):
    rows = P("dp", None)
    columns = P(None, "mp")
    lines = P("mp", None)
    in_specs = (rows, rows, rows, rows, P(), P(), P(), columns, lines, columns, lines)
    out_specs = (rows, rows, P(), P(), P(), columns, lines, columns, lines, P(), P())
    return jax.shard_map(shards, mesh=mesh, in_specs=in_specs, out_specs=out_specs, check_vma=False)
```

```python
import functools

import jax
import jax.numpy as jnp
from jax import lax
from jax.experimental import pallas as pl
from jax.experimental.pallas import tpu as pltpu
from jax.sharding import PartitionSpec as P

HD = 64
EPS = 1e-06
SCALE = HD ** (-0.5)
GELU_C = (2.0 / 3.141592653589793) ** 0.5
GELU_A = 0.044715
F32 = jnp.float32
BF16 = jnp.bfloat16


def dot(left, right, on=((1,), (0,))):
    return lax.dot_general(left, right, (on, ((), ())), preferred_element_type=F32)


NT = ((1,), (1,))
TN = ((0,), (0,))


def iota(shape, axis):
    return lax.broadcasted_iota(jnp.int32, shape, axis)


def sigmoid(value):
    return 1.0 / (1.0 + jnp.exp(-value))


def call(body, grid, in_specs, out_specs, out_shape, flops, nbytes, name, scratch=(), alias=None):
    return pl.pallas_call(
        body,
        grid_spec=pltpu.PrefetchScalarGridSpec(
            num_scalar_prefetch=1,
            grid=grid,
            in_specs=in_specs,
            out_specs=out_specs,
            scratch_shapes=list(scratch),
        ),
        out_shape=out_shape,
        cost_estimate=pl.CostEstimate(
            flops=int(flops), bytes_accessed=int(nbytes), transcendentals=0
        ),
        input_output_aliases=alias or {},
        name=name,
    )


def whole(shape):
    zeros = (0,) * len(shape)
    return pl.BlockSpec(shape, lambda *_: zeros)


def one_hot_rows(routes_row, length):
    routed = routes_row.shape[1]
    eye = iota((routed, routed), 0) == iota((routed, routed), 1)
    column = jnp.sum(jnp.where(eye, routes_row.astype(F32), 0.0), axis=1, keepdims=True)
    return iota((routed, length), 1) == column.astype(jnp.int32), eye


def head_mask(hot, eye, seg_line):
    seg_col = jnp.sum(jnp.where(hot, seg_line, 0.0), axis=1, keepdims=True)
    seg_row = jnp.sum(jnp.where(eye, seg_col, 0.0), axis=0, keepdims=True)
    routed = eye.shape[0]
    causal = iota((routed, routed), 0) >= iota((routed, routed), 1)
    return causal & (seg_col == seg_row)


def softmax_head(query, key, allowed):
    logits = jnp.where(allowed, dot(query, key, NT) * SCALE, -1e30)
    expon = jnp.exp(logits - jnp.max(logits, axis=1, keepdims=True))
    return expon / jnp.sum(expon, axis=1, keepdims=True)


def front_body(
    heads, slice_rows, where, tokens, routes, segments, gain, router, w_qkv,
    xr_out, a1_out, qkv_out, mask_out, mixed_out, score_out,
):
    step = pl.program_id(0)
    length = tokens.shape[0]
    hot, eye = one_hot_rows(routes[pl.ds(step, 1), :], length)
    seg_line = segments[pl.ds(step, 1), :].astype(F32)
    allowed = head_mask(hot, eye, seg_line)
    mask_out[...] = jnp.where(allowed, 1.0, 0.0).astype(BF16)
    rows = dot(jnp.where(hot, 1.0, 0.0).astype(BF16), tokens[...])
    xr_out[...] = rows.astype(BF16)
    vec = router[...].astype(F32)
    start = pl.multiple_of(where[0] * slice_rows, slice_rows)
    part = tokens[pl.ds(start, slice_rows), :].astype(F32)
    total = jnp.sum(sigmoid(jnp.sum(part * vec, axis=1, keepdims=True)), axis=0, keepdims=True)
    chosen = jnp.sum(sigmoid(jnp.sum(rows * vec, axis=1, keepdims=True)), axis=0, keepdims=True)

    @pl.when(step == 0)
    def _():
        score_out[...] = jnp.zeros_like(score_out)

    which = iota(score_out.shape, 0)
    score_out[...] += jnp.where(which == 0, total, jnp.where(which == 1, chosen, 0.0))
    inverse = lax.rsqrt(jnp.mean(rows * rows, axis=1, keepdims=True) + EPS)
    normed = (rows * inverse * gain[...].astype(F32)).astype(BF16)
    a1_out[...] = normed
    joint = dot(normed, w_qkv[...]).astype(BF16)
    qkv_out[...] = joint
    for head in range(heads):
        base = head * 3 * HD
        query = joint[:, base : base + HD]
        key = joint[:, base + HD : base + 2 * HD]
        value = joint[:, base + 2 * HD : base + 3 * HD]
        probs = softmax_head(query, key, allowed).astype(BF16)
        mixed_out[:, head * HD : (head + 1) * HD] = dot(probs, value).astype(BF16)


def cot_body(where, cotangent, routes, xr, router, w_down, dyr_out, gm_out, dh_out):
    step = pl.program_id(0)
    hot, _ = one_hot_rows(routes[pl.ds(step, 1), :], cotangent.shape[0])
    rows = dot(jnp.where(hot, 1.0, 0.0).astype(BF16), cotangent[...])
    dyr_out[...] = rows.astype(BF16)
    vec = router[...].astype(F32)
    rate = sigmoid(jnp.sum(xr[...].astype(F32) * vec, axis=1, keepdims=True))
    low = (rate * rows).astype(BF16)
    gm_out[...] = low
    dh_out[...] = dot(low, w_down[...], NT)


def middle_body(parts, table, *refs):
    mixed = refs[:parts]
    w_out, xr, dh, gain, w_up = refs[parts : parts + 5]
    attn_out, a2_out, hid_out, du_out, da2_out, gain_out = refs[parts + 5 :]
    attn = dot(mixed[0][...], w_out[0])
    for part in range(1, parts):
        attn = attn + dot(mixed[part][...], w_out[part])
    attn_out[...] = attn
    y = xr[...].astype(F32) + attn
    scaled = y * lax.rsqrt(jnp.mean(y * y, axis=1, keepdims=True) + EPS)
    a2 = (scaled * gain[...].astype(F32)).astype(BF16)
    a2_out[...] = a2
    u = dot(a2, w_up[...])
    square = u * u
    t = jnp.tanh(GELU_C * (u + GELU_A * (u * square)))
    hid_out[...] = (0.5 * u * (1.0 + t)).astype(BF16)
    slope = 0.5 * (1.0 + t) + (0.5 * GELU_C) * u * (1.0 - t * t) * (1.0 + 3.0 * GELU_A * square)
    du = (dh[...] * slope).astype(BF16)
    du_out[...] = du
    da2 = dot(du, w_up[...], NT)
    da2_out[0] = da2.astype(BF16)

    @pl.when(pl.program_id(0) == 0)
    def _():
        gain_out[...] = jnp.zeros_like(gain_out)

    gain_out[...] += jnp.sum((da2 * scaled).reshape(-1, 8, da2.shape[1]), axis=0)


def rows_body(parts, where, *refs):
    pieces = refs[:parts]
    attn, xr, dyr, gain, router, w_out = refs[parts : parts + 6]
    dyn_out, ga_out, do_out = refs[parts + 6 :]
    da2 = pieces[0][...].astype(F32)
    for piece in pieces[1:]:
        da2 = da2 + piece[...].astype(F32)
    rows = xr[...].astype(F32)
    y = rows + attn[...]
    inverse = lax.rsqrt(jnp.mean(y * y, axis=1, keepdims=True) + EPS)
    t = gain[...].astype(F32) * da2
    scaled = y * inverse
    dyn = inverse * (t - scaled * jnp.mean(t * scaled, axis=1, keepdims=True))
    dyn_out[...] = dyn
    rate = sigmoid(jnp.sum(rows * router[...].astype(F32), axis=1, keepdims=True))
    ga = (rate * dyr[...].astype(F32) + dyn).astype(BF16)
    ga_out[...] = ga
    for part in range(parts):
        do_out[part] = dot(ga, w_out[part], NT).astype(BF16)


def delta_body(parts, where, *refs):
    pieces = refs[:parts]
    attn, xr, dyr, dyn, router = refs[parts : parts + 5]
    upd_out, base_out, grad_router_out = refs[parts + 5 :]
    delta = attn[...]
    for piece in pieces:
        delta = delta + piece[...].astype(F32)
    rows = xr[...].astype(F32)
    grads = dyr[...].astype(F32)
    vec = router[...].astype(F32)
    rate = sigmoid(jnp.sum(rows * vec, axis=1, keepdims=True))
    upd_out[...] = (rows + rate * delta).astype(BF16)
    dlogit = jnp.sum(grads * delta, axis=1, keepdims=True) * rate * (1.0 - rate)
    base_out[...] = grads + dyn[...] + dlogit * vec

    @pl.when(pl.program_id(0) == 0)
    def _():
        grad_router_out[...] = jnp.zeros_like(grad_router_out)

    grad_router_out[...] += jnp.sum((dlogit * rows).reshape(-1, 8, rows.shape[1]), axis=0)


def back_body(heads, where, qkv, mask, dmixed, xr, gain, w_qkv, dqkv_out, da1_out, gain_out):
    joint = qkv[...]
    allowed = mask[...].astype(F32) > 0.5
    grads = dmixed[0]
    pieces = []
    for head in range(heads):
        base = head * 3 * HD
        query = joint[:, base : base + HD]
        key = joint[:, base + HD : base + 2 * HD]
        value = joint[:, base + 2 * HD : base + 3 * HD]
        dmix = grads[:, head * HD : (head + 1) * HD]
        probs = softmax_head(query, key, allowed)
        dprobs = dot(dmix, value, NT)
        spread = jnp.sum(probs * dprobs, axis=1, keepdims=True)
        dlog = (probs * (dprobs - spread)).astype(BF16)
        dquery = dot(dlog, key) * SCALE
        dkey = dot(dlog, query, TN) * SCALE
        dvalue = dot(probs.astype(BF16), dmix, TN)
        pieces += [dquery.astype(BF16), dkey.astype(BF16), dvalue.astype(BF16)]
    for at, piece in enumerate(pieces):
        dqkv_out[:, at * HD : (at + 1) * HD] = piece
    da1 = dot(dqkv_out[...], w_qkv[...], NT)
    da1_out[0] = da1.astype(BF16)
    rows = xr[...].astype(F32)
    scaled = rows * lax.rsqrt(jnp.mean(rows * rows, axis=1, keepdims=True) + EPS)

    @pl.when(pl.program_id(0) == 0)
    def _():
        gain_out[...] = jnp.zeros_like(gain_out)

    gain_out[...] += jnp.sum((da1 * scaled).reshape(-1, 8, da1.shape[1]), axis=0)


def last_body(parts, where, *refs):
    pieces = refs[:parts]
    xr, base, gain = refs[parts : parts + 3]
    (out,) = refs[parts + 3 :]
    da1 = pieces[0][...].astype(F32)
    for piece in pieces[1:]:
        da1 = da1 + piece[...].astype(F32)
    rows = xr[...].astype(F32)
    inverse = lax.rsqrt(jnp.mean(rows * rows, axis=1, keepdims=True) + EPS)
    t = gain[...].astype(F32) * da1
    scaled = rows * inverse
    dxn = inverse * (t - scaled * jnp.mean(t * scaled, axis=1, keepdims=True))
    out[...] = (base[...] + dxn).astype(BF16)


def put_body(where, source, routes, rows, *refs):
    out = refs[-1]
    length = source.shape[0]
    at = where[pl.program_id(0)]
    line = routes[pl.ds(at, 1), :]
    hot = iota((length, line.shape[1]), 0) == line
    picked = jnp.where(hot, 1.0, 0.0)
    taken = jnp.sum(picked, axis=1, keepdims=True) > 0.5
    moved = dot(picked.astype(BF16), rows[...])
    out[...] = jnp.where(taken, moved, source[...].astype(F32)).astype(BF16)


def put_rows(source, routes, rows, order, target, name):
    seqs, routed = routes.shape
    length = source.shape[0] // seqs
    width = source.shape[1]
    count = rows.shape[0] // routed
    in_specs = [
        pl.BlockSpec((length, width), lambda i, w: (w[i], 0)),
        whole(routes.shape),
        pl.BlockSpec((routed, width), lambda i, w: (i, 0)),
    ]
    args = [order, source, routes, rows]
    alias = None
    if target is not None:
        in_specs.append(pl.BlockSpec(memory_space=pl.ANY))
        args.append(target)
        alias = {4: 0}
    return call(
        put_body,
        (count,),
        in_specs,
        pl.BlockSpec((length, width), lambda i, w: (w[i], 0)),
        jax.ShapeDtypeStruct(source.shape, BF16),
        2 * count * length * routed * width,
        count * length * width * 4,
        name,
        alias=alias,
    )(*args)


def swap(value, axis, offset):
    size = lax.axis_size(axis)
    return lax.ppermute(value, axis, [(i, i ^ offset) for i in range(size)])


def block_of(value, index, rows):
    return lax.dynamic_slice_in_dim(value, index * rows, rows, 0)


def in_core_order(core, mine, other):
    return jnp.where(
        core == 0,
        jnp.concatenate([mine, other], axis=0),
        jnp.concatenate([other, mine], axis=0),
    )


def line_sum(value, depth):
    at = lax.axis_index("dp") // 2
    half = depth // 2

    def shift(array, pairs):
        return lax.ppermute(
            array, "dp", [(2 * a + c, 2 * b + c) for a, b in pairs for c in range(2)]
        )

    def mirrored(a, b):
        return [(a, b), (depth - 1 - a, depth - 1 - b)]

    for step in range(half - 1):
        got = shift(value, mirrored(step, step + 1))
        value = (value.astype(F32) + got.astype(F32)).astype(BF16)
    if depth > 1:
        got = shift(value, mirrored(half - 1, half))
        value = (value.astype(F32) + got.astype(F32)).astype(BF16)
    for step in reversed(range(half - 1)):
        got = shift(value, mirrored(step + 1, step))
        here = (at == step) | (at == depth - 1 - step)
        value = jnp.where(here, got, value)
    return value


def core_half(value, core):
    half = value.shape[0] // 2
    keep = block_of(value, core, half)
    give = block_of(value, 1 - core, half)
    got = swap(give.astype(BF16), "dp", 1)
    return (keep.astype(F32) + got.astype(F32)).astype(BF16)


def core_join(value, core):
    return in_core_order(core, value, swap(value, "dp", 1)).astype(F32)


def general(
    tokens, segments, routes, cotangent, gain_attn, gain_mlp, w_router, w_qkv, w_out, w_up, w_down
):
    seqs, length = segments.shape
    routed = routes.shape[1]
    width = tokens.shape[1]
    total = seqs * routed
    wide = w_out.shape[0]
    heads = wide // HD
    joint = w_qkv.shape[1]
    hidden = w_up.shape[1]
    parts = lax.axis_size("mp")
    depth = lax.axis_size("dp") // 2
    own = total // parts
    rank = lax.axis_index("mp")
    core = lax.axis_index("dp") % 2
    aligned = own % routed == 0
    per = own // routed if aligned else 1
    where = rank.reshape(1).astype(jnp.int32)
    gain_one = gain_attn.reshape(1, width)
    gain_two = gain_mlp.reshape(1, width)
    router = w_router.reshape(1, width)
    partners = list(range(1, parts))
    sds = jax.ShapeDtypeStruct

    share = block_of(w_out, core, wide // 2)
    mine = jnp.stack([swap(share, "mp", j) for j in partners])
    other = swap(mine, "dp", 1)
    w_all = jnp.where(
        core == 0,
        jnp.concatenate([mine, other], axis=1),
        jnp.concatenate([other, mine], axis=1),
    )
    w_all = jnp.concatenate([w_out[None], w_all], axis=0)

    xr, a1, qkv, mask, mixed, score = call(
        functools.partial(front_body, heads, length // parts),
        (seqs,),
        [
            pl.BlockSpec((length, width), lambda i, w: (i, 0)),
            whole(routes.shape),
            whole(segments.shape),
            whole((1, width)),
            whole((1, width)),
            whole(w_qkv.shape),
        ],
        [
            pl.BlockSpec((routed, width), lambda i, w: (i, 0)),
            pl.BlockSpec((routed, width), lambda i, w: (i, 0)),
            pl.BlockSpec((routed, joint), lambda i, w: (i, 0)),
            pl.BlockSpec((routed, routed), lambda i, w: (i, 0)),
            pl.BlockSpec((routed, wide), lambda i, w: (i, 0)),
            whole((8, 128)),
        ],
        [
            sds((total, width), BF16),
            sds((total, width), BF16),
            sds((total, joint), BF16),
            sds((total, routed), BF16),
            sds((total, wide), BF16),
            sds((8, 128), F32),
        ],
        2 * total * width * (length + joint) * 1.3,
        2 * seqs * length * width + 8 * total * width,
        "front",
    )(where, tokens, routes, segments, gain_one, router, w_qkv)

    mixed_all = [mixed] + [swap(mixed, "mp", j) for j in partners]

    dyr, gm, dh = call(
        cot_body,
        (seqs,),
        [
            pl.BlockSpec((length, width), lambda i, w: (i, 0)),
            whole(routes.shape),
            pl.BlockSpec((routed, width), lambda i, w: (i, 0)),
            whole((1, width)),
            whole(w_down.shape),
        ],
        [
            pl.BlockSpec((routed, width), lambda i, w: (i, 0)),
            pl.BlockSpec((routed, width), lambda i, w: (i, 0)),
            pl.BlockSpec((routed, hidden), lambda i, w: (i, 0)),
        ],
        [sds((total, width), BF16), sds((total, width), BF16), sds((total, hidden), F32)],
        2 * total * width * (length + hidden),
        2 * seqs * length * width + 6 * total * width + 4 * total * hidden,
        "cot",
    )(where, cotangent, routes, xr, router, w_down)

    order = partners[::-1] + [0]
    tile = min(own, 128)
    tiles = own // tile
    blocks = jnp.stack([rank ^ j for j in order])
    table = (blocks[:, None] * tiles + jnp.arange(tiles)[None, :]).reshape(-1).astype(jnp.int32)

    def by_row(i, t):
        return (t[i], 0)

    steps = parts * tiles
    attn, a2, hid, du, da2, gain_two_part = call(
        functools.partial(middle_body, parts),
        (steps,),
        [pl.BlockSpec((tile, wide), by_row)] * parts
        + [
            whole(w_all.shape),
            pl.BlockSpec((tile, width), by_row),
            pl.BlockSpec((tile, hidden), by_row),
            whole((1, width)),
            whole(w_up.shape),
        ],
        [
            pl.BlockSpec((tile, width), lambda i, t: (jnp.maximum(i - (steps - tiles), 0), 0)),
            pl.BlockSpec((tile, width), by_row),
            pl.BlockSpec((tile, hidden), by_row),
            pl.BlockSpec((tile, hidden), by_row),
            pl.BlockSpec((1, tile, width), lambda i, t: (i // tiles, i % tiles, 0)),
            whole((8, width)),
        ],
        [
            sds((own, width), F32),
            sds((total, width), BF16),
            sds((total, hidden), BF16),
            sds((total, hidden), BF16),
            sds((parts, own, width), BF16),
            sds((8, width), F32),
        ],
        2 * total * width * (parts * wide + 2 * hidden),
        total * (10 * width + 8 * hidden) + 2 * width * (hidden + parts * wide),
        "middle",
    )(table, *mixed_all, w_all, xr, dh, gain_two, w_up)

    da2_all = [da2[-1]] + [swap(da2[at], "mp", j) for at, j in enumerate(order[:-1])]

    mlp = dot(hid, w_down).astype(BF16)
    grad_up = dot(a2, du, TN).astype(BF16)
    grad_down = dot(hid, gm, TN).astype(BF16)
    mlp_all = [block_of(mlp, rank, own)] + [
        swap(block_of(mlp, rank ^ j, own), "mp", j) for j in partners
    ]

    own_tiles = lambda i, w: (w[0] * tiles + i, 0)
    flat = lambda i, w: (i, 0)
    row_block = pl.BlockSpec((tile, width), flat)
    own_block = pl.BlockSpec((tile, width), own_tiles)
    dyn, ga, dmix = call(
        functools.partial(rows_body, parts),
        (tiles,),
        [row_block] * parts
        + [row_block, own_block, own_block, whole((1, width)), whole((1, width)), whole(w_all.shape)],
        [row_block, row_block, pl.BlockSpec((parts, tile, wide), lambda i, w: (0, i, 0))],
        [sds((own, width), F32), sds((own, width), BF16), sds((parts, own, wide), BF16)],
        2 * own * width * parts * wide,
        own * width * 24 + 2 * width * width,
        "rows",
    )(where, *da2_all, attn, xr, dyr, gain_two, router, w_all)

    dmix_all = jnp.stack([dmix[0]] + [swap(dmix[j], "mp", j) for j in partners])

    upd, base, router_part = call(
        functools.partial(delta_body, parts),
        (tiles,),
        [row_block] * parts + [row_block, own_block, own_block, row_block, whole((1, width))],
        [row_block, row_block, whole((8, width))],
        [sds((own, width), BF16), sds((own, width), F32), sds((8, width), F32)],
        own * width * 20,
        own * width * 24,
        "delta",
    )(where, *mlp_all, attn, xr, dyr, dyn, router)
    upd_all = [upd] + [swap(upd, "mp", j) for j in partners]

    if aligned:
        by_owner = lambda i, w: ((i // per) ^ w[0], i % per, 0)
        da1_shape = (parts, own, width)
    else:
        dmix_all = dmix_all[jnp.arange(parts) ^ rank].reshape(1, total, wide)
        by_owner = lambda i, w: (0, i, 0)
        da1_shape = (1, total, width)
    dqkv, da1, gain_one_part = call(
        functools.partial(back_body, heads),
        (seqs,),
        [
            pl.BlockSpec((routed, joint), flat),
            pl.BlockSpec((routed, routed), flat),
            pl.BlockSpec((1, routed, wide), by_owner),
            pl.BlockSpec((routed, width), flat),
            whole((1, width)),
            whole(w_qkv.shape),
        ],
        [
            pl.BlockSpec((routed, joint), flat),
            pl.BlockSpec((1, routed, width), by_owner),
            whole((8, width)),
        ],
        [sds((total, joint), BF16), sds(da1_shape, BF16), sds((8, width), F32)],
        2 * total * width * joint * 1.5,
        total * (4 * joint + 6 * width) + 2 * width * joint,
        "back",
    )(where, qkv, mask, dmix_all, xr, gain_one, w_qkv)

    if aligned:
        da1_blocks = [da1[j] for j in range(parts)]
    else:
        da1_blocks = [block_of(da1[0], rank ^ j, own) for j in range(parts)]
    da1_all = [da1_blocks[0]] + [swap(da1_blocks[j], "mp", j) for j in partners]

    grad_qkv = dot(a1, dqkv, TN).astype(BF16)

    last = call(
        functools.partial(last_body, parts),
        (tiles,),
        [row_block] * parts + [own_block, row_block, whole((1, width))],
        row_block,
        sds((own, width), BF16),
        own * width * 20,
        own * width * 18,
        "last",
    )(where, *da1_all, xr, base, gain_one)
    last_all = [last] + [swap(last, "mp", j) for j in partners]

    def spread(source, rows_all, name):
        if not aligned:
            rows = jnp.stack(rows_all)[jnp.arange(parts) ^ rank].reshape(total, width)
            return put_rows(source, routes, rows, jnp.arange(seqs, dtype=jnp.int32), None, name)
        target = None
        for j, rows in enumerate(rows_all):
            seq = ((rank ^ j) * per + jnp.arange(per)).astype(jnp.int32)
            target = put_rows(source, routes, rows, seq, target, name)
        return target

    output = spread(tokens, upd_all, "put_out")
    grad_tokens = spread(cotangent, last_all, "put_grad")

    grad_up = core_join(line_sum(core_half(grad_up, core), depth), core)
    grad_down = core_join(line_sum(core_half(grad_down, core), depth), core)
    grad_qkv = core_join(line_sum(core_half(grad_qkv, core), depth), core)

    def out_part(j):
        rows = block_of(mixed_all[j], rank, own)
        return dot(rows, ga, TN).astype(BF16)

    outs = jnp.stack([out_part(j) for j in range(parts)], axis=1)
    outs = core_half(outs, core)
    half = outs[:, 0].astype(F32)
    for j in partners:
        half = half + swap(outs[:, j], "mp", j).astype(F32)
    grad_out = core_join(line_sum(half.astype(BF16), depth), core)

    lines = jnp.sum(
        jnp.stack([gain_one_part, gain_two_part, router_part]), axis=1
    )
    scores = jnp.concatenate(
        [score[0:1] / 1.0, score[1:2] / parts, jnp.zeros((6, 128), F32)], axis=0
    ).reshape(1, -1)
    scores = jnp.pad(scores, ((0, 0), (0, width - 1024))) if width > 1024 else scores[:, :width]
    small = jnp.concatenate([lines, scores, jnp.zeros((4, width), F32)], axis=0)
    bit = 1
    while bit < 2 * depth:
        small = small + swap(small, "dp", bit)
        bit *= 2
    bit = 1
    while bit < parts:
        small = small + swap(small, "mp", bit)
        bit *= 2
    score_total = small[3, 0]
    routed_total = small[3, 128]
    token_count = seqs * length * lax.axis_size("dp")
    return (
        output,
        grad_tokens,
        small[0],
        small[1],
        small[2],
        grad_qkv,
        grad_out,
        grad_up,
        grad_down,
        routed_total / score_total,
        score_total / token_count,
    )


STREAMS = ((1, 3, 0, 2), (2, 3, 0, 1))
FIRST = (1, 2)


def row(vector):
    return vector[...].astype(F32).reshape(1, -1)


def front_pair_body(heads, slice_rows, first, where, *refs):
    blocks = refs[:2]
    routes, segments, gain, router, w_qkv = refs[2:7]
    xr_out, a1_out, qkv_out, mask_out, lse_out, mixed_out, score_out = refs[7:]
    step = pl.program_id(0)
    length, width = blocks[0].shape
    routed = routes.shape[1]
    vec = jnp.broadcast_to(row(router), (8, width)).astype(BF16)
    start = pl.multiple_of(where[RANK] * slice_rows, slice_rows)
    rows_all, allowed_all = [], []
    total = jnp.zeros((8, 1), F32)
    for at, tokens in enumerate(blocks):
        seq = where[first + 2 * step + at]
        hot, eye = one_hot_rows(routes[pl.ds(seq, 1), :], length)
        seg_line = segments[pl.ds(seq, 1), :].astype(F32)
        allowed = head_mask(hot, eye, seg_line)
        mask_out[at * routed : (at + 1) * routed, :] = jnp.where(allowed, 1.0, 0.0).astype(BF16)
        rows_all.append(dot(jnp.where(hot, 1.0, 0.0).astype(BF16), tokens[...]))
        allowed_all.append(allowed)
        scored = sigmoid(dot(vec, tokens[pl.ds(start, slice_rows), :], NT))
        total = total + jnp.sum(scored, axis=1, keepdims=True)
    rows = jnp.concatenate(rows_all, axis=0)
    low = rows.astype(BF16)
    xr_out[...] = low
    chosen = jnp.sum(sigmoid(dot(vec, low, NT)), axis=1, keepdims=True)

    @pl.when(step == 0)
    def _():
        score_out[...] = jnp.zeros_like(score_out)

    which = iota(score_out.shape, 0)
    score_out[...] += jnp.where(which == 0, total, jnp.where(which == 1, chosen, 0.0))
    inverse = lax.rsqrt(jnp.mean(rows * rows, axis=1, keepdims=True) + EPS)
    normed = (rows * inverse * row(gain)).astype(BF16)
    a1_out[...] = normed
    joint = dot(normed, w_qkv[...]).astype(BF16)
    qkv_out[...] = joint
    logits = []
    for at in range(2):
        own = joint[at * routed : (at + 1) * routed]
        for head in range(heads):
            base = head * 3 * HD
            raw = dot(own[:, base : base + HD], own[:, base + HD : base + 2 * HD], NT)
            logits.append(jnp.where(allowed_all[at], raw * SCALE, -1e30))
    logits = jnp.concatenate(logits, axis=0)
    top = jnp.max(logits, axis=1, keepdims=True)
    expon = jnp.exp(logits - top)
    norm = jnp.sum(expon, axis=1, keepdims=True)
    sums = top + jnp.log(norm)
    probs = (expon * (1.0 / norm)).astype(BF16)
    for at in range(2):
        span = slice(at * routed, (at + 1) * routed)
        for head in range(heads):
            place = slice((at * heads + head) * routed, (at * heads + head + 1) * routed)
            base = head * 3 * HD
            value = joint[span, base + 2 * HD : base + 3 * HD]
            lse_out[span, head : head + 1] = sums[place]
            mixed_out[span, head * HD : (head + 1) * HD] = dot(probs[place], value).astype(BF16)


def cot_pair_body(where, *refs):
    blocks = refs[:2]
    routes, xr_a, xr_b, router, w_down, dyr_out, gm_out, dh_out = refs[2:]
    step = pl.program_id(0)
    length = blocks[0].shape[0]
    picked = []
    for at, block in enumerate(blocks):
        hot, _ = one_hot_rows(routes[pl.ds(where[2 * step + at], 1), :], length)
        picked.append(dot(jnp.where(hot, 1.0, 0.0).astype(BF16), block[...]))
    rows = jnp.concatenate(picked, axis=0)
    dyr_out[...] = rows.astype(BF16)
    xr = jnp.where(step < 2, xr_a[...].astype(F32), xr_b[...].astype(F32))
    rate = sigmoid(jnp.sum(xr * row(router), axis=1, keepdims=True))
    low = (rate * rows).astype(BF16)
    gm_out[...] = low
    dh_out[...] = dot(low, w_down[...], NT)


def flip(value, swapped):
    half = value.shape[0] // 2
    if swapped:
        return jnp.concatenate([value[half:], value[:half]], axis=0)
    return value


def middle_pair_body(stream, where, *refs):
    mixed = refs[:4]
    w_all, xr, dh, gain, w_up = refs[4:9]
    attn_out, a2_out, hid_out, du_out, send_out, keep_out = refs[9:]
    step = pl.program_id(0)
    plain = (0, FIRST[stream])
    joined = jnp.concatenate(
        [flip(mixed[part][...], part not in plain) for part in range(4)], axis=1
    )
    attn = dot(joined, w_all[...])
    half = attn.shape[0] // 2
    attn_out[...] = attn[:half]
    y = xr[...].astype(F32) + attn
    scaled = y * lax.rsqrt(jnp.mean(y * y, axis=1, keepdims=True) + EPS)
    a2 = (scaled * row(gain)).astype(BF16)
    a2_out[...] = a2
    u = dot(a2, w_up[...])
    square = u * u
    t = jnp.tanh(u * (GELU_C + (GELU_C * GELU_A) * square))
    cdf = 0.5 + 0.5 * t
    hid_out[...] = (u * cdf).astype(BF16)
    slope = cdf + (u * (1.0 - t * t)) * (0.5 * GELU_C + (1.5 * GELU_C * GELU_A) * square)
    du = (dh[...] * slope).astype(BF16)
    du_out[...] = du
    low = dot(du, w_up[...], NT).astype(BF16)

    @pl.when(step == 0)
    def _():
        send_out[0] = low[:half]
        send_out[1] = low[half:]

    @pl.when(step == 1)
    def _():
        keep_out[0] = low[:half]
        keep_out[1] = low[half:]


def summed(refs):
    rows = []
    for stream in range(2):
        keep, first, final = refs[3 * stream : 3 * stream + 3]
        rows.append(keep[0].astype(F32) + first[0].astype(F32) + final[...].astype(F32))
    return jnp.concatenate(rows, axis=0)


def both(left, right):
    return jnp.concatenate([left[...].astype(F32), right[...].astype(F32)], axis=0)


def fold(value):
    return jnp.sum(value.reshape(-1, 8, value.shape[1]), axis=0)


def rows_pair_body(where, *refs):
    da2 = summed(refs[:6])
    attn_a, attn_b, xr_a, xr_b, dyr_a, dyr_b, gain, router, w_all = refs[6:15]
    dyn_out, ga_out, gain_out, do_outs = refs[15], refs[16], refs[17], refs[18:]
    rows = both(xr_a, xr_b)
    y = rows + both(attn_a, attn_b)
    inverse = lax.rsqrt(jnp.mean(y * y, axis=1, keepdims=True) + EPS)
    scaled = y * inverse
    joint = da2 * scaled
    gain_out[...] = fold(joint)
    vec = row(gain)
    dyn = inverse * (vec * da2 - scaled * jnp.mean(vec * joint, axis=1, keepdims=True))
    dyn_out[...] = dyn
    rate = sigmoid(jnp.sum(rows * row(router), axis=1, keepdims=True))
    ga = (rate * both(dyr_a, dyr_b) + dyn).astype(BF16)
    ga_out[...] = ga
    wide = do_outs[0].shape[1]
    for part, out in enumerate(do_outs):
        out[...] = dot(ga, w_all[part * wide : (part + 1) * wide, :], NT).astype(BF16)


def delta_pair_body(where, *refs):
    mlp = summed(refs[:6])
    attn_a, attn_b, xr_a, xr_b, dyr_a, dyr_b, dyn, router = refs[6:14]
    upd_out, base_out, grad_router_out = refs[14:]
    delta = both(attn_a, attn_b) + mlp
    rows = both(xr_a, xr_b)
    grads = both(dyr_a, dyr_b)
    vec = row(router)
    rate = sigmoid(jnp.sum(rows * vec, axis=1, keepdims=True))
    upd_out[...] = (rows + rate * delta).astype(BF16)
    dlogit = jnp.sum(grads * delta, axis=1, keepdims=True) * rate * (1.0 - rate)
    base_out[...] = grads + dyn[...] + dlogit * vec
    grad_router_out[...] = fold(dlogit * rows)


def out_grad_body(where, *refs):
    ga, keep_out, give_out = refs[8:]
    half = keep_out.shape[1]
    grads = ga[...]
    for out, core in ((keep_out, where[CORE]), (give_out, 1 - where[CORE])):
        span = pl.ds(pl.multiple_of(core * half, half), half)
        for part in range(4):
            mixed = jnp.concatenate([refs[part][:, span], refs[4 + part][:, span]], axis=0)
            out[part] = dot(mixed, grads, TN).astype(BF16)


def back_pair_body(heads, stream, where, qkv, mask, lse, *refs):
    dmixed = refs[:4]
    w_qkv, dqkv_out, send_out, keep_out = refs[4:]
    step = pl.program_id(0)
    owners = STREAMS[stream]
    routed = mask.shape[1]
    logits, dprobs, norms, items = [], [], [], []
    for at in range(2):
        span = slice(at * routed, (at + 1) * routed)
        joint = qkv[span, :]
        allowed = mask[span, :].astype(F32) > 0.5
        grads = jnp.where(step == 0, dmixed[owners[at]][...], dmixed[owners[2 + at]][...])
        for head in range(heads):
            base = head * 3 * HD
            query = joint[:, base : base + HD]
            key = joint[:, base + HD : base + 2 * HD]
            value = joint[:, base + 2 * HD : base + 3 * HD]
            dmix = grads[:, head * HD : (head + 1) * HD]
            logits.append(jnp.where(allowed, dot(query, key, NT) * SCALE, -1e30))
            dprobs.append(dot(dmix, value, NT))
            norms.append(lse[span, head : head + 1])
            items.append((span, base, query, key, dmix))
    probs = jnp.exp(jnp.concatenate(logits, axis=0) - jnp.concatenate(norms, axis=0))
    dprobs = jnp.concatenate(dprobs, axis=0)
    spread = jnp.sum(probs * dprobs, axis=1, keepdims=True)
    dlogs = (probs * (dprobs - spread)).astype(BF16)
    probs = probs.astype(BF16)
    for at, (span, base, query, key, dmix) in enumerate(items):
        dlog = dlogs[at * routed : (at + 1) * routed]
        prob = probs[at * routed : (at + 1) * routed]
        dqkv_out[span, base : base + HD] = (dot(dlog, key) * SCALE).astype(BF16)
        dqkv_out[span, base + HD : base + 2 * HD] = (dot(dlog, query, TN) * SCALE).astype(BF16)
        dqkv_out[span, base + 2 * HD : base + 3 * HD] = dot(prob, dmix, TN).astype(BF16)
    low = dot(dqkv_out[...], w_qkv[...], NT).astype(BF16)

    @pl.when(step == 0)
    def _():
        send_out[0] = low[:routed]
        send_out[1] = low[routed:]

    @pl.when(step == 1)
    def _():
        keep_out[0] = low[:routed]
        keep_out[1] = low[routed:]


def last_pair_body(where, *refs):
    da1 = summed(refs[:6])
    xr_a, xr_b, base, gain, out, gain_out = refs[6:]
    rows = both(xr_a, xr_b)
    inverse = lax.rsqrt(jnp.mean(rows * rows, axis=1, keepdims=True) + EPS)
    scaled = rows * inverse
    joint = da1 * scaled
    gain_out[...] = fold(joint)
    vec = row(gain)
    dxn = inverse * (vec * da1 - scaled * jnp.mean(vec * joint, axis=1, keepdims=True))
    out[...] = (base[...] + dxn).astype(BF16)


def place_body(starts, where, source, routes, *refs):
    rows, out = refs[: len(starts)], refs[-1]
    step = pl.program_id(0)
    length = source.shape[0]
    line = routes[pl.ds(where[PUT + put_entry(starts, step)], 1), :]
    hot = iota((length, line.shape[1]), 0) == line
    picked = jnp.where(hot, 1.0, 0.0)
    taken = jnp.sum(picked, axis=1, keepdims=True) > 0.5
    fresh = rows[0][...]
    for at, start in enumerate(starts):
        if at:
            fresh = jnp.where(step >= start[0], rows[at][...], fresh)
    moved = dot(picked.astype(BF16), fresh)
    out[...] = jnp.where(taken, moved, source[...].astype(F32)).astype(BF16)


def put_entry(starts, step):
    entry = starts[0][1] + step
    for first, place in starts[1:]:
        entry = jnp.where(step >= first, place + step - first, entry)
    return entry


def place_rows(table, source, routes, parts, target, name):
    seqs, routed = routes.shape
    length = source.shape[0] // seqs
    width = source.shape[1]
    starts, step = [], 0
    block = lambda i, w: (w[PUT + put_entry(starts, i)], 0)
    in_specs = [pl.BlockSpec((length, width), block), whole(routes.shape)]
    args = [table, source, routes]
    for rows, place in parts:
        per = rows.shape[0] // routed
        starts.append((step, place))
        in_specs.append(
            pl.BlockSpec(
                (routed, width),
                lambda i, w, first=step, top=per - 1: (jnp.clip(i - first, 0, top), 0),
            )
        )
        args.append(rows)
        step += per
    alias = None
    if target is not None:
        in_specs.append(pl.BlockSpec(memory_space=pl.ANY))
        alias = {len(args): 0}
        args.append(target)
    return call(
        functools.partial(place_body, tuple(starts)),
        (step,),
        in_specs,
        pl.BlockSpec((length, width), block),
        jax.ShapeDtypeStruct(source.shape, BF16),
        1,
        1,
        name,
        alias=alias,
    )(*args)


def join_body(where, *refs):
    out = refs[-1]
    for at, ref in enumerate(refs[:-1]):

        @pl.when(pl.program_id(0) == at)
        def _(ref=ref):
            out[...] = ref[...].astype(F32)


def join(table, pieces, first):
    rows, columns = pieces[0].shape
    count = len(pieces)
    return call(
        join_body,
        (count,),
        [whole((rows, columns))] * count,
        pl.BlockSpec((rows, columns), lambda i, w: (w[first + i], 0)),
        jax.ShapeDtypeStruct((rows * count, columns), F32),
        1,
        1,
        "join",
    )(table, *pieces)


def after(value, *others):
    return lax.optimization_barrier((value, *others))[0]


def add(left, right):
    return (left.astype(F32) + right.astype(F32)).astype(BF16)


class Total:
    def __init__(self, value, core, bit):
        half = value.shape[0] // 2
        self.core, self.bit = core, bit
        self.keep = block_of(value, core, half)
        self.give = block_of(value, 1 - core, half)
        self.sent = swap(self.give, "dp", 1)

    def split(self, *others):
        got = after(self.sent, *others)
        rows = got.shape[0] // 2
        cut = lambda index: add(block_of(self.keep, index, rows), block_of(got, index, rows))
        far = cut(1 - self.bit)
        self.value = cut(self.bit)
        self.sent = swap(far, "dp", 2)
        return far

    def cross(self, *others):
        self.value = add(self.value, after(self.sent, *others))
        self.sent = swap(self.value, "dp", 4)
        return self.value

    def close(self, *others):
        self.value = add(self.value, after(self.sent, *others))
        self.sent = swap(self.value, "dp", 2)
        self.pair = swap(self.value, "dp", 1)
        return self.value

    def back(self, *others):
        self.side = after(self.sent, *others)
        self.corner = swap(self.side, "dp", 1)
        return self.side

    def pieces(self):
        return [self.value, self.pair, self.side, self.corner]


OWNERS = (1, 3, 0, 2, 2, 3, 0, 1)
HALVES = (0, 0, 0, 0, 1, 1, 1, 1)
RANK, CORE, QUARTER, PUT = 8, 9, 10, 16


def make_table(rank, core, bit):
    owners = jnp.array(OWNERS + (0,) * 8 + (0, 0, 1, 1, 2, 2, 3, 3), jnp.int32)
    halves = jnp.array(HALVES + (0,) * 8 + (0, 1) * 4, jnp.int32)
    at = jnp.arange(24, dtype=jnp.int32)
    table = 2 * (rank ^ owners) + halves
    quarter = at - QUARTER
    quarters = 2 * (core ^ (quarter % 2)) + (bit ^ (quarter // 2))
    table = jnp.where((at >= QUARTER) & (at < QUARTER + 4), quarters, table)
    table = jnp.where(at == 14, core, jnp.where(at == 15, 1 - core, table))
    return jnp.where(at == RANK, rank, jnp.where(at == CORE, core, table)).astype(jnp.int32)


def paired(
    tokens, segments, routes, cotangent, gain_attn, gain_mlp, w_router, w_qkv, w_out, w_up, w_down
):
    seqs, length = segments.shape
    routed = routes.shape[1]
    width = tokens.shape[1]
    wide = w_out.shape[0]
    heads = wide // HD
    joint = w_qkv.shape[1]
    hidden = w_up.shape[1]
    rank = lax.axis_index("mp")
    core = lax.axis_index("dp") % 2
    bit = lax.axis_index("dp") // 2 % 2
    half_rows = 4 * routed
    pair = 2 * routed
    sds = jax.ShapeDtypeStruct
    flat = lambda i, w: (i, 0)
    line = whole((width,))
    table = make_table(rank, core, bit)

    share = block_of(w_out, core, wide // 2)
    mine = jnp.stack([swap(share, "mp", j) for j in (1, 2, 3)])

    fronts = []
    for stream in range(2):
        fronts.append(
            call(
                functools.partial(front_pair_body, heads, length // 4, 4 * stream),
                (2,),
                [
                    pl.BlockSpec((length, width), lambda i, w, s=4 * stream: (w[2 * i + s], 0)),
                    pl.BlockSpec((length, width), lambda i, w, s=4 * stream: (w[2 * i + 1 + s], 0)),
                    whole(routes.shape),
                    whole(segments.shape),
                    line,
                    line,
                    whole(w_qkv.shape),
                ],
                [
                    pl.BlockSpec((pair, width), flat),
                    pl.BlockSpec((pair, width), flat),
                    pl.BlockSpec((pair, joint), flat),
                    pl.BlockSpec((pair, routed), flat),
                    pl.BlockSpec((pair, 128), flat),
                    pl.BlockSpec((pair, wide), flat),
                    whole((8, 128)),
                ],
                [
                    sds((half_rows, width), BF16),
                    sds((half_rows, width), BF16),
                    sds((half_rows, joint), BF16),
                    sds((half_rows, routed), BF16),
                    sds((half_rows, 128), F32),
                    sds((half_rows, wide), BF16),
                    sds((8, 128), F32),
                ],
                1,
                1,
                "front",
            )(
                after(table, fronts[0][5]) if fronts else table,
                tokens, tokens, routes, segments, gain_attn, w_router, w_qkv,
            )
        )
    xr, a1, qkv, mask, lse, heads_out, score = [list(kind) for kind in zip(*fronts)]

    dyr, gm, dh = call(
        cot_pair_body,
        (4,),
        [
            pl.BlockSpec((length, width), lambda i, w: (w[2 * i], 0)),
            pl.BlockSpec((length, width), lambda i, w: (w[2 * i + 1], 0)),
            whole(routes.shape),
            pl.BlockSpec((pair, width), lambda i, w: (jnp.minimum(i, 1), 0)),
            pl.BlockSpec((pair, width), lambda i, w: (jnp.maximum(i - 2, 0), 0)),
            line,
            whole(w_down.shape),
        ],
        [
            pl.BlockSpec((pair, width), flat),
            pl.BlockSpec((pair, width), flat),
            pl.BlockSpec((pair, hidden), flat),
        ],
        [
            sds((2 * half_rows, width), BF16),
            sds((2 * half_rows, width), BF16),
            sds((2 * half_rows, hidden), F32),
        ],
        1,
        1,
        "cot",
    )(table, cotangent, cotangent, routes, xr[0], xr[1], w_router, w_down)

    mixed = []
    for stream in range(2):
        near, far = FIRST[stream], FIRST[1 - stream]
        beside = swap(heads_out[stream], "mp", near)
        across = swap(heads_out[stream], "mp", far)
        held = after(beside, heads_out[1] if stream == 0 else gm)
        corner = swap(held, "mp", far)
        parts = [heads_out[stream], None, None, corner]
        parts[near], parts[far] = held, across
        mixed.append(parts)

    mine = after(mine, heads_out[1])
    other = after(swap(mine, "dp", 1), gm)
    w_all = jnp.where(
        core == 0,
        jnp.concatenate([mine, other], axis=1),
        jnp.concatenate([other, mine], axis=1),
    )
    w_all = jnp.concatenate([w_out[None], w_all], axis=0).reshape(4 * wide, width)

    middles = []
    for stream in range(2):
        near = FIRST[stream]
        specs = []
        for part in range(4):
            crossed = part in (near, 3)
            specs.append(
                pl.BlockSpec((pair, wide), (lambda i, w: (1 - i, 0)) if crossed else flat)
            )
        middles.append(
            call(
                functools.partial(middle_pair_body, stream),
                (2,),
                specs
                + [
                    whole(w_all.shape),
                    pl.BlockSpec((pair, width), flat),
                    pl.BlockSpec((pair, hidden), lambda i, w, s=stream: (i + 2 * s, 0)),
                    line,
                    whole(w_up.shape),
                ],
                [
                    whole((routed, width)),
                    pl.BlockSpec((pair, width), flat),
                    pl.BlockSpec((pair, hidden), flat),
                    pl.BlockSpec((pair, hidden), flat),
                    whole((2, routed, width)),
                    whole((2, routed, width)),
                ],
                [
                    sds((routed, width), F32),
                    sds((half_rows, width), BF16),
                    sds((half_rows, hidden), BF16),
                    sds((half_rows, hidden), BF16),
                    sds((2, routed, width), BF16),
                    sds((2, routed, width), BF16),
                ],
                1,
                1,
                "middle",
            )(
                after(table, middles[0][5]) if middles else table,
                *mixed[stream], w_all, xr[stream], dh, gain_mlp, w_up,
            )
        )
    attn, a2, hid, du, send, keep = [list(kind) for kind in zip(*middles)]

    first_a = after(swap(send[0], "mp", FIRST[0]), keep[1])
    ahead_a = add(keep[0][1], first_a[1])
    final_a = swap(ahead_a, "mp", FIRST[1])

    gms = [gm[:half_rows], gm[half_rows:]]
    hid = [after(hid[0], ahead_a), hid[1]]
    grad_down = (dot(hid[0], gms[0], TN) + dot(hid[1], gms[1], TN)).astype(BF16)
    down = Total(grad_down, core, bit)
    du = [after(du[0], down.give), du[1]]
    grad_up = (dot(a2[0], du[0], TN) + dot(a2[1], du[1], TN)).astype(BF16)
    up = Total(grad_up, core, bit)

    first_b = after(swap(send[1], "mp", FIRST[1]), up.give)
    ahead_b = add(keep[1][1], first_b[1])
    final_b = swap(ahead_b, "mp", FIRST[0])

    down_far = down.split(ahead_b)
    hid = [after(hid[0], down_far), hid[1]]
    mlp_send = [dot(hid[s][:pair], w_down).astype(BF16).reshape(2, routed, width) for s in (0, 1)]
    mlp_keep = [dot(hid[s][pair:], w_down).astype(BF16).reshape(2, routed, width) for s in (0, 1)]
    up_far = up.split(*mlp_send, *mlp_keep)

    own_xr = pl.BlockSpec((routed, width), lambda i, w: (2, 0))
    own_dyr = [pl.BlockSpec((routed, width), lambda i, w, s=s: (2 + 4 * s, 0)) for s in (0, 1)]
    pieces = [
        pl.BlockSpec((1, routed, width), lambda i, w: (0, 0, 0)),
        pl.BlockSpec((1, routed, width), lambda i, w: (0, 0, 0)),
        whole((routed, width)),
    ] * 2
    rows_out = call(
        rows_pair_body,
        (1,),
        pieces
        + [whole((routed, width))] * 2
        + [own_xr, own_xr, *own_dyr, line, line, whole(w_all.shape)],
        [whole((pair, width)), whole((pair, width)), whole((8, width))]
        + [whole((pair, wide))] * 4,
        [sds((pair, width), F32), sds((pair, width), BF16), sds((8, width), F32)]
        + [sds((pair, wide), BF16)] * 4,
        1,
        1,
        "rows",
    )(
        after(table, up_far), keep[0], first_a, final_a, keep[1], first_b,
        final_b, *attn, *xr, dyr, dyr, gain_mlp, w_router, w_all,
    )
    dyn, ga, gain_two_part = rows_out[:3]
    dmix = [rows_out[3]] + [swap(rows_out[3 + j], "mp", j) for j in (1, 2, 3)]

    down_now = down.cross(ga)
    out_specs = [
        pl.BlockSpec((routed, wide), lambda i, w, at=STREAMS[s].index(j): (at, 0))
        for s in (0, 1)
        for j in range(4)
    ]
    outs_keep, outs_give = call(
        out_grad_body,
        (1,),
        out_specs + [whole((pair, width))],
        [whole((4, wide // 2, width))] * 2,
        [sds((4, wide // 2, width), BF16)] * 2,
        1,
        1,
        "outs",
    )(after(table, down_now), *mixed[0], *mixed[1], ga)
    outs_got = swap(outs_give, "dp", 1)
    dmix = [dmix[0]] + [after(value, outs_keep) for value in dmix[1:]]
    mlp_send = [after(value, *dmix[1:]) for value in mlp_send]
    mlp_first = [swap(mlp_send[s], "mp", FIRST[s]) for s in (0, 1)]

    backs = []
    for stream in range(2):
        cut = pl.BlockSpec((routed, wide), lambda i, w, s=stream: (s, 0))
        if stream == 0:
            gated = after(table, outs_keep)
        else:
            waited = backs[0][2]
            mlp_first = [after(value, waited) for value in mlp_first]
            mlp_ahead = [add(mlp_keep[s][1], mlp_first[s][1]) for s in (0, 1)]
            mlp_final = [swap(mlp_ahead[s], "mp", FIRST[1 - s]) for s in (0, 1)]
            up_now = up.cross(waited)
            gated = after(table, *mlp_ahead, up_now)
        backs.append(
            call(
                functools.partial(back_pair_body, heads, stream),
                (2,),
                [
                    pl.BlockSpec((pair, joint), flat),
                    pl.BlockSpec((pair, routed), flat),
                    pl.BlockSpec((pair, 128), flat),
                    cut,
                    cut,
                    cut,
                    cut,
                    whole(w_qkv.shape),
                ],
                [
                    pl.BlockSpec((pair, joint), flat),
                    whole((2, routed, width)),
                    whole((2, routed, width)),
                ],
                [
                    sds((half_rows, joint), BF16),
                    sds((2, routed, width), BF16),
                    sds((2, routed, width), BF16),
                ],
                1,
                1,
                "back",
            )(gated, qkv[stream], mask[stream], lse[stream], *dmix, w_qkv)
        )
    dqkv, back_send, back_keep = [list(kind) for kind in zip(*backs)]

    upd, base, router_part = call(
        delta_pair_body,
        (1,),
        pieces
        + [whole((routed, width))] * 2
        + [own_xr, own_xr, *own_dyr, whole((pair, width)), line],
        [whole((pair, width)), whole((pair, width)), whole((8, width))],
        [sds((pair, width), BF16), sds((pair, width), F32), sds((8, width), F32)],
        1,
        1,
        "delta",
    )(
        after(table, back_keep[1]), mlp_keep[0], mlp_first[0], mlp_final[0], mlp_keep[1],
        mlp_first[1], mlp_final[1], *attn, *xr, dyr, dyr, dyn, w_router,
    )

    last_first_a = after(swap(back_send[0], "mp", FIRST[0]), base)
    last_ahead_a = add(back_keep[0][1], last_first_a[1])
    last_final_a = swap(last_ahead_a, "mp", FIRST[1])
    upd_near = [swap(after(upd, last_ahead_a), "mp", j) for j in (1, 2)]

    dqkv = [after(dqkv[0], last_ahead_a), dqkv[1]]
    grad_qkv = (dot(a1[0], dqkv[0], TN) + dot(a1[1], dqkv[1], TN)).astype(BF16)
    whole_qkv = Total(grad_qkv, core, bit)

    last_first_b = after(swap(back_send[1], "mp", FIRST[1]), whole_qkv.give)
    last_ahead_b = add(back_keep[1][1], last_first_b[1])
    last_final_b = swap(last_ahead_b, "mp", FIRST[0])
    down_now = down.close(last_ahead_b)
    outs_got = after(outs_got, down_now)
    outs_half = [add(outs_keep[j], outs_got[j]) for j in range(4)]
    qkv_far = whole_qkv.split(down_now, *outs_half)

    last, gain_one_part = call(
        last_pair_body,
        (1,),
        pieces + [own_xr, own_xr, whole((pair, width)), line],
        [whole((pair, width)), whole((8, width))],
        [sds((pair, width), BF16), sds((8, width), F32)],
        1,
        1,
        "last",
    )(
        after(table, qkv_far), back_keep[0], last_first_a, last_final_a, back_keep[1],
        last_first_b, last_final_b, *xr, base, gain_attn,
    )

    scores = score[0] + score[1]
    scores = jnp.concatenate([scores[0:1], scores[1:2] / 4], axis=1)
    scores = jnp.pad(scores, ((0, 4), (0, width - 256)))
    lines = jnp.sum(jnp.stack([gain_one_part, gain_two_part, router_part]), axis=1)
    small = jnp.concatenate([lines, scores], axis=0)
    small_hops = [("dp", 1), ("dp", 2), ("dp", 4), ("mp", 1), ("mp", 2)]

    def small_hop(small, *others):
        axis, offset = small_hops.pop(0)
        return small + after(swap(small, axis, offset), *others)

    def corner_of(near_rows, *others):
        left, right = [after(rows, *others) for rows in near_rows]
        corner = [swap(left[:routed], "mp", 2), swap(right[routed:], "mp", 1)]
        return [left, right], corner

    def put(source, parts, target, name, *others):
        return place_rows(after(table, *others), source, routes, parts, target, name)

    upd_near, upd_corner = corner_of(upd_near, last)
    last_near = [swap(last, "mp", j) for j in (1, 2)]
    output = put(tokens, [(upd, 0), (upd_near[0], 2)], None, "put_out", last)
    up_now = up.close(output)
    side = down.back(output)
    out_sent = [swap(after(outs_half[j], *last_near), "mp", j) for j in (1, 2, 3)]
    small = small_hop(small, output)
    output = put(
        tokens,
        [(upd_near[1], 4), (upd_corner[0], 6), (upd_corner[1], 7)],
        output,
        "put_out",
        up_now, side, small,
    )
    qkv_now = whole_qkv.cross(output)
    small = small_hop(small, output)
    last_near, last_corner = corner_of(last_near, output)
    grads = put(
        cotangent,
        [(last, 0), (last_near[0], 2), (last_near[1], 4)],
        None,
        "put_grad",
        qkv_now, small, *last_corner,
    )
    side = up.back(grads)
    out_half = outs_half[0].astype(F32)
    for got in out_sent:
        out_half = out_half + after(got, output).astype(F32)
    out_half = out_half.astype(BF16)
    out_half = add(out_half, after(swap(out_half, "dp", 2), grads))
    qkv_now = whole_qkv.close(grads)
    small = small_hop(small, grads)
    grad_down = join(after(table, side, qkv_now, small), down.pieces(), QUARTER)
    small = small_hop(small, grad_down)
    out_half = add(out_half, after(swap(out_half, "dp", 4), grad_down))
    side = whole_qkv.back(grad_down)
    grads = put(
        cotangent,
        [(last_corner[0], 6), (last_corner[1], 7)],
        grads,
        "put_grad",
        small, out_half, side,
    )
    small = small_hop(small, grads)
    grad_up = join(after(table, grads), up.pieces(), QUARTER)
    grad_qkv = join(after(table, grad_up), whole_qkv.pieces(), QUARTER)
    grad_out = join(after(table, grad_qkv), [out_half, swap(out_half, "dp", 1)], 14)

    score_total = small[3, 0]
    routed_total = small[3, 128]
    token_count = seqs * length * lax.axis_size("dp")
    return (
        output,
        grads,
        small[0],
        small[1],
        small[2],
        grad_qkv,
        grad_out,
        grad_up,
        grad_down,
        routed_total / score_total,
        score_total / token_count,
    )


def shards(*arrays):
    segments, routes, w_out = arrays[1], arrays[2], arrays[8]
    square = lax.axis_size("mp") == 4 and segments.shape[0] == 8 and lax.axis_size("dp") == 8
    if square and routes.shape[1] % 128 == 0 and w_out.shape[0] % 128 == 0:
        return paired(*arrays)
    return general(*arrays)


def solution(mesh):
    rows = P("dp", None)
    columns = P(None, "mp")
    lines = P("mp", None)
    in_specs = (rows, rows, rows, rows, P(), P(), P(), columns, lines, columns, lines)
    out_specs = (rows, rows, P(), P(), P(), columns, lines, columns, lines, P(), P())
    return jax.shard_map(shards, mesh=mesh, in_specs=in_specs, out_specs=out_specs, check_vma=False)
```

```python
import functools

import jax
import jax.numpy as jnp
from jax import lax
from jax.experimental import pallas as pl
from jax.experimental.pallas import tpu as pltpu
from jax.sharding import PartitionSpec as P

HD = 64
EPS = 1e-06
SCALE = HD ** (-0.5)
GELU_C = (2.0 / 3.141592653589793) ** 0.5
GELU_A = 0.044715
F32 = jnp.float32
BF16 = jnp.bfloat16


def dot(left, right, on=((1,), (0,))):
    return lax.dot_general(left, right, (on, ((), ())), preferred_element_type=F32)


NT = ((1,), (1,))
TN = ((0,), (0,))


def iota(shape, axis):
    return lax.broadcasted_iota(jnp.int32, shape, axis)


def sigmoid(value):
    return 1.0 / (1.0 + jnp.exp(-value))


def call(body, grid, in_specs, out_specs, out_shape, flops, nbytes, name, scratch=(), alias=None):
    return pl.pallas_call(
        body,
        grid_spec=pltpu.PrefetchScalarGridSpec(
            num_scalar_prefetch=1,
            grid=grid,
            in_specs=in_specs,
            out_specs=out_specs,
            scratch_shapes=list(scratch),
        ),
        out_shape=out_shape,
        cost_estimate=pl.CostEstimate(
            flops=int(flops), bytes_accessed=int(nbytes), transcendentals=0
        ),
        input_output_aliases=alias or {},
        name=name,
    )


def whole(shape):
    zeros = (0,) * len(shape)
    return pl.BlockSpec(shape, lambda *_: zeros)


def one_hot_rows(routes_row, length):
    routed = routes_row.shape[1]
    eye = iota((routed, routed), 0) == iota((routed, routed), 1)
    column = jnp.sum(jnp.where(eye, routes_row.astype(F32), 0.0), axis=1, keepdims=True)
    return iota((routed, length), 1) == column.astype(jnp.int32), eye


def head_mask(hot, eye, seg_line):
    seg_col = jnp.sum(jnp.where(hot, seg_line, 0.0), axis=1, keepdims=True)
    seg_row = jnp.sum(jnp.where(eye, seg_col, 0.0), axis=0, keepdims=True)
    routed = eye.shape[0]
    causal = iota((routed, routed), 0) >= iota((routed, routed), 1)
    return causal & (seg_col == seg_row)


def softmax_head(query, key, allowed):
    logits = jnp.where(allowed, dot(query, key, NT) * SCALE, -1e30)
    expon = jnp.exp(logits - jnp.max(logits, axis=1, keepdims=True))
    return expon / jnp.sum(expon, axis=1, keepdims=True)


def front_body(
    heads, slice_rows, where, tokens, routes, segments, gain, router, w_qkv,
    xr_out, a1_out, qkv_out, mask_out, mixed_out, score_out,
):
    step = pl.program_id(0)
    length = tokens.shape[0]
    hot, eye = one_hot_rows(routes[pl.ds(step, 1), :], length)
    seg_line = segments[pl.ds(step, 1), :].astype(F32)
    allowed = head_mask(hot, eye, seg_line)
    mask_out[...] = jnp.where(allowed, 1.0, 0.0).astype(BF16)
    rows = dot(jnp.where(hot, 1.0, 0.0).astype(BF16), tokens[...])
    xr_out[...] = rows.astype(BF16)
    vec = router[...].astype(F32)
    start = pl.multiple_of(where[0] * slice_rows, slice_rows)
    part = tokens[pl.ds(start, slice_rows), :].astype(F32)
    total = jnp.sum(sigmoid(jnp.sum(part * vec, axis=1, keepdims=True)), axis=0, keepdims=True)
    chosen = jnp.sum(sigmoid(jnp.sum(rows * vec, axis=1, keepdims=True)), axis=0, keepdims=True)

    @pl.when(step == 0)
    def _():
        score_out[...] = jnp.zeros_like(score_out)

    which = iota(score_out.shape, 0)
    score_out[...] += jnp.where(which == 0, total, jnp.where(which == 1, chosen, 0.0))
    inverse = lax.rsqrt(jnp.mean(rows * rows, axis=1, keepdims=True) + EPS)
    normed = (rows * inverse * gain[...].astype(F32)).astype(BF16)
    a1_out[...] = normed
    joint = dot(normed, w_qkv[...]).astype(BF16)
    qkv_out[...] = joint
    for head in range(heads):
        base = head * 3 * HD
        query = joint[:, base : base + HD]
        key = joint[:, base + HD : base + 2 * HD]
        value = joint[:, base + 2 * HD : base + 3 * HD]
        probs = softmax_head(query, key, allowed).astype(BF16)
        mixed_out[:, head * HD : (head + 1) * HD] = dot(probs, value).astype(BF16)


def cot_body(where, cotangent, routes, xr, router, w_down, dyr_out, gm_out, dh_out):
    step = pl.program_id(0)
    hot, _ = one_hot_rows(routes[pl.ds(step, 1), :], cotangent.shape[0])
    rows = dot(jnp.where(hot, 1.0, 0.0).astype(BF16), cotangent[...])
    dyr_out[...] = rows.astype(BF16)
    vec = router[...].astype(F32)
    rate = sigmoid(jnp.sum(xr[...].astype(F32) * vec, axis=1, keepdims=True))
    low = (rate * rows).astype(BF16)
    gm_out[...] = low
    dh_out[...] = dot(low, w_down[...], NT)


def middle_body(parts, table, *refs):
    mixed = refs[:parts]
    w_out, xr, dh, gain, w_up = refs[parts : parts + 5]
    attn_out, a2_out, hid_out, du_out, da2_out, gain_out = refs[parts + 5 :]
    attn = dot(mixed[0][...], w_out[0])
    for part in range(1, parts):
        attn = attn + dot(mixed[part][...], w_out[part])
    attn_out[...] = attn
    y = xr[...].astype(F32) + attn
    scaled = y * lax.rsqrt(jnp.mean(y * y, axis=1, keepdims=True) + EPS)
    a2 = (scaled * gain[...].astype(F32)).astype(BF16)
    a2_out[...] = a2
    u = dot(a2, w_up[...])
    square = u * u
    t = jnp.tanh(GELU_C * (u + GELU_A * (u * square)))
    hid_out[...] = (0.5 * u * (1.0 + t)).astype(BF16)
    slope = 0.5 * (1.0 + t) + (0.5 * GELU_C) * u * (1.0 - t * t) * (1.0 + 3.0 * GELU_A * square)
    du = (dh[...] * slope).astype(BF16)
    du_out[...] = du
    da2 = dot(du, w_up[...], NT)
    da2_out[0] = da2.astype(BF16)

    @pl.when(pl.program_id(0) == 0)
    def _():
        gain_out[...] = jnp.zeros_like(gain_out)

    gain_out[...] += jnp.sum((da2 * scaled).reshape(-1, 8, da2.shape[1]), axis=0)


def rows_body(parts, where, *refs):
    pieces = refs[:parts]
    attn, xr, dyr, gain, router, w_out = refs[parts : parts + 6]
    dyn_out, ga_out, do_out = refs[parts + 6 :]
    da2 = pieces[0][...].astype(F32)
    for piece in pieces[1:]:
        da2 = da2 + piece[...].astype(F32)
    rows = xr[...].astype(F32)
    y = rows + attn[...]
    inverse = lax.rsqrt(jnp.mean(y * y, axis=1, keepdims=True) + EPS)
    t = gain[...].astype(F32) * da2
    scaled = y * inverse
    dyn = inverse * (t - scaled * jnp.mean(t * scaled, axis=1, keepdims=True))
    dyn_out[...] = dyn
    rate = sigmoid(jnp.sum(rows * router[...].astype(F32), axis=1, keepdims=True))
    ga = (rate * dyr[...].astype(F32) + dyn).astype(BF16)
    ga_out[...] = ga
    for part in range(parts):
        do_out[part] = dot(ga, w_out[part], NT).astype(BF16)


def delta_body(parts, where, *refs):
    pieces = refs[:parts]
    attn, xr, dyr, dyn, router = refs[parts : parts + 5]
    upd_out, base_out, grad_router_out = refs[parts + 5 :]
    delta = attn[...]
    for piece in pieces:
        delta = delta + piece[...].astype(F32)
    rows = xr[...].astype(F32)
    grads = dyr[...].astype(F32)
    vec = router[...].astype(F32)
    rate = sigmoid(jnp.sum(rows * vec, axis=1, keepdims=True))
    upd_out[...] = (rows + rate * delta).astype(BF16)
    dlogit = jnp.sum(grads * delta, axis=1, keepdims=True) * rate * (1.0 - rate)
    base_out[...] = grads + dyn[...] + dlogit * vec

    @pl.when(pl.program_id(0) == 0)
    def _():
        grad_router_out[...] = jnp.zeros_like(grad_router_out)

    grad_router_out[...] += jnp.sum((dlogit * rows).reshape(-1, 8, rows.shape[1]), axis=0)


def back_body(heads, where, qkv, mask, dmixed, xr, gain, w_qkv, dqkv_out, da1_out, gain_out):
    joint = qkv[...]
    allowed = mask[...].astype(F32) > 0.5
    grads = dmixed[0]
    pieces = []
    for head in range(heads):
        base = head * 3 * HD
        query = joint[:, base : base + HD]
        key = joint[:, base + HD : base + 2 * HD]
        value = joint[:, base + 2 * HD : base + 3 * HD]
        dmix = grads[:, head * HD : (head + 1) * HD]
        probs = softmax_head(query, key, allowed)
        dprobs = dot(dmix, value, NT)
        spread = jnp.sum(probs * dprobs, axis=1, keepdims=True)
        dlog = (probs * (dprobs - spread)).astype(BF16)
        dquery = dot(dlog, key) * SCALE
        dkey = dot(dlog, query, TN) * SCALE
        dvalue = dot(probs.astype(BF16), dmix, TN)
        pieces += [dquery.astype(BF16), dkey.astype(BF16), dvalue.astype(BF16)]
    for at, piece in enumerate(pieces):
        dqkv_out[:, at * HD : (at + 1) * HD] = piece
    da1 = dot(dqkv_out[...], w_qkv[...], NT)
    da1_out[0] = da1.astype(BF16)
    rows = xr[...].astype(F32)
    scaled = rows * lax.rsqrt(jnp.mean(rows * rows, axis=1, keepdims=True) + EPS)

    @pl.when(pl.program_id(0) == 0)
    def _():
        gain_out[...] = jnp.zeros_like(gain_out)

    gain_out[...] += jnp.sum((da1 * scaled).reshape(-1, 8, da1.shape[1]), axis=0)


def last_body(parts, where, *refs):
    pieces = refs[:parts]
    xr, base, gain = refs[parts : parts + 3]
    (out,) = refs[parts + 3 :]
    da1 = pieces[0][...].astype(F32)
    for piece in pieces[1:]:
        da1 = da1 + piece[...].astype(F32)
    rows = xr[...].astype(F32)
    inverse = lax.rsqrt(jnp.mean(rows * rows, axis=1, keepdims=True) + EPS)
    t = gain[...].astype(F32) * da1
    scaled = rows * inverse
    dxn = inverse * (t - scaled * jnp.mean(t * scaled, axis=1, keepdims=True))
    out[...] = (base[...] + dxn).astype(BF16)


def put_body(where, source, routes, rows, *refs):
    out = refs[-1]
    length = source.shape[0]
    at = where[pl.program_id(0)]
    line = routes[pl.ds(at, 1), :]
    hot = iota((length, line.shape[1]), 0) == line
    picked = jnp.where(hot, 1.0, 0.0)
    taken = jnp.sum(picked, axis=1, keepdims=True) > 0.5
    moved = dot(picked.astype(BF16), rows[...])
    out[...] = jnp.where(taken, moved, source[...].astype(F32)).astype(BF16)


def put_rows(source, routes, rows, order, target, name):
    seqs, routed = routes.shape
    length = source.shape[0] // seqs
    width = source.shape[1]
    count = rows.shape[0] // routed
    in_specs = [
        pl.BlockSpec((length, width), lambda i, w: (w[i], 0)),
        whole(routes.shape),
        pl.BlockSpec((routed, width), lambda i, w: (i, 0)),
    ]
    args = [order, source, routes, rows]
    alias = None
    if target is not None:
        in_specs.append(pl.BlockSpec(memory_space=pl.ANY))
        args.append(target)
        alias = {4: 0}
    return call(
        put_body,
        (count,),
        in_specs,
        pl.BlockSpec((length, width), lambda i, w: (w[i], 0)),
        jax.ShapeDtypeStruct(source.shape, BF16),
        2 * count * length * routed * width,
        count * length * width * 4,
        name,
        alias=alias,
    )(*args)


def swap(value, axis, offset):
    size = lax.axis_size(axis)
    return lax.ppermute(value, axis, [(i, i ^ offset) for i in range(size)])


def block_of(value, index, rows):
    return lax.dynamic_slice_in_dim(value, index * rows, rows, 0)


def in_core_order(core, mine, other):
    return jnp.where(
        core == 0,
        jnp.concatenate([mine, other], axis=0),
        jnp.concatenate([other, mine], axis=0),
    )


def line_sum(value, depth):
    at = lax.axis_index("dp") // 2
    half = depth // 2

    def shift(array, pairs):
        return lax.ppermute(
            array, "dp", [(2 * a + c, 2 * b + c) for a, b in pairs for c in range(2)]
        )

    def mirrored(a, b):
        return [(a, b), (depth - 1 - a, depth - 1 - b)]

    for step in range(half - 1):
        got = shift(value, mirrored(step, step + 1))
        value = (value.astype(F32) + got.astype(F32)).astype(BF16)
    if depth > 1:
        got = shift(value, mirrored(half - 1, half))
        value = (value.astype(F32) + got.astype(F32)).astype(BF16)
    for step in reversed(range(half - 1)):
        got = shift(value, mirrored(step + 1, step))
        here = (at == step) | (at == depth - 1 - step)
        value = jnp.where(here, got, value)
    return value


def core_half(value, core):
    half = value.shape[0] // 2
    keep = block_of(value, core, half)
    give = block_of(value, 1 - core, half)
    got = swap(give.astype(BF16), "dp", 1)
    return (keep.astype(F32) + got.astype(F32)).astype(BF16)


def core_join(value, core):
    return in_core_order(core, value, swap(value, "dp", 1)).astype(F32)


def general(
    tokens, segments, routes, cotangent, gain_attn, gain_mlp, w_router, w_qkv, w_out, w_up, w_down
):
    seqs, length = segments.shape
    routed = routes.shape[1]
    width = tokens.shape[1]
    total = seqs * routed
    wide = w_out.shape[0]
    heads = wide // HD
    joint = w_qkv.shape[1]
    hidden = w_up.shape[1]
    parts = lax.axis_size("mp")
    depth = lax.axis_size("dp") // 2
    own = total // parts
    rank = lax.axis_index("mp")
    core = lax.axis_index("dp") % 2
    aligned = own % routed == 0
    per = own // routed if aligned else 1
    where = rank.reshape(1).astype(jnp.int32)
    gain_one = gain_attn.reshape(1, width)
    gain_two = gain_mlp.reshape(1, width)
    router = w_router.reshape(1, width)
    partners = list(range(1, parts))
    sds = jax.ShapeDtypeStruct

    share = block_of(w_out, core, wide // 2)
    mine = jnp.stack([swap(share, "mp", j) for j in partners])
    other = swap(mine, "dp", 1)
    w_all = jnp.where(
        core == 0,
        jnp.concatenate([mine, other], axis=1),
        jnp.concatenate([other, mine], axis=1),
    )
    w_all = jnp.concatenate([w_out[None], w_all], axis=0)

    xr, a1, qkv, mask, mixed, score = call(
        functools.partial(front_body, heads, length // parts),
        (seqs,),
        [
            pl.BlockSpec((length, width), lambda i, w: (i, 0)),
            whole(routes.shape),
            whole(segments.shape),
            whole((1, width)),
            whole((1, width)),
            whole(w_qkv.shape),
        ],
        [
            pl.BlockSpec((routed, width), lambda i, w: (i, 0)),
            pl.BlockSpec((routed, width), lambda i, w: (i, 0)),
            pl.BlockSpec((routed, joint), lambda i, w: (i, 0)),
            pl.BlockSpec((routed, routed), lambda i, w: (i, 0)),
            pl.BlockSpec((routed, wide), lambda i, w: (i, 0)),
            whole((8, 128)),
        ],
        [
            sds((total, width), BF16),
            sds((total, width), BF16),
            sds((total, joint), BF16),
            sds((total, routed), BF16),
            sds((total, wide), BF16),
            sds((8, 128), F32),
        ],
        2 * total * width * (length + joint) * 1.3,
        2 * seqs * length * width + 8 * total * width,
        "front",
    )(where, tokens, routes, segments, gain_one, router, w_qkv)

    mixed_all = [mixed] + [swap(mixed, "mp", j) for j in partners]

    dyr, gm, dh = call(
        cot_body,
        (seqs,),
        [
            pl.BlockSpec((length, width), lambda i, w: (i, 0)),
            whole(routes.shape),
            pl.BlockSpec((routed, width), lambda i, w: (i, 0)),
            whole((1, width)),
            whole(w_down.shape),
        ],
        [
            pl.BlockSpec((routed, width), lambda i, w: (i, 0)),
            pl.BlockSpec((routed, width), lambda i, w: (i, 0)),
            pl.BlockSpec((routed, hidden), lambda i, w: (i, 0)),
        ],
        [sds((total, width), BF16), sds((total, width), BF16), sds((total, hidden), F32)],
        2 * total * width * (length + hidden),
        2 * seqs * length * width + 6 * total * width + 4 * total * hidden,
        "cot",
    )(where, cotangent, routes, xr, router, w_down)

    order = partners[::-1] + [0]
    tile = min(own, 128)
    tiles = own // tile
    blocks = jnp.stack([rank ^ j for j in order])
    table = (blocks[:, None] * tiles + jnp.arange(tiles)[None, :]).reshape(-1).astype(jnp.int32)

    def by_row(i, t):
        return (t[i], 0)

    steps = parts * tiles
    attn, a2, hid, du, da2, gain_two_part = call(
        functools.partial(middle_body, parts),
        (steps,),
        [pl.BlockSpec((tile, wide), by_row)] * parts
        + [
            whole(w_all.shape),
            pl.BlockSpec((tile, width), by_row),
            pl.BlockSpec((tile, hidden), by_row),
            whole((1, width)),
            whole(w_up.shape),
        ],
        [
            pl.BlockSpec((tile, width), lambda i, t: (jnp.maximum(i - (steps - tiles), 0), 0)),
            pl.BlockSpec((tile, width), by_row),
            pl.BlockSpec((tile, hidden), by_row),
            pl.BlockSpec((tile, hidden), by_row),
            pl.BlockSpec((1, tile, width), lambda i, t: (i // tiles, i % tiles, 0)),
            whole((8, width)),
        ],
        [
            sds((own, width), F32),
            sds((total, width), BF16),
            sds((total, hidden), BF16),
            sds((total, hidden), BF16),
            sds((parts, own, width), BF16),
            sds((8, width), F32),
        ],
        2 * total * width * (parts * wide + 2 * hidden),
        total * (10 * width + 8 * hidden) + 2 * width * (hidden + parts * wide),
        "middle",
    )(table, *mixed_all, w_all, xr, dh, gain_two, w_up)

    da2_all = [da2[-1]] + [swap(da2[at], "mp", j) for at, j in enumerate(order[:-1])]

    mlp = dot(hid, w_down).astype(BF16)
    grad_up = dot(a2, du, TN).astype(BF16)
    grad_down = dot(hid, gm, TN).astype(BF16)
    mlp_all = [block_of(mlp, rank, own)] + [
        swap(block_of(mlp, rank ^ j, own), "mp", j) for j in partners
    ]

    own_tiles = lambda i, w: (w[0] * tiles + i, 0)
    flat = lambda i, w: (i, 0)
    row_block = pl.BlockSpec((tile, width), flat)
    own_block = pl.BlockSpec((tile, width), own_tiles)
    dyn, ga, dmix = call(
        functools.partial(rows_body, parts),
        (tiles,),
        [row_block] * parts
        + [row_block, own_block, own_block, whole((1, width)), whole((1, width)), whole(w_all.shape)],
        [row_block, row_block, pl.BlockSpec((parts, tile, wide), lambda i, w: (0, i, 0))],
        [sds((own, width), F32), sds((own, width), BF16), sds((parts, own, wide), BF16)],
        2 * own * width * parts * wide,
        own * width * 24 + 2 * width * width,
        "rows",
    )(where, *da2_all, attn, xr, dyr, gain_two, router, w_all)

    dmix_all = jnp.stack([dmix[0]] + [swap(dmix[j], "mp", j) for j in partners])

    upd, base, router_part = call(
        functools.partial(delta_body, parts),
        (tiles,),
        [row_block] * parts + [row_block, own_block, own_block, row_block, whole((1, width))],
        [row_block, row_block, whole((8, width))],
        [sds((own, width), BF16), sds((own, width), F32), sds((8, width), F32)],
        own * width * 20,
        own * width * 24,
        "delta",
    )(where, *mlp_all, attn, xr, dyr, dyn, router)
    upd_all = [upd] + [swap(upd, "mp", j) for j in partners]

    if aligned:
        by_owner = lambda i, w: ((i // per) ^ w[0], i % per, 0)
        da1_shape = (parts, own, width)
    else:
        dmix_all = dmix_all[jnp.arange(parts) ^ rank].reshape(1, total, wide)
        by_owner = lambda i, w: (0, i, 0)
        da1_shape = (1, total, width)
    dqkv, da1, gain_one_part = call(
        functools.partial(back_body, heads),
        (seqs,),
        [
            pl.BlockSpec((routed, joint), flat),
            pl.BlockSpec((routed, routed), flat),
            pl.BlockSpec((1, routed, wide), by_owner),
            pl.BlockSpec((routed, width), flat),
            whole((1, width)),
            whole(w_qkv.shape),
        ],
        [
            pl.BlockSpec((routed, joint), flat),
            pl.BlockSpec((1, routed, width), by_owner),
            whole((8, width)),
        ],
        [sds((total, joint), BF16), sds(da1_shape, BF16), sds((8, width), F32)],
        2 * total * width * joint * 1.5,
        total * (4 * joint + 6 * width) + 2 * width * joint,
        "back",
    )(where, qkv, mask, dmix_all, xr, gain_one, w_qkv)

    if aligned:
        da1_blocks = [da1[j] for j in range(parts)]
    else:
        da1_blocks = [block_of(da1[0], rank ^ j, own) for j in range(parts)]
    da1_all = [da1_blocks[0]] + [swap(da1_blocks[j], "mp", j) for j in partners]

    grad_qkv = dot(a1, dqkv, TN).astype(BF16)

    last = call(
        functools.partial(last_body, parts),
        (tiles,),
        [row_block] * parts + [own_block, row_block, whole((1, width))],
        row_block,
        sds((own, width), BF16),
        own * width * 20,
        own * width * 18,
        "last",
    )(where, *da1_all, xr, base, gain_one)
    last_all = [last] + [swap(last, "mp", j) for j in partners]

    def spread(source, rows_all, name):
        if not aligned:
            rows = jnp.stack(rows_all)[jnp.arange(parts) ^ rank].reshape(total, width)
            return put_rows(source, routes, rows, jnp.arange(seqs, dtype=jnp.int32), None, name)
        target = None
        for j, rows in enumerate(rows_all):
            seq = ((rank ^ j) * per + jnp.arange(per)).astype(jnp.int32)
            target = put_rows(source, routes, rows, seq, target, name)
        return target

    output = spread(tokens, upd_all, "put_out")
    grad_tokens = spread(cotangent, last_all, "put_grad")

    grad_up = core_join(line_sum(core_half(grad_up, core), depth), core)
    grad_down = core_join(line_sum(core_half(grad_down, core), depth), core)
    grad_qkv = core_join(line_sum(core_half(grad_qkv, core), depth), core)

    def out_part(j):
        rows = block_of(mixed_all[j], rank, own)
        return dot(rows, ga, TN).astype(BF16)

    outs = jnp.stack([out_part(j) for j in range(parts)], axis=1)
    outs = core_half(outs, core)
    half = outs[:, 0].astype(F32)
    for j in partners:
        half = half + swap(outs[:, j], "mp", j).astype(F32)
    grad_out = core_join(line_sum(half.astype(BF16), depth), core)

    lines = jnp.sum(
        jnp.stack([gain_one_part, gain_two_part, router_part]), axis=1
    )
    scores = jnp.concatenate(
        [score[0:1] / 1.0, score[1:2] / parts, jnp.zeros((6, 128), F32)], axis=0
    ).reshape(1, -1)
    scores = jnp.pad(scores, ((0, 0), (0, width - 1024))) if width > 1024 else scores[:, :width]
    small = jnp.concatenate([lines, scores, jnp.zeros((4, width), F32)], axis=0)
    bit = 1
    while bit < 2 * depth:
        small = small + swap(small, "dp", bit)
        bit *= 2
    bit = 1
    while bit < parts:
        small = small + swap(small, "mp", bit)
        bit *= 2
    score_total = small[3, 0]
    routed_total = small[3, 128]
    token_count = seqs * length * lax.axis_size("dp")
    return (
        output,
        grad_tokens,
        small[0],
        small[1],
        small[2],
        grad_qkv,
        grad_out,
        grad_up,
        grad_down,
        routed_total / score_total,
        score_total / token_count,
    )


STREAMS = ((1, 3, 0, 2), (2, 3, 0, 1))
FIRST = (1, 2)


def row(vector):
    return vector[...].astype(F32).reshape(1, -1)

def owner_spec(stream, rows, columns, slots=()):
    lead = tuple(slots)
    zeros = (0,) * len(lead)
    if stream == 0:
        return pl.BlockSpec(
            lead + (2, None, None, rows, columns), lambda i, w: zeros + (0, 1 - i, 0, 0, 0)
        )
    return pl.BlockSpec(
        lead + (None, 2, None, rows, columns), lambda i, w: zeros + (1 - i, 0, 1, 0, 0)
    )


def joined(value):
    return value.reshape(-1, value.shape[-1])


def parted(value):
    return value.reshape(2, -1, value.shape[-1])


def front_pair_body(heads, slice_rows, first, where, *refs):
    blocks = refs[:2]
    routes, segments, gain, router, w_qkv = refs[2:7]
    xr_out, give_out, keep_out, qkv_out, mask_out, lse_out, mixed_out, score_out = refs[-8:]
    step = pl.program_id(0)
    length, width = blocks[0].shape
    routed = routes.shape[1]
    vec = jnp.broadcast_to(row(router), (8, width)).astype(BF16)
    start = pl.multiple_of(where[RANK] * slice_rows, slice_rows)
    rows_all, allowed_all = [], []
    total = jnp.zeros((8, 1), F32)
    for at, tokens in enumerate(blocks):
        seq = where[first + 2 * step + at]
        hot, eye = one_hot_rows(routes[pl.ds(seq, 1), :], length)
        seg_line = segments[pl.ds(seq, 1), :].astype(F32)
        allowed = head_mask(hot, eye, seg_line)
        mask_out[at * routed : (at + 1) * routed, :] = jnp.where(allowed, 1.0, 0.0).astype(BF16)
        rows_all.append(dot(jnp.where(hot, 1.0, 0.0).astype(BF16), tokens[...]))
        allowed_all.append(allowed)
        scored = sigmoid(dot(vec, tokens[pl.ds(start, slice_rows), :], NT))
        total = total + jnp.sum(scored, axis=1, keepdims=True)
    rows = jnp.concatenate(rows_all, axis=0)
    low = rows.astype(BF16)
    xr_out[...] = parted(low)
    chosen = jnp.sum(sigmoid(dot(vec, low, NT)), axis=1, keepdims=True)

    @pl.when(step == 0)
    def _():
        score_out[...] = jnp.zeros_like(score_out)

    which = iota(score_out.shape, 0)
    score_out[...] += jnp.where(which == 0, total, jnp.where(which == 1, chosen, 0.0))
    inverse = lax.rsqrt(jnp.mean(rows * rows, axis=1, keepdims=True) + EPS)
    normed = (rows * inverse * row(gain)).astype(BF16)
    left, right = parted(normed[:, : width // 2]), parted(normed[:, width // 2 :])
    give_out[...] = jnp.where(where[CORE] == 0, right, left)
    keep_out[...] = jnp.where(where[CORE] == 0, left, right)
    joint = dot(normed, w_qkv[...]).astype(BF16)
    qkv_out[...] = joint
    logits = []
    for at in range(2):
        own = joint[at * routed : (at + 1) * routed]
        for head in range(heads):
            base = head * 3 * HD
            raw = dot(own[:, base : base + HD], own[:, base + HD : base + 2 * HD], NT)
            logits.append(jnp.where(allowed_all[at], raw * SCALE, -1e30))
    logits = jnp.concatenate(logits, axis=0)
    top = jnp.max(logits, axis=1, keepdims=True)
    expon = jnp.exp(logits - top)
    norm = jnp.sum(expon, axis=1, keepdims=True)
    sums = top + jnp.log(norm)
    probs = (expon * (1.0 / norm)).astype(BF16)
    for at in range(2):
        span = slice(at * routed, (at + 1) * routed)
        for head in range(heads):
            place = slice((at * heads + head) * routed, (at * heads + head + 1) * routed)
            base = head * 3 * HD
            value = joint[span, base + 2 * HD : base + 3 * HD]
            lse_out[span, head : head + 1] = sums[place]
            mixed_out[span, head * HD : (head + 1) * HD] = dot(probs[place], value).astype(BF16)


def cot_pair_body(where, *refs):
    blocks = refs[:2]
    routes, xr, router, w_down, dyr_out, gm_out, dh_out = refs[2:]
    step = pl.program_id(0)
    length = blocks[0].shape[0]
    picked = []
    for at, block in enumerate(blocks):
        hot, _ = one_hot_rows(routes[pl.ds(where[PUT + 2 * step + at], 1), :], length)
        picked.append(dot(jnp.where(hot, 1.0, 0.0).astype(BF16), block[...]))
    rows = jnp.concatenate(picked, axis=0)
    dyr_out[...] = rows.astype(BF16)
    rate = sigmoid(jnp.sum(xr[...].astype(F32) * row(router), axis=1, keepdims=True))
    low = (rate * rows).astype(BF16)
    gm_out[...] = low
    dh_out[...] = dot(low, w_down[...], NT)


def flip(value, swapped):
    half = value.shape[0] // 2
    if swapped:
        return jnp.concatenate([value[half:], value[:half]], axis=0)
    return value


def middle_pair_body(stream, where, *refs):
    mixed = refs[:4]
    w_parts = refs[4:8]
    xr, dh, gm, gain, w_up = refs[8:13]
    attn_out, left_give, left_keep, right_give, right_keep, hid_out, send_out, keep_out = refs[-8:]
    step = pl.program_id(0)
    plain = (0, FIRST[stream])
    attn = 0.0
    for part in range(4):
        attn = attn + dot(flip(mixed[part][...], part not in plain), w_parts[part][...])
    half = attn.shape[0] // 2
    attn_out[...] = attn[:half]
    y = joined(xr[...]).astype(F32) + attn
    scaled = y * lax.rsqrt(jnp.mean(y * y, axis=1, keepdims=True) + EPS)
    a2 = (scaled * row(gain)).astype(BF16)
    u = dot(a2, w_up[...])
    square = u * u
    t = jnp.tanh(u * (GELU_C + (GELU_C * GELU_A) * square))
    cdf = 0.5 + 0.5 * t
    hid = (u * cdf).astype(BF16)
    hid_out[...] = parted(hid)
    slope = cdf + (u * (1.0 - t * t)) * (0.5 * GELU_C + (1.5 * GELU_C * GELU_A) * square)
    du = (joined(dh[...]) * slope).astype(BF16)
    low = dot(du, w_up[...], NT).astype(BF16)
    first = where[CORE] == 0
    left_give[...] = parted(jnp.where(first, a2, hid))
    left_keep[...] = parted(jnp.where(first, hid, a2))
    down = joined(gm[...])
    right_give[...] = parted(jnp.where(first, du, down))
    right_keep[...] = parted(jnp.where(first, down, du))

    @pl.when(step == 0)
    def _():
        send_out[0] = low[:half]
        send_out[1] = low[half:]

    @pl.when(step == 1)
    def _():
        keep_out[0] = low[:half]
        keep_out[1] = low[half:]


def summed(refs):
    rows = []
    for stream in range(2):
        keep, first, final = refs[3 * stream : 3 * stream + 3]
        rows.append(keep[0].astype(F32) + first[0].astype(F32) + final[...].astype(F32))
    return jnp.concatenate(rows, axis=0)


def both(left, right):
    return jnp.concatenate([left[...].astype(F32), right[...].astype(F32)], axis=0)


def fold(value):
    return jnp.sum(value.reshape(-1, 8, value.shape[1]), axis=0)


def rows_pair_body(where, *refs):
    da2 = summed(refs[:6])
    attn_a, attn_b, xr, dyr, gain, router = refs[6:12]
    w_parts = refs[12:16]
    dyn_out, ga_out, gain_out, do_outs = refs[16], refs[17], refs[18], refs[19:]
    rows = xr[...].astype(F32)
    y = rows + both(attn_a, attn_b)
    inverse = lax.rsqrt(jnp.mean(y * y, axis=1, keepdims=True) + EPS)
    scaled = y * inverse
    joint = da2 * scaled
    gain_out[...] = fold(joint)
    vec = row(gain)
    dyn = inverse * (vec * da2 - scaled * jnp.mean(vec * joint, axis=1, keepdims=True))
    dyn_out[...] = dyn
    rate = sigmoid(jnp.sum(rows * row(router), axis=1, keepdims=True))
    ga = (rate * dyr[...].astype(F32) + dyn).astype(BF16)
    ga_out[...] = ga
    for weight, out in zip(w_parts, do_outs):
        out[...] = dot(ga, weight[...], NT).astype(BF16)


def delta_pair_body(where, *refs):
    attn_a, attn_b, xr, dyr, dyn, router = refs[4:10]
    upd_out, base_out, grad_router_out = refs[10:]
    delta = both(attn_a, attn_b)
    for piece in refs[:4]:
        delta = delta + piece[...].astype(F32)
    rows = xr[...].astype(F32)
    grads = dyr[...].astype(F32)
    vec = row(router)
    rate = sigmoid(jnp.sum(rows * vec, axis=1, keepdims=True))
    upd_out[...] = (rows + rate * delta).astype(BF16)
    dlogit = jnp.sum(grads * delta, axis=1, keepdims=True) * rate * (1.0 - rate)
    base_out[...] = grads + dyn[...] + dlogit * vec
    grad_router_out[...] = fold(dlogit * rows)


def out_grad_body(where, *refs):
    ga, keep_out, give_out = refs[8:]
    half = keep_out.shape[1]
    grads = ga[...]
    for out, core in ((keep_out, where[CORE]), (give_out, 1 - where[CORE])):
        span = pl.ds(pl.multiple_of(core * half, half), half)
        for part in range(4):
            mixed = jnp.concatenate([refs[part][:, span], refs[4 + part][:, span]], axis=0)
            out[part] = dot(mixed, grads, TN).astype(BF16)


def back_pair_body(heads, stream, where, qkv, mask, lse, *refs):
    dmixed = refs[:4]
    w_qkv = refs[4]
    dqkv_out, send_out, keep_out = refs[-3:]
    step = pl.program_id(0)
    owners = STREAMS[stream]
    routed = mask.shape[1]
    logits, dprobs, norms, items = [], [], [], []
    for at in range(2):
        span = slice(at * routed, (at + 1) * routed)
        joint = qkv[span, :]
        allowed = mask[span, :].astype(F32) > 0.5
        grads = jnp.where(step == 0, dmixed[owners[at]][...], dmixed[owners[2 + at]][...])
        for head in range(heads):
            base = head * 3 * HD
            query = joint[:, base : base + HD]
            key = joint[:, base + HD : base + 2 * HD]
            value = joint[:, base + 2 * HD : base + 3 * HD]
            dmix = grads[:, head * HD : (head + 1) * HD]
            logits.append(jnp.where(allowed, dot(query, key, NT) * SCALE, -1e30))
            dprobs.append(dot(dmix, value, NT))
            norms.append(lse[span, head : head + 1])
            items.append((span, base, query, key, dmix))
    probs = jnp.exp(jnp.concatenate(logits, axis=0) - jnp.concatenate(norms, axis=0))
    dprobs = jnp.concatenate(dprobs, axis=0)
    spread = jnp.sum(probs * dprobs, axis=1, keepdims=True)
    dlogs = (probs * (dprobs - spread)).astype(BF16)
    probs = probs.astype(BF16)
    for at, (span, base, query, key, dmix) in enumerate(items):
        part = span.start // routed
        dlog = dlogs[at * routed : (at + 1) * routed]
        prob = probs[at * routed : (at + 1) * routed]
        dqkv_out[part, :, base : base + HD] = (dot(dlog, key) * SCALE).astype(BF16)
        dqkv_out[part, :, base + HD : base + 2 * HD] = (dot(dlog, query, TN) * SCALE).astype(BF16)
        dqkv_out[part, :, base + 2 * HD : base + 3 * HD] = dot(prob, dmix, TN).astype(BF16)
    low = dot(joined(dqkv_out[...]), w_qkv[...], NT).astype(BF16)

    @pl.when(step == 0)
    def _():
        send_out[0] = low[:routed]
        send_out[1] = low[routed:]

    @pl.when(step == 1)
    def _():
        keep_out[0] = low[:routed]
        keep_out[1] = low[routed:]


def last_pair_body(where, *refs):
    da1 = summed(refs[:6])
    xr, base, gain, gain_two, router_part, score_a, score_b, out = refs[6:]
    rows = xr[...].astype(F32)
    inverse = lax.rsqrt(jnp.mean(rows * rows, axis=1, keepdims=True) + EPS)
    scaled = rows * inverse
    joint = da1 * scaled
    vec = row(gain)
    dxn = inverse * (vec * da1 - scaled * jnp.mean(vec * joint, axis=1, keepdims=True))
    count, width = rows.shape
    out[:count, :] = (base[...] + dxn).astype(BF16)
    scores = score_a[...] + score_b[...]
    scores = jnp.concatenate(
        [scores[0:1], scores[1:2] / 4, jnp.zeros((1, width - 256), F32)], axis=1
    )
    at = iota((16, width), 0)
    small = jnp.zeros((16, width), F32)
    lines = [fold(joint), gain_two[...], router_part[...]]
    lines = [jnp.sum(line, axis=0, keepdims=True) for line in lines] + [scores]
    for index, line in enumerate(lines):
        small = jnp.where(at % 8 == index, line, small)
    high = small.astype(BF16).astype(F32)
    out[count:, :] = jnp.where(at < 8, high, small - high).astype(BF16)


def place_body(starts, where, source, routes, *refs):
    rows, out = refs[: len(starts)], refs[-1]
    step = pl.program_id(0)
    length = source.shape[0]
    line = routes[pl.ds(where[PUT + put_entry(starts, step)], 1), :]
    hot = iota((length, line.shape[1]), 0) == line
    picked = jnp.where(hot, 1.0, 0.0)
    taken = jnp.sum(picked, axis=1, keepdims=True) > 0.5
    fresh = rows[0][...]
    for at, start in enumerate(starts):
        if at:
            fresh = jnp.where(step >= start[0], rows[at][...], fresh)
    moved = dot(picked.astype(BF16), fresh)
    out[...] = jnp.where(taken, moved, source[...].astype(F32)).astype(BF16)


def put_entry(starts, step):
    entry = starts[0][1] + step
    for first, place in starts[1:]:
        entry = jnp.where(step >= first, place + step - first, entry)
    return entry


def place_rows(table, source, routes, parts, target, name):
    seqs, routed = routes.shape
    length = source.shape[0] // seqs
    width = source.shape[1]
    starts, step = [], 0
    block = lambda i, w: (w[PUT + put_entry(starts, i)], 0)
    in_specs = [pl.BlockSpec((length, width), block), whole(routes.shape)]
    args = [table, source, routes]
    for rows, place in parts:
        per = rows.shape[0] // routed
        starts.append((step, place))
        in_specs.append(
            pl.BlockSpec(
                (routed, width),
                lambda i, w, first=step, top=per - 1: (jnp.clip(i - first, 0, top), 0),
            )
        )
        args.append(rows)
        step += per
    alias = None
    if target is not None:
        in_specs.append(pl.BlockSpec(memory_space=pl.ANY))
        alias = {len(args): 0}
        args.append(target)
    return call(
        functools.partial(place_body, tuple(starts)),
        (step,),
        in_specs,
        pl.BlockSpec((length, width), block),
        jax.ShapeDtypeStruct(source.shape, BF16),
        1,
        1,
        name,
        alias=alias,
    )(*args)


def halves_body(where, value, side, pair, corner, down_out, up_out):
    step = pl.program_id(0)
    for late, (own, other) in enumerate(((value, pair), (side, corner))):
        for core, outs in enumerate(((down_out, up_out), (up_out, down_out))):

            @pl.when((step // 2 == late) & (where[CORE] == core))
            def _(own=own, other=other, outs=outs):
                outs[0][...] = own[...].astype(F32)
                outs[1][...] = other[...].astype(F32)


def join_halves(table, pieces):
    rows, columns = pieces[0].shape
    block = (rows // 2, columns)
    early = pl.BlockSpec(block, lambda i, w: (jnp.minimum(i, 1), 0))
    late = pl.BlockSpec(block, lambda i, w: (jnp.maximum(i - 2, 0), 0))
    placed = pl.BlockSpec(block, lambda i, w: (2 * (w[BIT] ^ (i // 2)) + i % 2, 0))
    value, pair, side, corner = pieces
    return call(
        halves_body,
        (4,),
        [early, late, early, late],
        [placed, placed],
        [jax.ShapeDtypeStruct((2 * rows, columns), F32)] * 2,
        1,
        1,
        "join",
    )(table, value, side, pair, corner)


def tail_body(where, *refs):
    qkv_out, out_out = refs[-2:]
    for at in range(4):

        @pl.when(pl.program_id(0) == at)
        def _(at=at):
            qkv_out[...] = refs[at][...].astype(F32)
            if at < 2:
                out_out[...] = refs[4 + at][...].astype(F32)


def join_tail(table, pieces, outs):
    rows, columns = pieces[0].shape
    few, wide = outs[0].shape
    return call(
        tail_body,
        (4,),
        [whole((rows, columns))] * 4 + [whole((few, wide))] * 2,
        [
            pl.BlockSpec((rows, columns), lambda i, w: (w[QUARTER + i], 0)),
            pl.BlockSpec((few, wide), lambda i, w: (w[14 + jnp.minimum(i, 1)], 0)),
        ],
        [
            jax.ShapeDtypeStruct((4 * rows, columns), F32),
            jax.ShapeDtypeStruct((2 * few, wide), F32),
        ],
        1,
        1,
        "join",
    )(table, *pieces, *outs)


def after(value, *others):
    return lax.optimization_barrier((value, *others))[0]


def add(left, right):
    return (left.astype(F32) + right.astype(F32)).astype(BF16)


class Total:
    def __init__(self, give, keep, bit):
        self.keep, self.bit = keep, bit
        self.sent = swap(give, "dp", 1)

    def split(self, *others):
        got = after(self.sent, *others)
        rows = got.shape[0] // 2
        cut = lambda index: add(block_of(self.keep, index, rows), block_of(got, index, rows))
        far = cut(1 - self.bit)
        self.value = cut(self.bit)
        self.sent = swap(far, "dp", 2)
        return far

    def cross(self, *others):
        self.value = add(self.value, after(self.sent, *others))
        self.sent = swap(self.value, "dp", 4)
        return self.value

    def close(self, *others):
        self.value = add(self.value, after(self.sent, *others))
        self.sent = swap(self.value, "dp", 2)
        self.pair = swap(self.value, "dp", 1)
        return self.value

    def back(self, *others):
        self.side = after(self.sent, *others)
        self.corner = swap(self.side, "dp", 1)
        return self.side

    def pieces(self):
        return [self.value, self.pair, self.side, self.corner]


OWNERS = (1, 3, 0, 2, 2, 3, 0, 1)
HALVES = (0, 0, 0, 0, 1, 1, 1, 1)
RANK, CORE, QUARTER, PUT, BIT = 8, 9, 10, 16, 24


def make_table(rank, core, bit):
    owners = jnp.array(OWNERS + (0,) * 8 + (0, 0, 1, 1, 2, 2, 3, 3, 0), jnp.int32)
    halves = jnp.array(HALVES + (0,) * 8 + (0, 1) * 4 + (0,), jnp.int32)
    at = jnp.arange(25, dtype=jnp.int32)
    table = 2 * (rank ^ owners) + halves
    quarter = at - QUARTER
    quarters = 2 * (core ^ (quarter % 2)) + (bit ^ (quarter // 2))
    table = jnp.where((at >= QUARTER) & (at < QUARTER + 4), quarters, table)
    table = jnp.where(at == 14, core, jnp.where(at == 15, 1 - core, table))
    table = jnp.where(at == BIT, bit, table)
    return jnp.where(at == RANK, rank, jnp.where(at == CORE, core, table)).astype(jnp.int32)


def paired(
    tokens, segments, routes, cotangent, gain_attn, gain_mlp, w_router, w_qkv, w_out, w_up, w_down
):
    seqs, length = segments.shape
    routed = routes.shape[1]
    width = tokens.shape[1]
    wide = w_out.shape[0]
    heads = wide // HD
    joint = w_qkv.shape[1]
    hidden = w_up.shape[1]
    rank = lax.axis_index("mp")
    core = lax.axis_index("dp") % 2
    bit = lax.axis_index("dp") // 2 % 2
    half_rows = 4 * routed
    pair = 2 * routed
    total_rows = 8 * routed
    sds = jax.ShapeDtypeStruct
    flat = lambda i, w: (i, 0)
    line = whole((width,))
    table = make_table(rank, core, bit)
    anywhere = pl.BlockSpec(memory_space=pl.ANY)
    partners = (1, 2, 3)

    def held(columns, dtype=BF16):
        return sds((2, 2, 2, routed, columns), dtype)

    def rowed(value):
        return value.reshape(total_rows, value.shape[-1])

    def by_owner(value):
        return value.reshape(2, 2, 2, routed, value.shape[-1])

    w_parts = [w_out] + [swap(w_out, "mp", j) for j in partners]

    fronts = []
    for stream in range(2):
        carried = fronts[0][:3] if fronts else []
        fronts.append(
            call(
                functools.partial(front_pair_body, heads, length // 4, 4 * stream),
                (2,),
                [
                    pl.BlockSpec((length, width), lambda i, w, s=4 * stream: (w[2 * i + s], 0)),
                    pl.BlockSpec((length, width), lambda i, w, s=4 * stream: (w[2 * i + 1 + s], 0)),
                    whole(routes.shape),
                    whole(segments.shape),
                    line,
                    line,
                    whole(w_qkv.shape),
                ]
                + [anywhere] * len(carried),
                [
                    owner_spec(stream, routed, width),
                    owner_spec(stream, routed, width // 2),
                    owner_spec(stream, routed, width // 2),
                    pl.BlockSpec((pair, joint), flat),
                    pl.BlockSpec((pair, routed), flat),
                    pl.BlockSpec((pair, 128), flat),
                    pl.BlockSpec((pair, wide), flat),
                    whole((8, 128)),
                ],
                [
                    held(width),
                    held(width // 2),
                    held(width // 2),
                    sds((half_rows, joint), BF16),
                    sds((half_rows, routed), BF16),
                    sds((half_rows, 128), F32),
                    sds((half_rows, wide), BF16),
                    sds((8, 128), F32),
                ],
                1,
                1,
                "front",
                alias={8 + at: at for at in range(len(carried))},
            )(
                after(table, fronts[0][6]) if fronts else table,
                tokens, tokens, routes, segments, gain_attn, w_router, w_qkv, *carried,
            )
        )
    xr, a1_give, a1_keep = fronts[1][:3]
    qkv, mask, lse, heads_out, score = [list(kind) for kind in zip(*[f[3:] for f in fronts])]
    xr_rows = rowed(xr)

    dyr, gm, dh = call(
        cot_pair_body,
        (4,),
        [
            pl.BlockSpec((length, width), lambda i, w: (w[PUT + 2 * i], 0)),
            pl.BlockSpec((length, width), lambda i, w: (w[PUT + 2 * i + 1], 0)),
            whole(routes.shape),
            pl.BlockSpec((pair, width), flat),
            line,
            whole(w_down.shape),
        ],
        [
            pl.BlockSpec((pair, width), flat),
            pl.BlockSpec((pair, width), flat),
            pl.BlockSpec((pair, hidden), flat),
        ],
        [
            sds((total_rows, width), BF16),
            sds((total_rows, width), BF16),
            sds((total_rows, hidden), F32),
        ],
        1,
        1,
        "cot",
    )(table, cotangent, cotangent, routes, xr_rows, w_router, w_down)

    mixed = []
    for stream in range(2):
        near, far = FIRST[stream], FIRST[1 - stream]
        beside = swap(heads_out[stream], "mp", near)
        across = swap(heads_out[stream], "mp", far)
        came = after(beside, heads_out[1] if stream == 0 else gm)
        corner = swap(came, "mp", far)
        parts = [heads_out[stream], None, None, corner]
        parts[near], parts[far] = came, across
        mixed.append(parts)
    w_parts = [w_out] + [after(weight, heads_out[1]) for weight in w_parts[1:]]

    middles = []
    for stream in range(2):
        near = FIRST[stream]
        specs = []
        for part in range(4):
            crossed = part in (near, 3)
            specs.append(
                pl.BlockSpec((pair, wide), (lambda i, w: (1 - i, 0)) if crossed else flat)
            )
        carried = middles[0][1:6] if middles else []
        middles.append(
            call(
                functools.partial(middle_pair_body, stream),
                (2,),
                specs
                + [whole(w_out.shape)] * 4
                + [
                    owner_spec(stream, routed, width),
                    owner_spec(stream, routed, hidden),
                    owner_spec(stream, routed, width),
                    line,
                    whole(w_up.shape),
                ]
                + [anywhere] * len(carried),
                [whole((routed, width))]
                + [owner_spec(stream, routed, width)] * 5
                + [whole((2, routed, width))] * 2,
                [sds((routed, width), F32)]
                + [held(width)] * 5
                + [sds((2, routed, width), BF16)] * 2,
                1,
                1,
                "middle",
                alias={14 + at: 1 + at for at in range(len(carried))},
            )(
                after(table, middles[0][7]) if middles else table,
                *mixed[stream], *w_parts, xr, by_owner(dh), by_owner(gm), gain_mlp, w_up, *carried,
            )
        )
    attn = [middles[0][0], middles[1][0]]
    left_give, left_keep, right_give, right_keep, hid = [rowed(v) for v in middles[1][1:6]]
    send, keep = [[m[at] for m in middles] for at in (6, 7)]

    first_a = after(swap(send[0], "mp", FIRST[0]), keep[1])
    ahead_a = add(keep[0][1], first_a[1])
    final_a = swap(ahead_a, "mp", FIRST[1])

    ffn_give = dot(after(left_give, ahead_a), right_give, TN).astype(BF16)
    ffn_keep = dot(after(left_keep, ffn_give), right_keep, TN).astype(BF16)
    ffn = Total(ffn_give, ffn_keep, bit)
    mlp = [None] * 4

    def mlp_of(j, *others):
        mlp[j] = dot(after(hid[j * pair : (j + 1) * pair], *others), w_down).astype(BF16)
        return mlp[j]

    mlp_of(1, ffn_keep)
    ffn_far = ffn.split(mlp[1])

    first_b = after(swap(send[1], "mp", FIRST[1]), ffn_far)
    ahead_b = add(keep[1][1], first_b[1])
    final_b = swap(ahead_b, "mp", FIRST[0])
    mlp_of(2, ahead_b)
    mlp_all = [None, swap(after(mlp[1], ahead_b), "mp", 1), swap(mlp[2], "mp", 2), None]
    mlp_of(3, mlp[2])
    mlp_of(0, mlp[3])
    mlp_all[0] = mlp[0]

    own = pl.BlockSpec((pair, width), lambda i, w: (0, 0))
    pieces = [
        pl.BlockSpec((1, routed, width), lambda i, w: (0, 0, 0)),
        pl.BlockSpec((1, routed, width), lambda i, w: (0, 0, 0)),
        whole((routed, width)),
    ] * 2
    rows_out = call(
        rows_pair_body,
        (1,),
        pieces + [whole((routed, width))] * 2 + [own, own, line, line] + [whole(w_out.shape)] * 4,
        [whole((pair, width)), whole((pair, width)), whole((8, width))]
        + [whole((pair, wide))] * 4,
        [sds((pair, width), F32), sds((pair, width), BF16), sds((8, width), F32)]
        + [sds((pair, wide), BF16)] * 4,
        1,
        1,
        "rows",
    )(
        after(table, mlp[0]), keep[0], first_a, final_a, keep[1], first_b,
        final_b, *attn, xr_rows, dyr, gain_mlp, w_router, *w_parts,
    )
    dyn, ga, gain_two_part = rows_out[:3]
    dmix = [rows_out[3]] + [swap(rows_out[3 + j], "mp", j) for j in partners]

    out_specs = [
        pl.BlockSpec((routed, wide), lambda i, w, at=STREAMS[s].index(j): (at, 0))
        for s in (0, 1)
        for j in range(4)
    ]
    outs_keep, outs_give = call(
        out_grad_body,
        (1,),
        out_specs + [whole((pair, width))],
        [whole((4, wide // 2, width))] * 2,
        [sds((4, wide // 2, width), BF16)] * 2,
        1,
        1,
        "outs",
    )(after(table, ga), *mixed[0], *mixed[1], ga)
    outs_got = swap(outs_give, "dp", 1)
    dmix = [dmix[0]] + [after(value, outs_keep) for value in dmix[1:]]
    mlp_all[3] = swap(after(mlp[3], *dmix[1:]), "mp", 3)
    ffn_now = ffn.cross(*dmix[1:])

    backs = []
    for stream in range(2):
        cut = pl.BlockSpec((routed, wide), lambda i, w, s=stream: (s, 0))
        carried = backs[0][:1] if backs else []
        backs.append(
            call(
                functools.partial(back_pair_body, heads, stream),
                (2,),
                [
                    pl.BlockSpec((pair, joint), flat),
                    pl.BlockSpec((pair, routed), flat),
                    pl.BlockSpec((pair, 128), flat),
                    cut,
                    cut,
                    cut,
                    cut,
                    whole(w_qkv.shape),
                ]
                + [anywhere] * len(carried),
                [
                    owner_spec(stream, routed, joint),
                    whole((2, routed, width)),
                    whole((2, routed, width)),
                ],
                [
                    held(joint),
                    sds((2, routed, width), BF16),
                    sds((2, routed, width), BF16),
                ],
                1,
                1,
                "back",
                alias={9: 0} if carried else None,
            )(
                after(table, backs[0][2]) if backs else after(table, ffn_now),
                qkv[stream], mask[stream], lse[stream], *dmix, w_qkv, *carried,
            )
        )
    dqkv = rowed(backs[1][0])
    back_send, back_keep = [[b[at] for b in backs] for at in (1, 2)]
    mlp_all[1:] = [after(value, back_keep[1]) for value in mlp_all[1:]]

    upd, base, router_part = call(
        delta_pair_body,
        (1,),
        [whole((pair, width))] * 4
        + [whole((routed, width))] * 2
        + [own, own, whole((pair, width)), line],
        [whole((pair, width)), whole((pair, width)), whole((8, width))],
        [sds((pair, width), BF16), sds((pair, width), F32), sds((8, width), F32)],
        1,
        1,
        "delta",
    )(after(table, back_keep[1]), *mlp_all, *attn, xr_rows, dyr, dyn, w_router)

    last_first_a = after(swap(back_send[0], "mp", FIRST[0]), base)
    last_ahead_a = add(back_keep[0][1], last_first_a[1])
    last_final_a = swap(last_ahead_a, "mp", FIRST[1])

    qkv_give = dot(rowed(after(a1_give, last_ahead_a)), dqkv, TN).astype(BF16)
    qkv_keep = dot(rowed(after(a1_keep, qkv_give)), dqkv, TN).astype(BF16)
    whole_qkv = Total(qkv_give, qkv_keep, bit)

    last_first_b = after(swap(back_send[1], "mp", FIRST[1]), qkv_keep)
    last_ahead_b = add(back_keep[1][1], last_first_b[1])
    last_final_b = swap(last_ahead_b, "mp", FIRST[0])
    outs_got = after(outs_got, last_ahead_b)
    outs_half = [add(outs_keep[j], outs_got[j]) for j in range(4)]
    qkv_far = whole_qkv.split(*outs_half)

    def put(source, parts, target, name, *others):
        return place_rows(after(table, *others), source, routes, parts, target, name)

    output = put(tokens, [(upd, 0)], None, "put_out", qkv_far)
    upd_all = [swap(after(upd, qkv_far), "mp", j) for j in partners]
    last = call(
        last_pair_body,
        (1,),
        pieces
        + [own, whole((pair, width)), line]
        + [whole((8, width))] * 2
        + [whole((8, 128))] * 2,
        [whole((pair + 16, width))],
        [sds((pair + 16, width), BF16)],
        1,
        1,
        "last",
    )(
        after(table, output), back_keep[0], last_first_a, last_final_a, back_keep[1],
        last_first_b, last_final_b, xr_rows, base, gain_attn, gain_two_part, router_part, *score,
    )[0]
    ffn_now = ffn.close(last)
    grads = put(cotangent, [(last, 0)], None, "put_grad", ffn_now)
    last_all = [swap(last, "mp", j) for j in partners]
    qkv_now = whole_qkv.cross(grads)
    upd_all = [after(value, grads) for value in upd_all]
    output = put(
        tokens,
        [(rows, 2 * j) for j, rows in zip(partners, upd_all)],
        output,
        "put_out",
        qkv_now,
    )
    out_sent = [swap(after(outs_half[j], grads), "mp", j) for j in partners]
    side = ffn.back(output)
    last_all = [last] + [after(value, output) for value in last_all]
    small = 0.0
    for rows in last_all:
        small = small + rows[pair : pair + 8].astype(F32) + rows[pair + 8 :].astype(F32)
    qkv_now = whole_qkv.close(output)
    out_half = outs_half[0].astype(F32)
    for got in out_sent:
        out_half = out_half + after(got, output).astype(F32)
    out_half = out_half.astype(BF16)
    grads = put(
        cotangent,
        [(rows, 2 * j) for j, rows in zip(partners, last_all[1:])],
        grads,
        "put_grad",
        side, qkv_now, small, out_half,
    )
    out_half = add(out_half, after(swap(out_half, "dp", 2), grads))
    small = small + after(swap(small, "dp", 2), grads)
    side = whole_qkv.back(grads)
    grad_down, grad_up = join_halves(after(table, out_half, small, side), ffn.pieces())
    out_half = add(out_half, after(swap(out_half, "dp", 4), grad_up))
    small = small + after(swap(small, "dp", 4), grad_up)
    small = small + swap(small, "dp", 1)
    grad_qkv, grad_out = join_tail(
        after(table, grad_up), whole_qkv.pieces(), [out_half, swap(out_half, "dp", 1)]
    )

    score_total = small[3, 0]
    routed_total = small[3, 128]
    token_count = seqs * length * lax.axis_size("dp")
    return (
        output,
        grads,
        small[0],
        small[1],
        small[2],
        grad_qkv,
        grad_out,
        grad_up,
        grad_down,
        routed_total / score_total,
        score_total / token_count,
    )


def shards(*arrays):
    tokens, segments, routes, w_out, w_up = (arrays[at] for at in (0, 1, 2, 8, 9))
    square = lax.axis_size("mp") == 4 and segments.shape[0] == 8 and lax.axis_size("dp") == 8
    square = square and w_up.shape[1] == tokens.shape[1] and tokens.shape[1] % 256 == 0
    if square and routes.shape[1] % 128 == 0 and w_out.shape[0] % 128 == 0:
        return paired(*arrays)
    return general(*arrays)


def solution(mesh):
    rows = P("dp", None)
    columns = P(None, "mp")
    lines = P("mp", None)
    in_specs = (rows, rows, rows, rows, P(), P(), P(), columns, lines, columns, lines)
    out_specs = (rows, rows, P(), P(), P(), columns, lines, columns, lines, P(), P())
    return jax.shard_map(shards, mesh=mesh, in_specs=in_specs, out_specs=out_specs, check_vma=False)
```

```python
import functools

import jax
import jax.numpy as jnp
from jax import lax
from jax.experimental import pallas as pl
from jax.experimental.pallas import tpu as pltpu
from jax.sharding import PartitionSpec as P

HD = 64
EPS = 1e-06
SCALE = HD ** (-0.5)
GELU_C = (2.0 / 3.141592653589793) ** 0.5
GELU_A = 0.044715
F32 = jnp.float32
BF16 = jnp.bfloat16


def dot(left, right, on=((1,), (0,))):
    return lax.dot_general(left, right, (on, ((), ())), preferred_element_type=F32)


NT = ((1,), (1,))
TN = ((0,), (0,))


def iota(shape, axis):
    return lax.broadcasted_iota(jnp.int32, shape, axis)


def sigmoid(value):
    return 1.0 / (1.0 + jnp.exp(-value))


LENGTHS = {
    "front": 5.2, "cot": 3.2, "middle": 5.5, "rows": 5.7, "outs": 3.9, "back": 1.0,
    "delta": 0.01, "mlp": 0.01, "last": 1.0, "put_own": 0.01, "put_out": 2.4, "put_grad": 2.4, "join": 1.5,
}
RATE = 1.5e9


def call(body, grid, in_specs, out_specs, out_shape, flops, nbytes, name, scratch=(), alias=None):
    if flops == 1:
        flops = LENGTHS[name] * grid[0] * RATE
        nbytes = 1
    return pl.pallas_call(
        body,
        grid_spec=pltpu.PrefetchScalarGridSpec(
            num_scalar_prefetch=1,
            grid=grid,
            in_specs=in_specs,
            out_specs=out_specs,
            scratch_shapes=list(scratch),
        ),
        out_shape=out_shape,
        cost_estimate=pl.CostEstimate(
            flops=int(flops), bytes_accessed=int(nbytes), transcendentals=0
        ),
        input_output_aliases=alias or {},
        name=name,
    )


def whole(shape):
    zeros = (0,) * len(shape)
    return pl.BlockSpec(shape, lambda *_: zeros)


def one_hot_rows(routes_row, length):
    routed = routes_row.shape[1]
    eye = iota((routed, routed), 0) == iota((routed, routed), 1)
    column = jnp.sum(jnp.where(eye, routes_row.astype(F32), 0.0), axis=1, keepdims=True)
    return iota((routed, length), 1) == column.astype(jnp.int32), eye


def head_mask(hot, eye, seg_line):
    seg_col = jnp.sum(jnp.where(hot, seg_line, 0.0), axis=1, keepdims=True)
    seg_row = jnp.sum(jnp.where(eye, seg_col, 0.0), axis=0, keepdims=True)
    routed = eye.shape[0]
    causal = iota((routed, routed), 0) >= iota((routed, routed), 1)
    return causal & (seg_col == seg_row)


def softmax_head(query, key, allowed):
    logits = jnp.where(allowed, dot(query, key, NT) * SCALE, -1e30)
    expon = jnp.exp(logits - jnp.max(logits, axis=1, keepdims=True))
    return expon / jnp.sum(expon, axis=1, keepdims=True)


def front_body(
    heads, slice_rows, where, tokens, routes, segments, gain, router, w_qkv,
    xr_out, a1_out, qkv_out, mask_out, mixed_out, score_out,
):
    step = pl.program_id(0)
    length = tokens.shape[0]
    hot, eye = one_hot_rows(routes[pl.ds(step, 1), :], length)
    seg_line = segments[pl.ds(step, 1), :].astype(F32)
    allowed = head_mask(hot, eye, seg_line)
    mask_out[...] = jnp.where(allowed, 1.0, 0.0).astype(BF16)
    rows = dot(jnp.where(hot, 1.0, 0.0).astype(BF16), tokens[...])
    xr_out[...] = rows.astype(BF16)
    vec = router[...].astype(F32)
    start = pl.multiple_of(where[0] * slice_rows, slice_rows)
    part = tokens[pl.ds(start, slice_rows), :].astype(F32)
    total = jnp.sum(sigmoid(jnp.sum(part * vec, axis=1, keepdims=True)), axis=0, keepdims=True)
    chosen = jnp.sum(sigmoid(jnp.sum(rows * vec, axis=1, keepdims=True)), axis=0, keepdims=True)

    @pl.when(step == 0)
    def _():
        score_out[...] = jnp.zeros_like(score_out)

    which = iota(score_out.shape, 0)
    score_out[...] += jnp.where(which == 0, total, jnp.where(which == 1, chosen, 0.0))
    inverse = lax.rsqrt(jnp.mean(rows * rows, axis=1, keepdims=True) + EPS)
    normed = (rows * inverse * gain[...].astype(F32)).astype(BF16)
    a1_out[...] = normed
    joint = dot(normed, w_qkv[...]).astype(BF16)
    qkv_out[...] = joint
    for head in range(heads):
        base = head * 3 * HD
        query = joint[:, base : base + HD]
        key = joint[:, base + HD : base + 2 * HD]
        value = joint[:, base + 2 * HD : base + 3 * HD]
        probs = softmax_head(query, key, allowed).astype(BF16)
        mixed_out[:, head * HD : (head + 1) * HD] = dot(probs, value).astype(BF16)


def cot_body(where, cotangent, routes, xr, router, w_down, dyr_out, gm_out, dh_out):
    step = pl.program_id(0)
    hot, _ = one_hot_rows(routes[pl.ds(step, 1), :], cotangent.shape[0])
    rows = dot(jnp.where(hot, 1.0, 0.0).astype(BF16), cotangent[...])
    dyr_out[...] = rows.astype(BF16)
    vec = router[...].astype(F32)
    rate = sigmoid(jnp.sum(xr[...].astype(F32) * vec, axis=1, keepdims=True))
    low = (rate * rows).astype(BF16)
    gm_out[...] = low
    dh_out[...] = dot(low, w_down[...], NT)


def middle_body(parts, table, *refs):
    mixed = refs[:parts]
    w_out, xr, dh, gain, w_up = refs[parts : parts + 5]
    attn_out, a2_out, hid_out, du_out, da2_out, gain_out = refs[parts + 5 :]
    attn = dot(mixed[0][...], w_out[0])
    for part in range(1, parts):
        attn = attn + dot(mixed[part][...], w_out[part])
    attn_out[...] = attn
    y = xr[...].astype(F32) + attn
    scaled = y * lax.rsqrt(jnp.mean(y * y, axis=1, keepdims=True) + EPS)
    a2 = (scaled * gain[...].astype(F32)).astype(BF16)
    a2_out[...] = a2
    u = dot(a2, w_up[...])
    square = u * u
    t = jnp.tanh(GELU_C * (u + GELU_A * (u * square)))
    hid_out[...] = (0.5 * u * (1.0 + t)).astype(BF16)
    slope = 0.5 * (1.0 + t) + (0.5 * GELU_C) * u * (1.0 - t * t) * (1.0 + 3.0 * GELU_A * square)
    du = (dh[...] * slope).astype(BF16)
    du_out[...] = du
    da2 = dot(du, w_up[...], NT)
    da2_out[0] = da2.astype(BF16)

    @pl.when(pl.program_id(0) == 0)
    def _():
        gain_out[...] = jnp.zeros_like(gain_out)

    gain_out[...] += jnp.sum((da2 * scaled).reshape(-1, 8, da2.shape[1]), axis=0)


def rows_body(parts, where, *refs):
    pieces = refs[:parts]
    attn, xr, dyr, gain, router, w_out = refs[parts : parts + 6]
    dyn_out, ga_out, do_out = refs[parts + 6 :]
    da2 = pieces[0][...].astype(F32)
    for piece in pieces[1:]:
        da2 = da2 + piece[...].astype(F32)
    rows = xr[...].astype(F32)
    y = rows + attn[...]
    inverse = lax.rsqrt(jnp.mean(y * y, axis=1, keepdims=True) + EPS)
    t = gain[...].astype(F32) * da2
    scaled = y * inverse
    dyn = inverse * (t - scaled * jnp.mean(t * scaled, axis=1, keepdims=True))
    dyn_out[...] = dyn
    rate = sigmoid(jnp.sum(rows * router[...].astype(F32), axis=1, keepdims=True))
    ga = (rate * dyr[...].astype(F32) + dyn).astype(BF16)
    ga_out[...] = ga
    for part in range(parts):
        do_out[part] = dot(ga, w_out[part], NT).astype(BF16)


def delta_body(parts, where, *refs):
    pieces = refs[:parts]
    attn, xr, dyr, dyn, router = refs[parts : parts + 5]
    upd_out, base_out, grad_router_out = refs[parts + 5 :]
    delta = attn[...]
    for piece in pieces:
        delta = delta + piece[...].astype(F32)
    rows = xr[...].astype(F32)
    grads = dyr[...].astype(F32)
    vec = router[...].astype(F32)
    rate = sigmoid(jnp.sum(rows * vec, axis=1, keepdims=True))
    upd_out[...] = (rows + rate * delta).astype(BF16)
    dlogit = jnp.sum(grads * delta, axis=1, keepdims=True) * rate * (1.0 - rate)
    base_out[...] = grads + dyn[...] + dlogit * vec

    @pl.when(pl.program_id(0) == 0)
    def _():
        grad_router_out[...] = jnp.zeros_like(grad_router_out)

    grad_router_out[...] += jnp.sum((dlogit * rows).reshape(-1, 8, rows.shape[1]), axis=0)


def back_body(heads, where, qkv, mask, dmixed, xr, gain, w_qkv, dqkv_out, da1_out, gain_out):
    joint = qkv[...]
    allowed = mask[...].astype(F32) > 0.5
    grads = dmixed[0]
    pieces = []
    for head in range(heads):
        base = head * 3 * HD
        query = joint[:, base : base + HD]
        key = joint[:, base + HD : base + 2 * HD]
        value = joint[:, base + 2 * HD : base + 3 * HD]
        dmix = grads[:, head * HD : (head + 1) * HD]
        probs = softmax_head(query, key, allowed)
        dprobs = dot(dmix, value, NT)
        spread = jnp.sum(probs * dprobs, axis=1, keepdims=True)
        dlog = (probs * (dprobs - spread)).astype(BF16)
        dquery = dot(dlog, key) * SCALE
        dkey = dot(dlog, query, TN) * SCALE
        dvalue = dot(probs.astype(BF16), dmix, TN)
        pieces += [dquery.astype(BF16), dkey.astype(BF16), dvalue.astype(BF16)]
    for at, piece in enumerate(pieces):
        dqkv_out[:, at * HD : (at + 1) * HD] = piece
    da1 = dot(dqkv_out[...], w_qkv[...], NT)
    da1_out[0] = da1.astype(BF16)
    rows = xr[...].astype(F32)
    scaled = rows * lax.rsqrt(jnp.mean(rows * rows, axis=1, keepdims=True) + EPS)

    @pl.when(pl.program_id(0) == 0)
    def _():
        gain_out[...] = jnp.zeros_like(gain_out)

    gain_out[...] += jnp.sum((da1 * scaled).reshape(-1, 8, da1.shape[1]), axis=0)


def last_body(parts, where, *refs):
    pieces = refs[:parts]
    xr, base, gain = refs[parts : parts + 3]
    (out,) = refs[parts + 3 :]
    da1 = pieces[0][...].astype(F32)
    for piece in pieces[1:]:
        da1 = da1 + piece[...].astype(F32)
    rows = xr[...].astype(F32)
    inverse = lax.rsqrt(jnp.mean(rows * rows, axis=1, keepdims=True) + EPS)
    t = gain[...].astype(F32) * da1
    scaled = rows * inverse
    dxn = inverse * (t - scaled * jnp.mean(t * scaled, axis=1, keepdims=True))
    out[...] = (base[...] + dxn).astype(BF16)


def put_body(where, source, routes, rows, *refs):
    out = refs[-1]
    length = source.shape[0]
    at = where[pl.program_id(0)]
    line = routes[pl.ds(at, 1), :]
    hot = iota((length, line.shape[1]), 0) == line
    picked = jnp.where(hot, 1.0, 0.0)
    taken = jnp.sum(picked, axis=1, keepdims=True) > 0.5
    moved = dot(picked.astype(BF16), rows[...])
    out[...] = jnp.where(taken, moved, source[...].astype(F32)).astype(BF16)


def put_rows(source, routes, rows, order, target, name):
    seqs, routed = routes.shape
    length = source.shape[0] // seqs
    width = source.shape[1]
    count = rows.shape[0] // routed
    in_specs = [
        pl.BlockSpec((length, width), lambda i, w: (w[i], 0)),
        whole(routes.shape),
        pl.BlockSpec((routed, width), lambda i, w: (i, 0)),
    ]
    args = [order, source, routes, rows]
    alias = None
    if target is not None:
        in_specs.append(pl.BlockSpec(memory_space=pl.ANY))
        args.append(target)
        alias = {4: 0}
    return call(
        put_body,
        (count,),
        in_specs,
        pl.BlockSpec((length, width), lambda i, w: (w[i], 0)),
        jax.ShapeDtypeStruct(source.shape, BF16),
        2 * count * length * routed * width,
        count * length * width * 4,
        name,
        alias=alias,
    )(*args)


def swap(value, axis, offset):
    size = lax.axis_size(axis)
    return lax.ppermute(value, axis, [(i, i ^ offset) for i in range(size)])


def block_of(value, index, rows):
    return lax.dynamic_slice_in_dim(value, index * rows, rows, 0)


def in_core_order(core, mine, other):
    return jnp.where(
        core == 0,
        jnp.concatenate([mine, other], axis=0),
        jnp.concatenate([other, mine], axis=0),
    )


def line_sum(value, depth):
    at = lax.axis_index("dp") // 2
    half = depth // 2

    def shift(array, pairs):
        return lax.ppermute(
            array, "dp", [(2 * a + c, 2 * b + c) for a, b in pairs for c in range(2)]
        )

    def mirrored(a, b):
        return [(a, b), (depth - 1 - a, depth - 1 - b)]

    for step in range(half - 1):
        got = shift(value, mirrored(step, step + 1))
        value = (value.astype(F32) + got.astype(F32)).astype(BF16)
    if depth > 1:
        got = shift(value, mirrored(half - 1, half))
        value = (value.astype(F32) + got.astype(F32)).astype(BF16)
    for step in reversed(range(half - 1)):
        got = shift(value, mirrored(step + 1, step))
        here = (at == step) | (at == depth - 1 - step)
        value = jnp.where(here, got, value)
    return value


def core_half(value, core):
    half = value.shape[0] // 2
    keep = block_of(value, core, half)
    give = block_of(value, 1 - core, half)
    got = swap(give.astype(BF16), "dp", 1)
    return (keep.astype(F32) + got.astype(F32)).astype(BF16)


def core_join(value, core):
    return in_core_order(core, value, swap(value, "dp", 1)).astype(F32)


def general(
    tokens, segments, routes, cotangent, gain_attn, gain_mlp, w_router, w_qkv, w_out, w_up, w_down
):
    seqs, length = segments.shape
    routed = routes.shape[1]
    width = tokens.shape[1]
    total = seqs * routed
    wide = w_out.shape[0]
    heads = wide // HD
    joint = w_qkv.shape[1]
    hidden = w_up.shape[1]
    parts = lax.axis_size("mp")
    depth = lax.axis_size("dp") // 2
    own = total // parts
    rank = lax.axis_index("mp")
    core = lax.axis_index("dp") % 2
    aligned = own % routed == 0
    per = own // routed if aligned else 1
    where = rank.reshape(1).astype(jnp.int32)
    gain_one = gain_attn.reshape(1, width)
    gain_two = gain_mlp.reshape(1, width)
    router = w_router.reshape(1, width)
    partners = list(range(1, parts))
    sds = jax.ShapeDtypeStruct

    share = block_of(w_out, core, wide // 2)
    mine = jnp.stack([swap(share, "mp", j) for j in partners])
    other = swap(mine, "dp", 1)
    w_all = jnp.where(
        core == 0,
        jnp.concatenate([mine, other], axis=1),
        jnp.concatenate([other, mine], axis=1),
    )
    w_all = jnp.concatenate([w_out[None], w_all], axis=0)

    xr, a1, qkv, mask, mixed, score = call(
        functools.partial(front_body, heads, length // parts),
        (seqs,),
        [
            pl.BlockSpec((length, width), lambda i, w: (i, 0)),
            whole(routes.shape),
            whole(segments.shape),
            whole((1, width)),
            whole((1, width)),
            whole(w_qkv.shape),
        ],
        [
            pl.BlockSpec((routed, width), lambda i, w: (i, 0)),
            pl.BlockSpec((routed, width), lambda i, w: (i, 0)),
            pl.BlockSpec((routed, joint), lambda i, w: (i, 0)),
            pl.BlockSpec((routed, routed), lambda i, w: (i, 0)),
            pl.BlockSpec((routed, wide), lambda i, w: (i, 0)),
            whole((8, 128)),
        ],
        [
            sds((total, width), BF16),
            sds((total, width), BF16),
            sds((total, joint), BF16),
            sds((total, routed), BF16),
            sds((total, wide), BF16),
            sds((8, 128), F32),
        ],
        2 * total * width * (length + joint) * 1.3,
        2 * seqs * length * width + 8 * total * width,
        "front",
    )(where, tokens, routes, segments, gain_one, router, w_qkv)

    mixed_all = [mixed] + [swap(mixed, "mp", j) for j in partners]

    dyr, gm, dh = call(
        cot_body,
        (seqs,),
        [
            pl.BlockSpec((length, width), lambda i, w: (i, 0)),
            whole(routes.shape),
            pl.BlockSpec((routed, width), lambda i, w: (i, 0)),
            whole((1, width)),
            whole(w_down.shape),
        ],
        [
            pl.BlockSpec((routed, width), lambda i, w: (i, 0)),
            pl.BlockSpec((routed, width), lambda i, w: (i, 0)),
            pl.BlockSpec((routed, hidden), lambda i, w: (i, 0)),
        ],
        [sds((total, width), BF16), sds((total, width), BF16), sds((total, hidden), F32)],
        2 * total * width * (length + hidden),
        2 * seqs * length * width + 6 * total * width + 4 * total * hidden,
        "cot",
    )(where, cotangent, routes, xr, router, w_down)

    order = partners[::-1] + [0]
    tile = min(own, 128)
    tiles = own // tile
    blocks = jnp.stack([rank ^ j for j in order])
    table = (blocks[:, None] * tiles + jnp.arange(tiles)[None, :]).reshape(-1).astype(jnp.int32)

    def by_row(i, t):
        return (t[i], 0)

    steps = parts * tiles
    attn, a2, hid, du, da2, gain_two_part = call(
        functools.partial(middle_body, parts),
        (steps,),
        [pl.BlockSpec((tile, wide), by_row)] * parts
        + [
            whole(w_all.shape),
            pl.BlockSpec((tile, width), by_row),
            pl.BlockSpec((tile, hidden), by_row),
            whole((1, width)),
            whole(w_up.shape),
        ],
        [
            pl.BlockSpec((tile, width), lambda i, t: (jnp.maximum(i - (steps - tiles), 0), 0)),
            pl.BlockSpec((tile, width), by_row),
            pl.BlockSpec((tile, hidden), by_row),
            pl.BlockSpec((tile, hidden), by_row),
            pl.BlockSpec((1, tile, width), lambda i, t: (i // tiles, i % tiles, 0)),
            whole((8, width)),
        ],
        [
            sds((own, width), F32),
            sds((total, width), BF16),
            sds((total, hidden), BF16),
            sds((total, hidden), BF16),
            sds((parts, own, width), BF16),
            sds((8, width), F32),
        ],
        2 * total * width * (parts * wide + 2 * hidden),
        total * (10 * width + 8 * hidden) + 2 * width * (hidden + parts * wide),
        "middle",
    )(table, *mixed_all, w_all, xr, dh, gain_two, w_up)

    da2_all = [da2[-1]] + [swap(da2[at], "mp", j) for at, j in enumerate(order[:-1])]

    mlp = dot(hid, w_down).astype(BF16)
    grad_up = dot(a2, du, TN).astype(BF16)
    grad_down = dot(hid, gm, TN).astype(BF16)
    mlp_all = [block_of(mlp, rank, own)] + [
        swap(block_of(mlp, rank ^ j, own), "mp", j) for j in partners
    ]

    own_tiles = lambda i, w: (w[0] * tiles + i, 0)
    flat = lambda i, w: (i, 0)
    row_block = pl.BlockSpec((tile, width), flat)
    own_block = pl.BlockSpec((tile, width), own_tiles)
    dyn, ga, dmix = call(
        functools.partial(rows_body, parts),
        (tiles,),
        [row_block] * parts
        + [row_block, own_block, own_block, whole((1, width)), whole((1, width)), whole(w_all.shape)],
        [row_block, row_block, pl.BlockSpec((parts, tile, wide), lambda i, w: (0, i, 0))],
        [sds((own, width), F32), sds((own, width), BF16), sds((parts, own, wide), BF16)],
        2 * own * width * parts * wide,
        own * width * 24 + 2 * width * width,
        "rows",
    )(where, *da2_all, attn, xr, dyr, gain_two, router, w_all)

    dmix_all = jnp.stack([dmix[0]] + [swap(dmix[j], "mp", j) for j in partners])

    upd, base, router_part = call(
        functools.partial(delta_body, parts),
        (tiles,),
        [row_block] * parts + [row_block, own_block, own_block, row_block, whole((1, width))],
        [row_block, row_block, whole((8, width))],
        [sds((own, width), BF16), sds((own, width), F32), sds((8, width), F32)],
        own * width * 20,
        own * width * 24,
        "delta",
    )(where, *mlp_all, attn, xr, dyr, dyn, router)
    upd_all = [upd] + [swap(upd, "mp", j) for j in partners]

    if aligned:
        by_owner = lambda i, w: ((i // per) ^ w[0], i % per, 0)
        da1_shape = (parts, own, width)
    else:
        dmix_all = dmix_all[jnp.arange(parts) ^ rank].reshape(1, total, wide)
        by_owner = lambda i, w: (0, i, 0)
        da1_shape = (1, total, width)
    dqkv, da1, gain_one_part = call(
        functools.partial(back_body, heads),
        (seqs,),
        [
            pl.BlockSpec((routed, joint), flat),
            pl.BlockSpec((routed, routed), flat),
            pl.BlockSpec((1, routed, wide), by_owner),
            pl.BlockSpec((routed, width), flat),
            whole((1, width)),
            whole(w_qkv.shape),
        ],
        [
            pl.BlockSpec((routed, joint), flat),
            pl.BlockSpec((1, routed, width), by_owner),
            whole((8, width)),
        ],
        [sds((total, joint), BF16), sds(da1_shape, BF16), sds((8, width), F32)],
        2 * total * width * joint * 1.5,
        total * (4 * joint + 6 * width) + 2 * width * joint,
        "back",
    )(where, qkv, mask, dmix_all, xr, gain_one, w_qkv)

    if aligned:
        da1_blocks = [da1[j] for j in range(parts)]
    else:
        da1_blocks = [block_of(da1[0], rank ^ j, own) for j in range(parts)]
    da1_all = [da1_blocks[0]] + [swap(da1_blocks[j], "mp", j) for j in partners]

    grad_qkv = dot(a1, dqkv, TN).astype(BF16)

    last = call(
        functools.partial(last_body, parts),
        (tiles,),
        [row_block] * parts + [own_block, row_block, whole((1, width))],
        row_block,
        sds((own, width), BF16),
        own * width * 20,
        own * width * 18,
        "last",
    )(where, *da1_all, xr, base, gain_one)
    last_all = [last] + [swap(last, "mp", j) for j in partners]

    def spread(source, rows_all, name):
        if not aligned:
            rows = jnp.stack(rows_all)[jnp.arange(parts) ^ rank].reshape(total, width)
            return put_rows(source, routes, rows, jnp.arange(seqs, dtype=jnp.int32), None, name)
        target = None
        for j, rows in enumerate(rows_all):
            seq = ((rank ^ j) * per + jnp.arange(per)).astype(jnp.int32)
            target = put_rows(source, routes, rows, seq, target, name)
        return target

    output = spread(tokens, upd_all, "put_out")
    grad_tokens = spread(cotangent, last_all, "put_grad")

    grad_up = core_join(line_sum(core_half(grad_up, core), depth), core)
    grad_down = core_join(line_sum(core_half(grad_down, core), depth), core)
    grad_qkv = core_join(line_sum(core_half(grad_qkv, core), depth), core)

    def out_part(j):
        rows = block_of(mixed_all[j], rank, own)
        return dot(rows, ga, TN).astype(BF16)

    outs = jnp.stack([out_part(j) for j in range(parts)], axis=1)
    outs = core_half(outs, core)
    half = outs[:, 0].astype(F32)
    for j in partners:
        half = half + swap(outs[:, j], "mp", j).astype(F32)
    grad_out = core_join(line_sum(half.astype(BF16), depth), core)

    lines = jnp.sum(
        jnp.stack([gain_one_part, gain_two_part, router_part]), axis=1
    )
    scores = jnp.concatenate(
        [score[0:1] / 1.0, score[1:2] / parts, jnp.zeros((6, 128), F32)], axis=0
    ).reshape(1, -1)
    scores = jnp.pad(scores, ((0, 0), (0, width - 1024))) if width > 1024 else scores[:, :width]
    small = jnp.concatenate([lines, scores, jnp.zeros((4, width), F32)], axis=0)
    bit = 1
    while bit < 2 * depth:
        small = small + swap(small, "dp", bit)
        bit *= 2
    bit = 1
    while bit < parts:
        small = small + swap(small, "mp", bit)
        bit *= 2
    score_total = small[3, 0]
    routed_total = small[3, 128]
    token_count = seqs * length * lax.axis_size("dp")
    return (
        output,
        grad_tokens,
        small[0],
        small[1],
        small[2],
        grad_qkv,
        grad_out,
        grad_up,
        grad_down,
        routed_total / score_total,
        score_total / token_count,
    )


STREAMS = ((1, 3, 0, 2), (2, 3, 0, 1))
FIRST = (1, 2)


def row(vector):
    return vector[...].astype(F32).reshape(1, -1)

def owner_spec(stream, rows, columns, slots=()):
    lead = tuple(slots)
    zeros = (0,) * len(lead)
    if stream == 0:
        return pl.BlockSpec(
            lead + (2, None, None, rows, columns), lambda i, w: zeros + (0, 1 - i, 0, 0, 0)
        )
    return pl.BlockSpec(
        lead + (None, 2, None, rows, columns), lambda i, w: zeros + (1 - i, 0, 1, 0, 0)
    )


def joined(value):
    return value.reshape(-1, value.shape[-1])


def parted(value):
    return value.reshape(2, -1, value.shape[-1])


def front_pair_body(heads, slice_rows, first, where, *refs):
    blocks = refs[:2]
    routes, segments, gain, router, w_qkv = refs[2:7]
    xr_out, give_out, keep_out, qkv_out, mask_out, lse_out, mixed_out, score_out = refs[-8:]
    step = pl.program_id(0)
    length, width = blocks[0].shape
    routed = routes.shape[1]
    vec = jnp.broadcast_to(row(router), (8, width)).astype(BF16)
    start = pl.multiple_of(where[RANK] * slice_rows, slice_rows)
    rows_all, allowed_all = [], []
    total = jnp.zeros((8, 1), F32)
    for at, tokens in enumerate(blocks):
        seq = where[first + 2 * step + at]
        hot, eye = one_hot_rows(routes[pl.ds(seq, 1), :], length)
        seg_line = segments[pl.ds(seq, 1), :].astype(F32)
        allowed = head_mask(hot, eye, seg_line)
        mask_out[at * routed : (at + 1) * routed, :] = jnp.where(allowed, 1.0, 0.0).astype(BF16)
        rows_all.append(dot(jnp.where(hot, 1.0, 0.0).astype(BF16), tokens[...]))
        allowed_all.append(allowed)
        scored = sigmoid(dot(vec, tokens[pl.ds(start, slice_rows), :], NT))
        total = total + jnp.sum(scored, axis=1, keepdims=True)
    rows = jnp.concatenate(rows_all, axis=0)
    low = rows.astype(BF16)
    xr_out[...] = parted(low)
    chosen = jnp.sum(sigmoid(dot(vec, low, NT)), axis=1, keepdims=True)

    @pl.when(step == 0)
    def _():
        score_out[...] = jnp.zeros_like(score_out)

    which = iota(score_out.shape, 0)
    score_out[...] += jnp.where(which == 0, total, jnp.where(which == 1, chosen, 0.0))
    inverse = lax.rsqrt(jnp.mean(rows * rows, axis=1, keepdims=True) + EPS)
    normed = (rows * inverse * row(gain)).astype(BF16)
    left, right = parted(normed[:, : width // 2]), parted(normed[:, width // 2 :])
    give_out[...] = jnp.where(where[CORE] == 0, right, left)
    keep_out[...] = jnp.where(where[CORE] == 0, left, right)
    joint = dot(normed, w_qkv[...]).astype(BF16)
    qkv_out[...] = joint
    logits = []
    for at in range(2):
        own = joint[at * routed : (at + 1) * routed]
        for head in range(heads):
            base = head * 3 * HD
            raw = dot(own[:, base : base + HD], own[:, base + HD : base + 2 * HD], NT)
            logits.append(jnp.where(allowed_all[at], raw * SCALE, -1e30))
    logits = jnp.concatenate(logits, axis=0)
    top = jnp.max(logits, axis=1, keepdims=True)
    expon = jnp.exp(logits - top)
    norm = jnp.sum(expon, axis=1, keepdims=True)
    sums = top + jnp.log(norm)
    probs = (expon * (1.0 / norm)).astype(BF16)
    for at in range(2):
        span = slice(at * routed, (at + 1) * routed)
        for head in range(heads):
            place = slice((at * heads + head) * routed, (at * heads + head + 1) * routed)
            base = head * 3 * HD
            value = joint[span, base + 2 * HD : base + 3 * HD]
            lse_out[span, head : head + 1] = sums[place]
            mixed_out[span, head * HD : (head + 1) * HD] = dot(probs[place], value).astype(BF16)


def cot_pair_body(where, *refs):
    blocks = refs[:2]
    routes, xr, router, w_down, dyr_out, gm_out, dh_out = refs[2:]
    step = pl.program_id(0)
    length = blocks[0].shape[0]
    picked = []
    for at, block in enumerate(blocks):
        hot, _ = one_hot_rows(routes[pl.ds(where[PUT + 2 * step + at], 1), :], length)
        picked.append(dot(jnp.where(hot, 1.0, 0.0).astype(BF16), block[...]))
    rows = jnp.concatenate(picked, axis=0)
    dyr_out[...] = rows.astype(BF16)
    rate = sigmoid(jnp.sum(xr[...].astype(F32) * row(router), axis=1, keepdims=True))
    low = (rate * rows).astype(BF16)
    gm_out[...] = low
    dh_out[...] = dot(low, w_down[...], NT)


def flip(value, swapped):
    half = value.shape[0] // 2
    if swapped:
        return jnp.concatenate([value[half:], value[:half]], axis=0)
    return value


def middle_pair_body(stream, where, *refs):
    mixed = refs[:4]
    w_parts = refs[4:8]
    xr, dh, gm, gain, w_up = refs[8:13]
    attn_out, left_give, left_keep, right_give, right_keep, hid_out, send_out, keep_out = refs[-8:]
    step = pl.program_id(0)
    plain = (0, FIRST[stream])
    attn = 0.0
    for part in range(4):
        attn = attn + dot(flip(mixed[part][...], part not in plain), w_parts[part][...])
    half = attn.shape[0] // 2
    attn_out[...] = attn[:half]
    y = joined(xr[...]).astype(F32) + attn
    scaled = y * lax.rsqrt(jnp.mean(y * y, axis=1, keepdims=True) + EPS)
    a2 = (scaled * row(gain)).astype(BF16)
    u = dot(a2, w_up[...])
    square = u * u
    t = jnp.tanh(u * (GELU_C + (GELU_C * GELU_A) * square))
    cdf = 0.5 + 0.5 * t
    hid = (u * cdf).astype(BF16)
    hid_out[...] = parted(hid)
    slope = cdf + (u * (1.0 - t * t)) * (0.5 * GELU_C + (1.5 * GELU_C * GELU_A) * square)
    du = (joined(dh[...]) * slope).astype(BF16)
    low = dot(du, w_up[...], NT).astype(BF16)
    first = where[CORE] == 0
    left_give[...] = parted(jnp.where(first, a2, hid))
    left_keep[...] = parted(jnp.where(first, hid, a2))
    down = joined(gm[...])
    right_give[...] = parted(jnp.where(first, du, down))
    right_keep[...] = parted(jnp.where(first, down, du))

    @pl.when(step == 0)
    def _():
        send_out[0] = low[:half]
        send_out[1] = low[half:]

    @pl.when(step == 1)
    def _():
        keep_out[0] = low[:half]
        keep_out[1] = low[half:]


def mlp_body(where, hid, w_down, *outs):
    value = dot(hid[...], w_down[...]).astype(BF16)
    for at, out in enumerate(outs):

        @pl.when(pl.program_id(0) == at)
        def _(out=out):
            out[...] = value


def summed(refs):
    rows = []
    for stream in range(2):
        keep, first, final = refs[3 * stream : 3 * stream + 3]
        rows.append(keep[0].astype(F32) + first[0].astype(F32) + final[...].astype(F32))
    return jnp.concatenate(rows, axis=0)


def both(left, right):
    return jnp.concatenate([left[...].astype(F32), right[...].astype(F32)], axis=0)


def fold(value):
    return jnp.sum(value.reshape(-1, 8, value.shape[1]), axis=0)


def rows_pair_body(where, *refs):
    da2 = summed(refs[:6])
    attn_a, attn_b, xr, dyr, gain, router = refs[6:12]
    w_parts = refs[12:16]
    dyn_out, ga_out, gain_out, do_outs = refs[16], refs[17], refs[18], refs[19:]
    rows = xr[...].astype(F32)
    y = rows + both(attn_a, attn_b)
    inverse = lax.rsqrt(jnp.mean(y * y, axis=1, keepdims=True) + EPS)
    scaled = y * inverse
    joint = da2 * scaled
    gain_out[...] = fold(joint)
    vec = row(gain)
    dyn = inverse * (vec * da2 - scaled * jnp.mean(vec * joint, axis=1, keepdims=True))
    dyn_out[...] = dyn
    rate = sigmoid(jnp.sum(rows * row(router), axis=1, keepdims=True))
    ga = (rate * dyr[...].astype(F32) + dyn).astype(BF16)
    ga_out[...] = ga
    for weight, out in zip(w_parts, do_outs):
        out[...] = dot(ga, weight[...], NT).astype(BF16)


def delta_pair_body(where, *refs):
    attn_a, attn_b, xr, dyr, dyn, router = refs[4:10]
    upd_out, base_out, grad_router_out = refs[10:]
    delta = both(attn_a, attn_b)
    for piece in refs[:4]:
        delta = delta + piece[...].astype(F32)
    rows = xr[...].astype(F32)
    grads = dyr[...].astype(F32)
    vec = row(router)
    rate = sigmoid(jnp.sum(rows * vec, axis=1, keepdims=True))
    upd_out[...] = (rows + rate * delta).astype(BF16)
    dlogit = jnp.sum(grads * delta, axis=1, keepdims=True) * rate * (1.0 - rate)
    base_out[...] = grads + dyn[...] + dlogit * vec
    grad_router_out[...] = fold(dlogit * rows)


def out_grad_body(where, *refs):
    ga, keep_out, give_out = refs[8:]
    half = keep_out.shape[1]
    grads = ga[...]
    for out, core in ((keep_out, where[CORE]), (give_out, 1 - where[CORE])):
        span = pl.ds(pl.multiple_of(core * half, half), half)
        for at, part in enumerate(STREAMS[0]):
            mixed = jnp.concatenate([refs[part][:, span], refs[4 + part][:, span]], axis=0)
            out[at] = dot(mixed, grads, TN).astype(BF16)


def back_pair_body(heads, stream, where, qkv, mask, lse, *refs):
    dmixed = refs[:4]
    w_qkv = refs[4]
    dqkv_out, send_out, keep_out = refs[-3:]
    step = pl.program_id(0)
    owners = STREAMS[stream]
    routed = mask.shape[1]
    logits, dprobs, norms, items = [], [], [], []
    for at in range(2):
        span = slice(at * routed, (at + 1) * routed)
        joint = qkv[span, :]
        allowed = mask[span, :].astype(F32) > 0.5
        grads = jnp.where(step == 0, dmixed[owners[at]][...], dmixed[owners[2 + at]][...])
        for head in range(heads):
            base = head * 3 * HD
            query = joint[:, base : base + HD]
            key = joint[:, base + HD : base + 2 * HD]
            value = joint[:, base + 2 * HD : base + 3 * HD]
            dmix = grads[:, head * HD : (head + 1) * HD]
            logits.append(jnp.where(allowed, dot(query, key, NT) * SCALE, -1e30))
            dprobs.append(dot(dmix, value, NT))
            norms.append(lse[span, head : head + 1])
            items.append((span, base, query, key, dmix))
    probs = jnp.exp(jnp.concatenate(logits, axis=0) - jnp.concatenate(norms, axis=0))
    dprobs = jnp.concatenate(dprobs, axis=0)
    spread = jnp.sum(probs * dprobs, axis=1, keepdims=True)
    dlogs = (probs * (dprobs - spread)).astype(BF16)
    probs = probs.astype(BF16)
    for at, (span, base, query, key, dmix) in enumerate(items):
        part = span.start // routed
        dlog = dlogs[at * routed : (at + 1) * routed]
        prob = probs[at * routed : (at + 1) * routed]
        dqkv_out[part, :, base : base + HD] = (dot(dlog, key) * SCALE).astype(BF16)
        dqkv_out[part, :, base + HD : base + 2 * HD] = (dot(dlog, query, TN) * SCALE).astype(BF16)
        dqkv_out[part, :, base + 2 * HD : base + 3 * HD] = dot(prob, dmix, TN).astype(BF16)
    low = dot(joined(dqkv_out[...]), w_qkv[...], NT).astype(BF16)

    @pl.when(step == 0)
    def _():
        send_out[0] = low[:routed]
        send_out[1] = low[routed:]

    @pl.when(step == 1)
    def _():
        keep_out[0] = low[:routed]
        keep_out[1] = low[routed:]


def last_pair_body(where, *refs):
    da1 = summed(refs[:6])
    xr, base, gain, gain_two, router_part, score_a, score_b, out = refs[6:]
    rows = xr[...].astype(F32)
    inverse = lax.rsqrt(jnp.mean(rows * rows, axis=1, keepdims=True) + EPS)
    scaled = rows * inverse
    joint = da1 * scaled
    vec = row(gain)
    dxn = inverse * (vec * da1 - scaled * jnp.mean(vec * joint, axis=1, keepdims=True))
    count, width = rows.shape
    out[:count, :] = (base[...] + dxn).astype(BF16)
    scores = score_a[...] + score_b[...]
    scores = jnp.concatenate(
        [scores[0:1], scores[1:2] / 4, jnp.zeros((1, width - 256), F32)], axis=1
    )
    at = iota((16, width), 0)
    small = jnp.zeros((16, width), F32)
    lines = [fold(joint), gain_two[...], router_part[...]]
    lines = [jnp.sum(line, axis=0, keepdims=True) for line in lines] + [scores]
    for index, line in enumerate(lines):
        small = jnp.where(at % 8 == index, line, small)
    high = small.astype(BF16).astype(F32)
    out[count:, :] = jnp.where(at < 8, high, small - high).astype(BF16)


def place_body(starts, where, source, routes, *refs):
    rows, out = refs[: len(starts)], refs[-1]
    step = pl.program_id(0)
    line = routes[pl.ds(where[PUT + put_entry(starts, step)], 1), :]
    fresh = rows[0][...]
    for at, start in enumerate(starts):
        if at:
            fresh = jnp.where(step >= start[0], rows[at][...], fresh)
    chunk = source.shape[0]

    def place(at, carry):
        first = pl.multiple_of(at * chunk, chunk)
        hot = iota((chunk, line.shape[1]), 0) + first == line
        picked = jnp.where(hot, 1.0, 0.0)
        taken = jnp.sum(picked, axis=1, keepdims=True) > 0.5
        moved = dot(picked.astype(BF16), fresh)
        span = pl.ds(first, chunk)
        out[span, :] = jnp.where(taken, moved, source[span, :].astype(F32)).astype(BF16)
        return carry

    lax.fori_loop(0, source.shape[0] // chunk, place, 0)


def put_entry(starts, step):
    entry = starts[0][1] + step
    for first, place in starts[1:]:
        entry = jnp.where(step >= first, place + step - first, entry)
    return entry


def place_rows(table, source, routes, parts, target, name):
    seqs, routed = routes.shape
    length = source.shape[0] // seqs
    width = source.shape[1]
    starts, step = [], 0
    block = lambda i, w: (w[PUT + put_entry(starts, i)], 0)
    in_specs = [pl.BlockSpec((length, width), block), whole(routes.shape)]
    args = [table, source, routes]
    for rows, place in parts:
        per = rows.shape[0] // routed
        starts.append((step, place))
        in_specs.append(
            pl.BlockSpec(
                (routed, width),
                lambda i, w, first=step, top=per - 1: (jnp.clip(i - first, 0, top), 0),
            )
        )
        args.append(rows)
        step += per
    alias = None
    if target is not None:
        in_specs.append(pl.BlockSpec(memory_space=pl.ANY))
        alias = {len(args): 0}
        args.append(target)
    return call(
        functools.partial(place_body, tuple(starts)),
        (step,),
        in_specs,
        pl.BlockSpec((length, width), block),
        jax.ShapeDtypeStruct(source.shape, BF16),
        1,
        1,
        name,
        alias=alias,
    )(*args)


def halves_body(where, value, side, pair, corner, down_out, up_out):
    step = pl.program_id(0)
    for late, (own, other) in enumerate(((value, pair), (side, corner))):
        for core, outs in enumerate(((down_out, up_out), (up_out, down_out))):

            @pl.when((step // 2 == late) & (where[CORE] == core))
            def _(own=own, other=other, outs=outs):
                outs[0][...] = own[...].astype(F32)
                outs[1][...] = other[...].astype(F32)


def join_halves(table, pieces):
    rows, columns = pieces[0].shape
    block = (rows // 2, columns)
    early = pl.BlockSpec(block, lambda i, w: (jnp.minimum(i, 1), 0))
    late = pl.BlockSpec(block, lambda i, w: (jnp.maximum(i - 2, 0), 0))
    placed = pl.BlockSpec(block, lambda i, w: (2 * (w[BIT] ^ (i // 2)) + i % 2, 0))
    value, pair, side, corner = pieces
    return call(
        halves_body,
        (4,),
        [early, late, early, late],
        [placed, placed],
        [jax.ShapeDtypeStruct((2 * rows, columns), F32)] * 2,
        1,
        1,
        "join",
    )(table, value, side, pair, corner)


def tail_body(where, *refs):
    qkv_out, out_out = refs[-2:]
    for at in range(4):

        @pl.when(pl.program_id(0) == at)
        def _(at=at):
            qkv_out[...] = refs[at][...].astype(F32)
            if at < 2:
                out_out[...] = refs[4 + at][...].astype(F32)


def join_tail(table, pieces, outs):
    rows, columns = pieces[0].shape
    few, wide = outs[0].shape
    return call(
        tail_body,
        (4,),
        [whole((rows, columns))] * 4 + [whole((few, wide))] * 2,
        [
            pl.BlockSpec((rows, columns), lambda i, w: (w[QUARTER + i], 0)),
            pl.BlockSpec((few, wide), lambda i, w: (w[14 + jnp.minimum(i, 1)], 0)),
        ],
        [
            jax.ShapeDtypeStruct((4 * rows, columns), F32),
            jax.ShapeDtypeStruct((2 * few, wide), F32),
        ],
        1,
        1,
        "join",
    )(table, *pieces, *outs)


def after(value, *others):
    return lax.optimization_barrier((value, *others))[0]


def add(left, right):
    return (left.astype(F32) + right.astype(F32)).astype(BF16)


class Total:
    def __init__(self, give, keep, bit):
        self.keep, self.bit = keep, bit
        self.sent = swap(give, "dp", 1)

    def split(self, *others):
        got = after(self.sent, *others)
        rows = got.shape[0] // 2
        cut = lambda index: add(block_of(self.keep, index, rows), block_of(got, index, rows))
        far = cut(1 - self.bit)
        self.value = cut(self.bit)
        self.sent = swap(far, "dp", 2)
        return far

    def cross(self, *others):
        self.value = add(self.value, after(self.sent, *others))
        self.sent = swap(self.value, "dp", 4)
        return self.value

    def close(self, *others):
        self.value = add(self.value, after(self.sent, *others))
        self.sent = swap(self.value, "dp", 2)
        return self.value

    def share(self, *others):
        self.pair = swap(after(self.value, *others), "dp", 1)

    def back(self, *others):
        self.side = after(self.sent, *others)
        self.corner = swap(self.side, "dp", 1)
        return self.side

    def pieces(self):
        return [self.value, self.pair, self.side, self.corner]


OWNERS = (1, 3, 0, 2, 2, 3, 0, 1)
HALVES = (0, 0, 0, 0, 1, 1, 1, 1)
RANK, CORE, QUARTER, PUT, BIT = 8, 9, 10, 16, 24


def make_table(rank, core, bit):
    owners = jnp.array(OWNERS + (0,) * 8 + (0, 0, 1, 1, 2, 2, 3, 3, 0), jnp.int32)
    halves = jnp.array(HALVES + (0,) * 8 + (0, 1) * 4 + (0,), jnp.int32)
    at = jnp.arange(25, dtype=jnp.int32)
    table = 2 * (rank ^ owners) + halves
    quarter = at - QUARTER
    quarters = 2 * (core ^ (quarter % 2)) + (bit ^ (quarter // 2))
    table = jnp.where((at >= QUARTER) & (at < QUARTER + 4), quarters, table)
    table = jnp.where(at == 14, core, jnp.where(at == 15, 1 - core, table))
    table = jnp.where(at == BIT, bit, table)
    return jnp.where(at == RANK, rank, jnp.where(at == CORE, core, table)).astype(jnp.int32)


def paired(
    tokens, segments, routes, cotangent, gain_attn, gain_mlp, w_router, w_qkv, w_out, w_up, w_down
):
    seqs, length = segments.shape
    routed = routes.shape[1]
    width = tokens.shape[1]
    wide = w_out.shape[0]
    heads = wide // HD
    joint = w_qkv.shape[1]
    hidden = w_up.shape[1]
    rank = lax.axis_index("mp")
    core = lax.axis_index("dp") % 2
    bit = lax.axis_index("dp") // 2 % 2
    half_rows = 4 * routed
    pair = 2 * routed
    total_rows = 8 * routed
    sds = jax.ShapeDtypeStruct
    flat = lambda i, w: (i, 0)
    line = whole((width,))
    table = make_table(rank, core, bit)
    anywhere = pl.BlockSpec(memory_space=pl.ANY)
    partners = (1, 2, 3)

    def held(columns, dtype=BF16):
        return sds((2, 2, 2, routed, columns), dtype)

    def rowed(value):
        return value.reshape(total_rows, value.shape[-1])

    def by_owner(value):
        return value.reshape(2, 2, 2, routed, value.shape[-1])

    w_parts = [w_out] + [swap(w_out, "mp", j) for j in partners]

    fronts = []
    for stream in range(2):
        carried = fronts[0][:3] if fronts else []
        fronts.append(
            call(
                functools.partial(front_pair_body, heads, length // 4, 4 * stream),
                (2,),
                [
                    pl.BlockSpec((length, width), lambda i, w, s=4 * stream: (w[2 * i + s], 0)),
                    pl.BlockSpec((length, width), lambda i, w, s=4 * stream: (w[2 * i + 1 + s], 0)),
                    whole(routes.shape),
                    whole(segments.shape),
                    line,
                    line,
                    whole(w_qkv.shape),
                ]
                + [anywhere] * len(carried),
                [
                    owner_spec(stream, routed, width),
                    owner_spec(stream, routed, width // 2),
                    owner_spec(stream, routed, width // 2),
                    pl.BlockSpec((pair, joint), flat),
                    pl.BlockSpec((pair, routed), flat),
                    pl.BlockSpec((pair, 128), flat),
                    pl.BlockSpec((pair, wide), flat),
                    whole((8, 128)),
                ],
                [
                    held(width),
                    held(width // 2),
                    held(width // 2),
                    sds((half_rows, joint), BF16),
                    sds((half_rows, routed), BF16),
                    sds((half_rows, 128), F32),
                    sds((half_rows, wide), BF16),
                    sds((8, 128), F32),
                ],
                1,
                1,
                "front",
                alias={8 + at: at for at in range(len(carried))},
            )(
                after(table, fronts[0][6]) if fronts else table,
                tokens, tokens, routes, segments, gain_attn, w_router, w_qkv, *carried,
            )
        )
    xr, a1_give, a1_keep = fronts[1][:3]
    qkv, mask, lse, heads_out, score = [list(kind) for kind in zip(*[f[3:] for f in fronts])]
    xr_rows = rowed(xr)

    dyr, gm, dh = call(
        cot_pair_body,
        (4,),
        [
            pl.BlockSpec((length, width), lambda i, w: (w[PUT + 2 * i], 0)),
            pl.BlockSpec((length, width), lambda i, w: (w[PUT + 2 * i + 1], 0)),
            whole(routes.shape),
            pl.BlockSpec((pair, width), flat),
            line,
            whole(w_down.shape),
        ],
        [
            pl.BlockSpec((pair, width), flat),
            pl.BlockSpec((pair, width), flat),
            pl.BlockSpec((pair, hidden), flat),
        ],
        [
            sds((total_rows, width), BF16),
            sds((total_rows, width), BF16),
            sds((total_rows, hidden), F32),
        ],
        1,
        1,
        "cot",
    )(table, cotangent, cotangent, routes, xr_rows, w_router, w_down)

    w_parts = [w_out] + [after(weight, heads_out[1]) for weight in w_parts[1:]]
    mixed = []
    for stream in range(2):
        near, far = FIRST[stream], FIRST[1 - stream]
        rows = after(heads_out[1], *w_parts[1:]) if stream else heads_out[0]
        beside = swap(rows, "mp", near)
        across = swap(rows, "mp", far)
        came = after(beside, gm) if stream else after(beside, *w_parts[1:])
        corner = swap(came, "mp", far)
        parts = [heads_out[stream], None, None, corner]
        parts[near], parts[far] = came, across
        mixed.append(parts)

    middles = []
    for stream in range(2):
        near = FIRST[stream]
        specs = []
        for part in range(4):
            crossed = part in (near, 3)
            specs.append(
                pl.BlockSpec((pair, wide), (lambda i, w: (1 - i, 0)) if crossed else flat)
            )
        carried = middles[0][1:6] if middles else []
        middles.append(
            call(
                functools.partial(middle_pair_body, stream),
                (2,),
                specs
                + [whole(w_out.shape)] * 4
                + [
                    owner_spec(stream, routed, width),
                    owner_spec(stream, routed, hidden),
                    owner_spec(stream, routed, width),
                    line,
                    whole(w_up.shape),
                ]
                + [anywhere] * len(carried),
                [whole((routed, width))]
                + [owner_spec(stream, routed, width)] * 5
                + [whole((2, routed, width))] * 2,
                [sds((routed, width), F32)]
                + [held(width)] * 5
                + [sds((2, routed, width), BF16)] * 2,
                1,
                1,
                "middle",
                alias={14 + at: 1 + at for at in range(len(carried))},
            )(
                after(table, middles[0][7]) if middles else table,
                *mixed[stream], *w_parts, xr, by_owner(dh), by_owner(gm), gain_mlp, w_up, *carried,
            )
        )
    attn = [middles[0][0], middles[1][0]]
    left_give, left_keep, right_give, right_keep, hid = [rowed(v) for v in middles[1][1:6]]
    send, keep = [[m[at] for m in middles] for at in (6, 7)]

    first_a = after(swap(send[0], "mp", FIRST[0]), keep[1])
    ahead_a = add(keep[0][1], first_a[1])
    final_a = swap(ahead_a, "mp", FIRST[1])

    ffn_give = dot(after(left_give, ahead_a), right_give, TN).astype(BF16)
    mlp = call(
        mlp_body,
        (4,),
        [pl.BlockSpec((pair, hidden), flat), whole(w_down.shape)],
        [whole((pair, width))] * 4,
        [sds((pair, width), BF16)] * 4,
        1,
        1,
        "mlp",
    )(after(table, ffn_give), hid, w_down)
    first_b = after(swap(send[1], "mp", FIRST[1]), mlp[0])
    ahead_b = add(keep[1][1], first_b[1])
    final_b = swap(ahead_b, "mp", FIRST[0])
    ffn_keep = dot(after(left_keep, ahead_b), right_keep, TN).astype(BF16)
    ffn = Total(after(ffn_give, ahead_b), ffn_keep, bit)
    ffn_far = ffn.split(ffn_keep)
    mlp_all = [mlp[0], swap(after(mlp[1], ahead_b), "mp", 1), None, None]

    own = pl.BlockSpec((pair, width), lambda i, w: (0, 0))
    pieces = [
        pl.BlockSpec((1, routed, width), lambda i, w: (0, 0, 0)),
        pl.BlockSpec((1, routed, width), lambda i, w: (0, 0, 0)),
        whole((routed, width)),
    ] * 2
    rows_out = call(
        rows_pair_body,
        (1,),
        pieces + [whole((routed, width))] * 2 + [own, own, line, line] + [whole(w_out.shape)] * 4,
        [whole((pair, width)), whole((pair, width)), whole((8, width))]
        + [whole((pair, wide))] * 4,
        [sds((pair, width), F32), sds((pair, width), BF16), sds((8, width), F32)]
        + [sds((pair, wide), BF16)] * 4,
        1,
        1,
        "rows",
    )(
        after(table, ffn_far), keep[0], first_a, final_a, keep[1], first_b,
        final_b, *attn, xr_rows, dyr, gain_mlp, w_router, *w_parts,
    )
    dyn, ga, gain_two_part = rows_out[:3]
    dmix = [rows_out[3]] + [swap(rows_out[3 + j], "mp", j) for j in partners]

    out_specs = [
        pl.BlockSpec((routed, wide), lambda i, w, at=STREAMS[s].index(j): (at, 0))
        for s in (0, 1)
        for j in range(4)
    ]
    outs_keep, outs_give = call(
        out_grad_body,
        (1,),
        out_specs + [whole((pair, width))],
        [whole((4, wide // 2, width))] * 2,
        [sds((4, wide // 2, width), BF16)] * 2,
        1,
        1,
        "outs",
    )(after(table, ga), *mixed[0], *mixed[1], ga)
    outs_got = swap(outs_give, "dp", 1)
    dmix = [dmix[0]] + [after(value, outs_keep) for value in dmix[1:]]
    mlp_all[1] = after(mlp_all[1], *dmix[1:])
    mlp_all[2] = swap(after(mlp[2], mlp_all[1]), "mp", 2)
    mlp_all[3] = swap(after(mlp[3], mlp_all[1]), "mp", 3)
    ffn_now = ffn.cross(mlp_all[1])

    backs = []
    for stream in range(2):
        cut = pl.BlockSpec((routed, wide), lambda i, w, s=stream: (s, 0))
        carried = backs[0][:1] if backs else []
        backs.append(
            call(
                functools.partial(back_pair_body, heads, stream),
                (2,),
                [
                    pl.BlockSpec((pair, joint), flat),
                    pl.BlockSpec((pair, routed), flat),
                    pl.BlockSpec((pair, 128), flat),
                    cut,
                    cut,
                    cut,
                    cut,
                    whole(w_qkv.shape),
                ]
                + [anywhere] * len(carried),
                [
                    owner_spec(stream, routed, joint),
                    whole((2, routed, width)),
                    whole((2, routed, width)),
                ],
                [
                    held(joint),
                    sds((2, routed, width), BF16),
                    sds((2, routed, width), BF16),
                ],
                1,
                1,
                "back",
                alias={9: 0} if carried else None,
            )(
                after(table, backs[0][2]) if backs else after(table, ffn_now),
                qkv[stream], mask[stream], lse[stream], *dmix, w_qkv, *carried,
            )
        )
    dqkv = rowed(backs[1][0])
    back_send, back_keep = [[b[at] for b in backs] for at in (1, 2)]
    mlp_all[2] = after(mlp_all[2], back_keep[1])
    outs_got = after(outs_got, back_keep[1])
    qkv_give = dot(rowed(a1_give), dqkv, TN).astype(BF16)
    last_first_a = after(swap(back_send[0], "mp", FIRST[0]), qkv_give)
    last_ahead_a = add(back_keep[0][1], last_first_a[1])
    last_final_a = swap(last_ahead_a, "mp", FIRST[1])
    qkv_keep = dot(rowed(after(a1_keep, last_ahead_a)), dqkv, TN).astype(BF16)
    whole_qkv = Total(qkv_give, qkv_keep, bit)
    outs_x = add(after(outs_keep, qkv_keep)[:2], outs_got[:2])
    outs_sent = swap(outs_x, "mp", 1)
    mlp_all[3] = after(mlp_all[3], outs_x)

    upd, base, router_part = call(
        delta_pair_body,
        (1,),
        [whole((pair, width))] * 4
        + [whole((routed, width))] * 2
        + [own, own, whole((pair, width)), line],
        [whole((pair, width)), whole((pair, width)), whole((8, width))],
        [sds((pair, width), BF16), sds((pair, width), F32), sds((8, width), F32)],
        1,
        1,
        "delta",
    )(after(table, outs_x), *mlp_all, *attn, xr_rows, dyr, dyn, w_router)

    last_first_b = after(swap(back_send[1], "mp", FIRST[1]), base)
    last_ahead_b = add(back_keep[1][1], last_first_b[1])
    last_final_b = swap(last_ahead_b, "mp", FIRST[0])

    outs_sent = after(outs_sent, last_ahead_b)

    def outs_of(at, *more):
        value = outs_keep[2 + at].astype(F32) + outs_got[2 + at].astype(F32)
        for other in (outs_sent[at], *more):
            value = value + other.astype(F32)
        return value.astype(BF16)


    def put(source, parts, target, name, *others):
        return place_rows(after(table, *others), source, routes, parts, target, name)

    outs_ahead = outs_of(1)
    outs_final = swap(outs_ahead, "mp", 2)
    qkv_far = whole_qkv.split(outs_ahead)

    output = put(tokens, [(upd, 0)], None, "put_own", qkv_far)
    ffn_now = ffn.close(output)
    upd_all = [upd, swap(after(upd, output), "mp", 1), None, None]
    out_half = outs_of(0, after(outs_final, ffn_now))
    last = call(
        last_pair_body,
        (1,),
        pieces
        + [own, whole((pair, width)), line]
        + [whole((8, width))] * 2
        + [whole((8, 128))] * 2,
        [whole((pair + 16, width))],
        [sds((pair + 16, width), BF16)],
        1,
        1,
        "last",
    )(
        after(table, out_half), back_keep[0], last_first_a, last_final_a, back_keep[1],
        last_first_b, last_final_b, xr_rows, base, gain_attn, gain_two_part, router_part, *score,
    )[0]
    upd_all[2] = swap(after(upd, last), "mp", 2)
    grads = put(cotangent, [(last, 0)], None, "put_own", last)
    qkv_now = whole_qkv.cross(grads)
    upd_all[1:3] = [after(value, qkv_now) for value in upd_all[1:3]]
    last_all = [last] + [swap(after(last, *upd_all[1:3]), "mp", j) for j in (1, 2)] + [None]
    upd_all[3] = swap(upd_all[1], "mp", 2)
    output = put(tokens, [(upd_all[1], 2), (upd_all[2], 4)], output, "put_out", grads)
    last_all[1:3] = [after(value, output) for value in last_all[1:3]]
    last_all[3] = swap(last_all[2], "mp", 1)
    out_sent = swap(after(out_half, *last_all[1:3]), "dp", 2)
    grads = put(cotangent, [(last_all[1], 2), (last_all[2], 4)], grads, "put_grad", qkv_now)
    upd_all[3] = after(upd_all[3], grads)
    output = put(tokens, [(upd_all[3], 6)], output, "put_out", grads)
    out_half = add(out_half, after(out_sent, output))
    out_sent = swap(out_half, "dp", 4)
    qkv_now = whole_qkv.close(out_half)
    ffn.share(qkv_now)
    last_all[3] = after(last_all[3], qkv_now)
    small = 0.0
    for rows in last_all:
        small = small + rows[pair : pair + 8].astype(F32) + rows[pair + 8 :].astype(F32)
    small_sent = swap(small, "dp", 2)
    grads = put(cotangent, [(last_all[3], 6)], grads, "put_grad", small)
    small = small + after(small_sent, grads)
    small_sent = swap(small, "dp", 4)
    side = ffn.back(small)
    ffn.pair = after(ffn.pair, side)
    whole_qkv.share(ffn.pair)
    grad_down, grad_up = join_halves(after(table, side), ffn.pieces())
    side = whole_qkv.back(grad_up)
    whole_qkv.pair = after(whole_qkv.pair, side)
    small = small + after(small_sent, whole_qkv.pair)
    small_sent = swap(small, "dp", 1)
    out_half = add(out_half, after(out_sent, small))
    out_sent = swap(out_half, "dp", 1)
    grad_qkv, grad_out = join_tail(
        after(table, out_half), whole_qkv.pieces(), [out_half, out_sent]
    )
    small = small + after(small_sent, grad_out)

    score_total = small[3, 0]
    routed_total = small[3, 128]
    token_count = seqs * length * lax.axis_size("dp")
    return (
        output,
        grads,
        small[0],
        small[1],
        small[2],
        grad_qkv,
        grad_out,
        grad_up,
        grad_down,
        routed_total / score_total,
        score_total / token_count,
    )


def shards(*arrays):
    tokens, segments, routes, w_out, w_up = (arrays[at] for at in (0, 1, 2, 8, 9))
    square = lax.axis_size("mp") == 4 and segments.shape[0] == 8 and lax.axis_size("dp") == 8
    square = square and w_up.shape[1] == tokens.shape[1] and tokens.shape[1] % 256 == 0
    if square and routes.shape[1] % 128 == 0 and w_out.shape[0] % 128 == 0:
        return paired(*arrays)
    return general(*arrays)


def solution(mesh):
    rows = P("dp", None)
    columns = P(None, "mp")
    lines = P("mp", None)
    in_specs = (rows, rows, rows, rows, P(), P(), P(), columns, lines, columns, lines)
    out_specs = (rows, rows, P(), P(), P(), columns, lines, columns, lines, P(), P())
    return jax.shard_map(shards, mesh=mesh, in_specs=in_specs, out_specs=out_specs, check_vma=False)
```

```python
import functools

import jax
import jax.numpy as jnp
from jax import lax
from jax.experimental import pallas as pl
from jax.experimental.pallas import tpu as pltpu
from jax.sharding import PartitionSpec as P

HD = 64
EPS = 1e-06
SCALE = HD ** (-0.5)
GELU_C = (2.0 / 3.141592653589793) ** 0.5
GELU_A = 0.044715
F32 = jnp.float32
BF16 = jnp.bfloat16


def dot(left, right, on=((1,), (0,))):
    return lax.dot_general(left, right, (on, ((), ())), preferred_element_type=F32)


NT = ((1,), (1,))
TN = ((0,), (0,))


def iota(shape, axis):
    return lax.broadcasted_iota(jnp.int32, shape, axis)


def sigmoid(value):
    return 1.0 / (1.0 + jnp.exp(-value))


LENGTHS = {
    "front": 5.2, "cot": 3.2, "middle": 5.5, "rows": 2.8, "outs": 3.9, "back": 1.0,
    "delta": 0.01, "mlp": 0.01, "last": 0.33, "put_own": 0.01, "put_out": 2.4, "put_grad": 2.4, "join": 1.5,
}
RATE = 1.5e9


def call(body, grid, in_specs, out_specs, out_shape, flops, nbytes, name, scratch=(), alias=None):
    if flops == 1:
        flops = LENGTHS[name] * grid[0] * RATE
        nbytes = 1
    return pl.pallas_call(
        body,
        grid_spec=pltpu.PrefetchScalarGridSpec(
            num_scalar_prefetch=1,
            grid=grid,
            in_specs=in_specs,
            out_specs=out_specs,
            scratch_shapes=list(scratch),
        ),
        out_shape=out_shape,
        cost_estimate=pl.CostEstimate(
            flops=int(flops), bytes_accessed=int(nbytes), transcendentals=0
        ),
        input_output_aliases=alias or {},
        name=name,
    )


def whole(shape):
    zeros = (0,) * len(shape)
    return pl.BlockSpec(shape, lambda *_: zeros)


def one_hot_rows(routes_row, length):
    routed = routes_row.shape[1]
    eye = iota((routed, routed), 0) == iota((routed, routed), 1)
    column = jnp.sum(jnp.where(eye, routes_row.astype(F32), 0.0), axis=1, keepdims=True)
    return iota((routed, length), 1) == column.astype(jnp.int32), eye


def head_mask(hot, eye, seg_line):
    seg_col = jnp.sum(jnp.where(hot, seg_line, 0.0), axis=1, keepdims=True)
    seg_row = jnp.sum(jnp.where(eye, seg_col, 0.0), axis=0, keepdims=True)
    routed = eye.shape[0]
    causal = iota((routed, routed), 0) >= iota((routed, routed), 1)
    return causal & (seg_col == seg_row)


def softmax_head(query, key, allowed):
    logits = jnp.where(allowed, dot(query, key, NT) * SCALE, -1e30)
    expon = jnp.exp(logits - jnp.max(logits, axis=1, keepdims=True))
    return expon / jnp.sum(expon, axis=1, keepdims=True)


def front_body(
    heads, slice_rows, where, tokens, routes, segments, gain, router, w_qkv,
    xr_out, a1_out, qkv_out, mask_out, mixed_out, score_out,
):
    step = pl.program_id(0)
    length = tokens.shape[0]
    hot, eye = one_hot_rows(routes[pl.ds(step, 1), :], length)
    seg_line = segments[pl.ds(step, 1), :].astype(F32)
    allowed = head_mask(hot, eye, seg_line)
    mask_out[...] = jnp.where(allowed, 1.0, 0.0).astype(BF16)
    rows = dot(jnp.where(hot, 1.0, 0.0).astype(BF16), tokens[...])
    xr_out[...] = rows.astype(BF16)
    vec = router[...].astype(F32)
    start = pl.multiple_of(where[0] * slice_rows, slice_rows)
    part = tokens[pl.ds(start, slice_rows), :].astype(F32)
    total = jnp.sum(sigmoid(jnp.sum(part * vec, axis=1, keepdims=True)), axis=0, keepdims=True)
    chosen = jnp.sum(sigmoid(jnp.sum(rows * vec, axis=1, keepdims=True)), axis=0, keepdims=True)

    @pl.when(step == 0)
    def _():
        score_out[...] = jnp.zeros_like(score_out)

    which = iota(score_out.shape, 0)
    score_out[...] += jnp.where(which == 0, total, jnp.where(which == 1, chosen, 0.0))
    inverse = lax.rsqrt(jnp.mean(rows * rows, axis=1, keepdims=True) + EPS)
    normed = (rows * inverse * gain[...].astype(F32)).astype(BF16)
    a1_out[...] = normed
    joint = dot(normed, w_qkv[...]).astype(BF16)
    qkv_out[...] = joint
    for head in range(heads):
        base = head * 3 * HD
        query = joint[:, base : base + HD]
        key = joint[:, base + HD : base + 2 * HD]
        value = joint[:, base + 2 * HD : base + 3 * HD]
        probs = softmax_head(query, key, allowed).astype(BF16)
        mixed_out[:, head * HD : (head + 1) * HD] = dot(probs, value).astype(BF16)


def cot_body(where, cotangent, routes, xr, router, w_down, dyr_out, gm_out, dh_out):
    step = pl.program_id(0)
    hot, _ = one_hot_rows(routes[pl.ds(step, 1), :], cotangent.shape[0])
    rows = dot(jnp.where(hot, 1.0, 0.0).astype(BF16), cotangent[...])
    dyr_out[...] = rows.astype(BF16)
    vec = router[...].astype(F32)
    rate = sigmoid(jnp.sum(xr[...].astype(F32) * vec, axis=1, keepdims=True))
    low = (rate * rows).astype(BF16)
    gm_out[...] = low
    dh_out[...] = dot(low, w_down[...], NT)


def middle_body(parts, table, *refs):
    mixed = refs[:parts]
    w_out, xr, dh, gain, w_up = refs[parts : parts + 5]
    attn_out, a2_out, hid_out, du_out, da2_out, gain_out = refs[parts + 5 :]
    attn = dot(mixed[0][...], w_out[0])
    for part in range(1, parts):
        attn = attn + dot(mixed[part][...], w_out[part])
    attn_out[...] = attn
    y = xr[...].astype(F32) + attn
    scaled = y * lax.rsqrt(jnp.mean(y * y, axis=1, keepdims=True) + EPS)
    a2 = (scaled * gain[...].astype(F32)).astype(BF16)
    a2_out[...] = a2
    u = dot(a2, w_up[...])
    square = u * u
    t = jnp.tanh(GELU_C * (u + GELU_A * (u * square)))
    hid_out[...] = (0.5 * u * (1.0 + t)).astype(BF16)
    slope = 0.5 * (1.0 + t) + (0.5 * GELU_C) * u * (1.0 - t * t) * (1.0 + 3.0 * GELU_A * square)
    du = (dh[...] * slope).astype(BF16)
    du_out[...] = du
    da2 = dot(du, w_up[...], NT)
    da2_out[0] = da2.astype(BF16)

    @pl.when(pl.program_id(0) == 0)
    def _():
        gain_out[...] = jnp.zeros_like(gain_out)

    gain_out[...] += jnp.sum((da2 * scaled).reshape(-1, 8, da2.shape[1]), axis=0)


def rows_body(parts, where, *refs):
    pieces = refs[:parts]
    attn, xr, dyr, gain, router, w_out = refs[parts : parts + 6]
    dyn_out, ga_out, do_out = refs[parts + 6 :]
    da2 = pieces[0][...].astype(F32)
    for piece in pieces[1:]:
        da2 = da2 + piece[...].astype(F32)
    rows = xr[...].astype(F32)
    y = rows + attn[...]
    inverse = lax.rsqrt(jnp.mean(y * y, axis=1, keepdims=True) + EPS)
    t = gain[...].astype(F32) * da2
    scaled = y * inverse
    dyn = inverse * (t - scaled * jnp.mean(t * scaled, axis=1, keepdims=True))
    dyn_out[...] = dyn
    rate = sigmoid(jnp.sum(rows * router[...].astype(F32), axis=1, keepdims=True))
    ga = (rate * dyr[...].astype(F32) + dyn).astype(BF16)
    ga_out[...] = ga
    for part in range(parts):
        do_out[part] = dot(ga, w_out[part], NT).astype(BF16)


def delta_body(parts, where, *refs):
    pieces = refs[:parts]
    attn, xr, dyr, dyn, router = refs[parts : parts + 5]
    upd_out, base_out, grad_router_out = refs[parts + 5 :]
    delta = attn[...]
    for piece in pieces:
        delta = delta + piece[...].astype(F32)
    rows = xr[...].astype(F32)
    grads = dyr[...].astype(F32)
    vec = router[...].astype(F32)
    rate = sigmoid(jnp.sum(rows * vec, axis=1, keepdims=True))
    upd_out[...] = (rows + rate * delta).astype(BF16)
    dlogit = jnp.sum(grads * delta, axis=1, keepdims=True) * rate * (1.0 - rate)
    base_out[...] = grads + dyn[...] + dlogit * vec

    @pl.when(pl.program_id(0) == 0)
    def _():
        grad_router_out[...] = jnp.zeros_like(grad_router_out)

    grad_router_out[...] += jnp.sum((dlogit * rows).reshape(-1, 8, rows.shape[1]), axis=0)


def back_body(heads, where, qkv, mask, dmixed, xr, gain, w_qkv, dqkv_out, da1_out, gain_out):
    joint = qkv[...]
    allowed = mask[...].astype(F32) > 0.5
    grads = dmixed[0]
    pieces = []
    for head in range(heads):
        base = head * 3 * HD
        query = joint[:, base : base + HD]
        key = joint[:, base + HD : base + 2 * HD]
        value = joint[:, base + 2 * HD : base + 3 * HD]
        dmix = grads[:, head * HD : (head + 1) * HD]
        probs = softmax_head(query, key, allowed)
        dprobs = dot(dmix, value, NT)
        spread = jnp.sum(probs * dprobs, axis=1, keepdims=True)
        dlog = (probs * (dprobs - spread)).astype(BF16)
        dquery = dot(dlog, key) * SCALE
        dkey = dot(dlog, query, TN) * SCALE
        dvalue = dot(probs.astype(BF16), dmix, TN)
        pieces += [dquery.astype(BF16), dkey.astype(BF16), dvalue.astype(BF16)]
    for at, piece in enumerate(pieces):
        dqkv_out[:, at * HD : (at + 1) * HD] = piece
    da1 = dot(dqkv_out[...], w_qkv[...], NT)
    da1_out[0] = da1.astype(BF16)
    rows = xr[...].astype(F32)
    scaled = rows * lax.rsqrt(jnp.mean(rows * rows, axis=1, keepdims=True) + EPS)

    @pl.when(pl.program_id(0) == 0)
    def _():
        gain_out[...] = jnp.zeros_like(gain_out)

    gain_out[...] += jnp.sum((da1 * scaled).reshape(-1, 8, da1.shape[1]), axis=0)


def last_body(parts, where, *refs):
    pieces = refs[:parts]
    xr, base, gain = refs[parts : parts + 3]
    (out,) = refs[parts + 3 :]
    da1 = pieces[0][...].astype(F32)
    for piece in pieces[1:]:
        da1 = da1 + piece[...].astype(F32)
    rows = xr[...].astype(F32)
    inverse = lax.rsqrt(jnp.mean(rows * rows, axis=1, keepdims=True) + EPS)
    t = gain[...].astype(F32) * da1
    scaled = rows * inverse
    dxn = inverse * (t - scaled * jnp.mean(t * scaled, axis=1, keepdims=True))
    out[...] = (base[...] + dxn).astype(BF16)


def put_body(where, source, routes, rows, *refs):
    out = refs[-1]
    length = source.shape[0]
    at = where[pl.program_id(0)]
    line = routes[pl.ds(at, 1), :]
    hot = iota((length, line.shape[1]), 0) == line
    picked = jnp.where(hot, 1.0, 0.0)
    taken = jnp.sum(picked, axis=1, keepdims=True) > 0.5
    moved = dot(picked.astype(BF16), rows[...])
    out[...] = jnp.where(taken, moved, source[...].astype(F32)).astype(BF16)


def put_rows(source, routes, rows, order, target, name):
    seqs, routed = routes.shape
    length = source.shape[0] // seqs
    width = source.shape[1]
    count = rows.shape[0] // routed
    in_specs = [
        pl.BlockSpec((length, width), lambda i, w: (w[i], 0)),
        whole(routes.shape),
        pl.BlockSpec((routed, width), lambda i, w: (i, 0)),
    ]
    args = [order, source, routes, rows]
    alias = None
    if target is not None:
        in_specs.append(pl.BlockSpec(memory_space=pl.ANY))
        args.append(target)
        alias = {4: 0}
    return call(
        put_body,
        (count,),
        in_specs,
        pl.BlockSpec((length, width), lambda i, w: (w[i], 0)),
        jax.ShapeDtypeStruct(source.shape, BF16),
        2 * count * length * routed * width,
        count * length * width * 4,
        name,
        alias=alias,
    )(*args)


def swap(value, axis, offset):
    size = lax.axis_size(axis)
    return lax.ppermute(value, axis, [(i, i ^ offset) for i in range(size)])


def block_of(value, index, rows):
    return lax.dynamic_slice_in_dim(value, index * rows, rows, 0)


def in_core_order(core, mine, other):
    return jnp.where(
        core == 0,
        jnp.concatenate([mine, other], axis=0),
        jnp.concatenate([other, mine], axis=0),
    )


def line_sum(value, depth):
    at = lax.axis_index("dp") // 2
    half = depth // 2

    def shift(array, pairs):
        return lax.ppermute(
            array, "dp", [(2 * a + c, 2 * b + c) for a, b in pairs for c in range(2)]
        )

    def mirrored(a, b):
        return [(a, b), (depth - 1 - a, depth - 1 - b)]

    for step in range(half - 1):
        got = shift(value, mirrored(step, step + 1))
        value = (value.astype(F32) + got.astype(F32)).astype(BF16)
    if depth > 1:
        got = shift(value, mirrored(half - 1, half))
        value = (value.astype(F32) + got.astype(F32)).astype(BF16)
    for step in reversed(range(half - 1)):
        got = shift(value, mirrored(step + 1, step))
        here = (at == step) | (at == depth - 1 - step)
        value = jnp.where(here, got, value)
    return value


def core_half(value, core):
    half = value.shape[0] // 2
    keep = block_of(value, core, half)
    give = block_of(value, 1 - core, half)
    got = swap(give.astype(BF16), "dp", 1)
    return (keep.astype(F32) + got.astype(F32)).astype(BF16)


def core_join(value, core):
    return in_core_order(core, value, swap(value, "dp", 1)).astype(F32)


def general(
    tokens, segments, routes, cotangent, gain_attn, gain_mlp, w_router, w_qkv, w_out, w_up, w_down
):
    seqs, length = segments.shape
    routed = routes.shape[1]
    width = tokens.shape[1]
    total = seqs * routed
    wide = w_out.shape[0]
    heads = wide // HD
    joint = w_qkv.shape[1]
    hidden = w_up.shape[1]
    parts = lax.axis_size("mp")
    depth = lax.axis_size("dp") // 2
    own = total // parts
    rank = lax.axis_index("mp")
    core = lax.axis_index("dp") % 2
    aligned = own % routed == 0
    per = own // routed if aligned else 1
    where = rank.reshape(1).astype(jnp.int32)
    gain_one = gain_attn.reshape(1, width)
    gain_two = gain_mlp.reshape(1, width)
    router = w_router.reshape(1, width)
    partners = list(range(1, parts))
    sds = jax.ShapeDtypeStruct

    share = block_of(w_out, core, wide // 2)
    mine = jnp.stack([swap(share, "mp", j) for j in partners])
    other = swap(mine, "dp", 1)
    w_all = jnp.where(
        core == 0,
        jnp.concatenate([mine, other], axis=1),
        jnp.concatenate([other, mine], axis=1),
    )
    w_all = jnp.concatenate([w_out[None], w_all], axis=0)

    xr, a1, qkv, mask, mixed, score = call(
        functools.partial(front_body, heads, length // parts),
        (seqs,),
        [
            pl.BlockSpec((length, width), lambda i, w: (i, 0)),
            whole(routes.shape),
            whole(segments.shape),
            whole((1, width)),
            whole((1, width)),
            whole(w_qkv.shape),
        ],
        [
            pl.BlockSpec((routed, width), lambda i, w: (i, 0)),
            pl.BlockSpec((routed, width), lambda i, w: (i, 0)),
            pl.BlockSpec((routed, joint), lambda i, w: (i, 0)),
            pl.BlockSpec((routed, routed), lambda i, w: (i, 0)),
            pl.BlockSpec((routed, wide), lambda i, w: (i, 0)),
            whole((8, 128)),
        ],
        [
            sds((total, width), BF16),
            sds((total, width), BF16),
            sds((total, joint), BF16),
            sds((total, routed), BF16),
            sds((total, wide), BF16),
            sds((8, 128), F32),
        ],
        2 * total * width * (length + joint) * 1.3,
        2 * seqs * length * width + 8 * total * width,
        "front",
    )(where, tokens, routes, segments, gain_one, router, w_qkv)

    mixed_all = [mixed] + [swap(mixed, "mp", j) for j in partners]

    dyr, gm, dh = call(
        cot_body,
        (seqs,),
        [
            pl.BlockSpec((length, width), lambda i, w: (i, 0)),
            whole(routes.shape),
            pl.BlockSpec((routed, width), lambda i, w: (i, 0)),
            whole((1, width)),
            whole(w_down.shape),
        ],
        [
            pl.BlockSpec((routed, width), lambda i, w: (i, 0)),
            pl.BlockSpec((routed, width), lambda i, w: (i, 0)),
            pl.BlockSpec((routed, hidden), lambda i, w: (i, 0)),
        ],
        [sds((total, width), BF16), sds((total, width), BF16), sds((total, hidden), F32)],
        2 * total * width * (length + hidden),
        2 * seqs * length * width + 6 * total * width + 4 * total * hidden,
        "cot",
    )(where, cotangent, routes, xr, router, w_down)

    order = partners[::-1] + [0]
    tile = min(own, 128)
    tiles = own // tile
    blocks = jnp.stack([rank ^ j for j in order])
    table = (blocks[:, None] * tiles + jnp.arange(tiles)[None, :]).reshape(-1).astype(jnp.int32)

    def by_row(i, t):
        return (t[i], 0)

    steps = parts * tiles
    attn, a2, hid, du, da2, gain_two_part = call(
        functools.partial(middle_body, parts),
        (steps,),
        [pl.BlockSpec((tile, wide), by_row)] * parts
        + [
            whole(w_all.shape),
            pl.BlockSpec((tile, width), by_row),
            pl.BlockSpec((tile, hidden), by_row),
            whole((1, width)),
            whole(w_up.shape),
        ],
        [
            pl.BlockSpec((tile, width), lambda i, t: (jnp.maximum(i - (steps - tiles), 0), 0)),
            pl.BlockSpec((tile, width), by_row),
            pl.BlockSpec((tile, hidden), by_row),
            pl.BlockSpec((tile, hidden), by_row),
            pl.BlockSpec((1, tile, width), lambda i, t: (i // tiles, i % tiles, 0)),
            whole((8, width)),
        ],
        [
            sds((own, width), F32),
            sds((total, width), BF16),
            sds((total, hidden), BF16),
            sds((total, hidden), BF16),
            sds((parts, own, width), BF16),
            sds((8, width), F32),
        ],
        2 * total * width * (parts * wide + 2 * hidden),
        total * (10 * width + 8 * hidden) + 2 * width * (hidden + parts * wide),
        "middle",
    )(table, *mixed_all, w_all, xr, dh, gain_two, w_up)

    da2_all = [da2[-1]] + [swap(da2[at], "mp", j) for at, j in enumerate(order[:-1])]

    mlp = dot(hid, w_down).astype(BF16)
    grad_up = dot(a2, du, TN).astype(BF16)
    grad_down = dot(hid, gm, TN).astype(BF16)
    mlp_all = [block_of(mlp, rank, own)] + [
        swap(block_of(mlp, rank ^ j, own), "mp", j) for j in partners
    ]

    own_tiles = lambda i, w: (w[0] * tiles + i, 0)
    flat = lambda i, w: (i, 0)
    row_block = pl.BlockSpec((tile, width), flat)
    own_block = pl.BlockSpec((tile, width), own_tiles)
    dyn, ga, dmix = call(
        functools.partial(rows_body, parts),
        (tiles,),
        [row_block] * parts
        + [row_block, own_block, own_block, whole((1, width)), whole((1, width)), whole(w_all.shape)],
        [row_block, row_block, pl.BlockSpec((parts, tile, wide), lambda i, w: (0, i, 0))],
        [sds((own, width), F32), sds((own, width), BF16), sds((parts, own, wide), BF16)],
        2 * own * width * parts * wide,
        own * width * 24 + 2 * width * width,
        "rows",
    )(where, *da2_all, attn, xr, dyr, gain_two, router, w_all)

    dmix_all = jnp.stack([dmix[0]] + [swap(dmix[j], "mp", j) for j in partners])

    upd, base, router_part = call(
        functools.partial(delta_body, parts),
        (tiles,),
        [row_block] * parts + [row_block, own_block, own_block, row_block, whole((1, width))],
        [row_block, row_block, whole((8, width))],
        [sds((own, width), BF16), sds((own, width), F32), sds((8, width), F32)],
        own * width * 20,
        own * width * 24,
        "delta",
    )(where, *mlp_all, attn, xr, dyr, dyn, router)
    upd_all = [upd] + [swap(upd, "mp", j) for j in partners]

    if aligned:
        by_owner = lambda i, w: ((i // per) ^ w[0], i % per, 0)
        da1_shape = (parts, own, width)
    else:
        dmix_all = dmix_all[jnp.arange(parts) ^ rank].reshape(1, total, wide)
        by_owner = lambda i, w: (0, i, 0)
        da1_shape = (1, total, width)
    dqkv, da1, gain_one_part = call(
        functools.partial(back_body, heads),
        (seqs,),
        [
            pl.BlockSpec((routed, joint), flat),
            pl.BlockSpec((routed, routed), flat),
            pl.BlockSpec((1, routed, wide), by_owner),
            pl.BlockSpec((routed, width), flat),
            whole((1, width)),
            whole(w_qkv.shape),
        ],
        [
            pl.BlockSpec((routed, joint), flat),
            pl.BlockSpec((1, routed, width), by_owner),
            whole((8, width)),
        ],
        [sds((total, joint), BF16), sds(da1_shape, BF16), sds((8, width), F32)],
        2 * total * width * joint * 1.5,
        total * (4 * joint + 6 * width) + 2 * width * joint,
        "back",
    )(where, qkv, mask, dmix_all, xr, gain_one, w_qkv)

    if aligned:
        da1_blocks = [da1[j] for j in range(parts)]
    else:
        da1_blocks = [block_of(da1[0], rank ^ j, own) for j in range(parts)]
    da1_all = [da1_blocks[0]] + [swap(da1_blocks[j], "mp", j) for j in partners]

    grad_qkv = dot(a1, dqkv, TN).astype(BF16)

    last = call(
        functools.partial(last_body, parts),
        (tiles,),
        [row_block] * parts + [own_block, row_block, whole((1, width))],
        row_block,
        sds((own, width), BF16),
        own * width * 20,
        own * width * 18,
        "last",
    )(where, *da1_all, xr, base, gain_one)
    last_all = [last] + [swap(last, "mp", j) for j in partners]

    def spread(source, rows_all, name):
        if not aligned:
            rows = jnp.stack(rows_all)[jnp.arange(parts) ^ rank].reshape(total, width)
            return put_rows(source, routes, rows, jnp.arange(seqs, dtype=jnp.int32), None, name)
        target = None
        for j, rows in enumerate(rows_all):
            seq = ((rank ^ j) * per + jnp.arange(per)).astype(jnp.int32)
            target = put_rows(source, routes, rows, seq, target, name)
        return target

    output = spread(tokens, upd_all, "put_out")
    grad_tokens = spread(cotangent, last_all, "put_grad")

    grad_up = core_join(line_sum(core_half(grad_up, core), depth), core)
    grad_down = core_join(line_sum(core_half(grad_down, core), depth), core)
    grad_qkv = core_join(line_sum(core_half(grad_qkv, core), depth), core)

    def out_part(j):
        rows = block_of(mixed_all[j], rank, own)
        return dot(rows, ga, TN).astype(BF16)

    outs = jnp.stack([out_part(j) for j in range(parts)], axis=1)
    outs = core_half(outs, core)
    half = outs[:, 0].astype(F32)
    for j in partners:
        half = half + swap(outs[:, j], "mp", j).astype(F32)
    grad_out = core_join(line_sum(half.astype(BF16), depth), core)

    lines = jnp.sum(
        jnp.stack([gain_one_part, gain_two_part, router_part]), axis=1
    )
    scores = jnp.concatenate(
        [score[0:1] / 1.0, score[1:2] / parts, jnp.zeros((6, 128), F32)], axis=0
    ).reshape(1, -1)
    scores = jnp.pad(scores, ((0, 0), (0, width - 1024))) if width > 1024 else scores[:, :width]
    small = jnp.concatenate([lines, scores, jnp.zeros((4, width), F32)], axis=0)
    bit = 1
    while bit < 2 * depth:
        small = small + swap(small, "dp", bit)
        bit *= 2
    bit = 1
    while bit < parts:
        small = small + swap(small, "mp", bit)
        bit *= 2
    score_total = small[3, 0]
    routed_total = small[3, 128]
    token_count = seqs * length * lax.axis_size("dp")
    return (
        output,
        grad_tokens,
        small[0],
        small[1],
        small[2],
        grad_qkv,
        grad_out,
        grad_up,
        grad_down,
        routed_total / score_total,
        score_total / token_count,
    )


STREAMS = ((1, 3, 0, 2), (2, 3, 0, 1))
FIRST = (1, 2)


def row(vector):
    return vector[...].astype(F32).reshape(1, -1)

def owner_spec(stream, rows, columns, slots=()):
    lead = tuple(slots)
    zeros = (0,) * len(lead)
    if stream == 0:
        return pl.BlockSpec(
            lead + (2, None, None, rows, columns), lambda i, w: zeros + (0, 1 - i, 0, 0, 0)
        )
    return pl.BlockSpec(
        lead + (None, 2, None, rows, columns), lambda i, w: zeros + (1 - i, 0, 1, 0, 0)
    )


def joined(value):
    return value.reshape(-1, value.shape[-1])


def parted(value):
    return value.reshape(2, -1, value.shape[-1])


def front_pair_body(heads, slice_rows, first, where, *refs):
    blocks = refs[:2]
    routes, segments, gain, router, w_qkv = refs[2:7]
    xr_out, give_out, keep_out, qkv_out, mask_out, lse_out, mixed_out, score_out = refs[-8:]
    step = pl.program_id(0)
    length, width = blocks[0].shape
    routed = routes.shape[1]
    vec = jnp.broadcast_to(row(router), (8, width)).astype(BF16)
    start = pl.multiple_of(where[RANK] * slice_rows, slice_rows)
    rows_all, allowed_all = [], []
    total = jnp.zeros((8, 1), F32)
    for at, tokens in enumerate(blocks):
        seq = where[first + 2 * step + at]
        hot, eye = one_hot_rows(routes[pl.ds(seq, 1), :], length)
        seg_line = segments[pl.ds(seq, 1), :].astype(F32)
        allowed = head_mask(hot, eye, seg_line)
        mask_out[at * routed : (at + 1) * routed, :] = jnp.where(allowed, 1.0, 0.0).astype(BF16)
        rows_all.append(dot(jnp.where(hot, 1.0, 0.0).astype(BF16), tokens[...]))
        allowed_all.append(allowed)
        scored = sigmoid(dot(vec, tokens[pl.ds(start, slice_rows), :], NT))
        total = total + jnp.sum(scored, axis=1, keepdims=True)
    rows = jnp.concatenate(rows_all, axis=0)
    low = rows.astype(BF16)
    xr_out[...] = parted(low)
    chosen = jnp.sum(sigmoid(dot(vec, low, NT)), axis=1, keepdims=True)

    @pl.when(step == 0)
    def _():
        score_out[...] = jnp.zeros_like(score_out)

    which = iota(score_out.shape, 0)
    score_out[...] += jnp.where(which == 0, total, jnp.where(which == 1, chosen, 0.0))
    inverse = lax.rsqrt(jnp.mean(rows * rows, axis=1, keepdims=True) + EPS)
    normed = (rows * inverse * row(gain)).astype(BF16)
    left, right = parted(normed[:, : width // 2]), parted(normed[:, width // 2 :])
    give_out[...] = jnp.where(where[CORE] == 0, right, left)
    keep_out[...] = jnp.where(where[CORE] == 0, left, right)
    joint = dot(normed, w_qkv[...]).astype(BF16)
    qkv_out[...] = joint
    logits = []
    for at in range(2):
        own = joint[at * routed : (at + 1) * routed]
        for head in range(heads):
            base = head * 3 * HD
            raw = dot(own[:, base : base + HD], own[:, base + HD : base + 2 * HD], NT)
            logits.append(jnp.where(allowed_all[at], raw * SCALE, -1e30))
    logits = jnp.concatenate(logits, axis=0)
    top = jnp.max(logits, axis=1, keepdims=True)
    expon = jnp.exp(logits - top)
    norm = jnp.sum(expon, axis=1, keepdims=True)
    sums = top + jnp.log(norm)
    probs = (expon * (1.0 / norm)).astype(BF16)
    for at in range(2):
        span = slice(at * routed, (at + 1) * routed)
        for head in range(heads):
            place = slice((at * heads + head) * routed, (at * heads + head + 1) * routed)
            base = head * 3 * HD
            value = joint[span, base + 2 * HD : base + 3 * HD]
            lse_out[span, head : head + 1] = sums[place]
            mixed_out[span, head * HD : (head + 1) * HD] = dot(probs[place], value).astype(BF16)


def cot_pair_body(where, *refs):
    blocks = refs[:2]
    routes, xr, router, w_down, dyr_out, gm_out, dh_out = refs[2:]
    step = pl.program_id(0)
    length = blocks[0].shape[0]
    picked = []
    for at, block in enumerate(blocks):
        hot, _ = one_hot_rows(routes[pl.ds(where[PUT + 2 * step + at], 1), :], length)
        picked.append(dot(jnp.where(hot, 1.0, 0.0).astype(BF16), block[...]))
    rows = jnp.concatenate(picked, axis=0)
    dyr_out[...] = rows.astype(BF16)
    rate = sigmoid(jnp.sum(xr[...].astype(F32) * row(router), axis=1, keepdims=True))
    low = (rate * rows).astype(BF16)
    gm_out[...] = low
    dh_out[...] = dot(low, w_down[...], NT)


def flip(value, swapped):
    half = value.shape[0] // 2
    if swapped:
        return jnp.concatenate([value[half:], value[:half]], axis=0)
    return value


def middle_pair_body(stream, where, *refs):
    mixed = refs[:4]
    w_parts = refs[4:8]
    xr, dh, gm, gain, w_up = refs[8:13]
    attn_out, left_give, left_keep, right_give, right_keep, hid_out, send_out, keep_out = refs[-8:]
    step = pl.program_id(0)
    plain = (0, FIRST[stream])
    attn = 0.0
    for part in range(4):
        attn = attn + dot(flip(mixed[part][...], part not in plain), w_parts[part][...])
    half = attn.shape[0] // 2
    attn_out[...] = attn[:half]
    y = joined(xr[...]).astype(F32) + attn
    scaled = y * lax.rsqrt(jnp.mean(y * y, axis=1, keepdims=True) + EPS)
    a2 = (scaled * row(gain)).astype(BF16)
    u = dot(a2, w_up[...])
    square = u * u
    t = jnp.tanh(u * (GELU_C + (GELU_C * GELU_A) * square))
    cdf = 0.5 + 0.5 * t
    hid = (u * cdf).astype(BF16)
    hid_out[...] = parted(hid)
    slope = cdf + (u * (1.0 - t * t)) * (0.5 * GELU_C + (1.5 * GELU_C * GELU_A) * square)
    du = (joined(dh[...]) * slope).astype(BF16)
    low = dot(du, w_up[...], NT).astype(BF16)
    first = where[CORE] == 0
    left_give[...] = parted(jnp.where(first, a2, hid))
    left_keep[...] = parted(jnp.where(first, hid, a2))
    down = joined(gm[...])
    right_give[...] = parted(jnp.where(first, du, down))
    right_keep[...] = parted(jnp.where(first, down, du))

    @pl.when(step == 0)
    def _():
        send_out[0] = low[:half]
        send_out[1] = low[half:]

    @pl.when(step == 1)
    def _():
        keep_out[0] = low[:half]
        keep_out[1] = low[half:]


def mlp_body(where, hid, w_down, *outs):
    value = dot(hid[...], w_down[...]).astype(BF16)
    for at, out in enumerate(outs):

        @pl.when(pl.program_id(0) == at)
        def _(out=out):
            out[...] = value


def either(step, left, right):
    return jnp.where(step == 0, left, right).astype(F32)


def summed(step, refs):
    keep, first, final = [
        either(step, refs[at][...], refs[3 + at][...]) for at in range(3)
    ]
    return joined(keep) + joined(first) + final


def fold(value):
    return jnp.sum(value.reshape(-1, 8, value.shape[1]), axis=0)


def collect(step, out, value):
    @pl.when(step == 0)
    def _():
        out[...] = jnp.zeros_like(out)

    out[...] += value


def rows_pair_body(where, *refs):
    step = pl.program_id(0)
    da2 = summed(step, refs[:6])
    attn_a, attn_b, xr, dyr, gain, router = refs[6:12]
    w_parts = refs[12:16]
    dyn_out, ga_out, gain_out, do_outs = refs[16], refs[17], refs[18], refs[19:]
    rows = xr[...].astype(F32)
    y = rows + either(step, attn_a[...], attn_b[...])
    inverse = lax.rsqrt(jnp.mean(y * y, axis=1, keepdims=True) + EPS)
    scaled = y * inverse
    joint = da2 * scaled
    collect(step, gain_out, fold(joint))
    vec = row(gain)
    dyn = inverse * (vec * da2 - scaled * jnp.mean(vec * joint, axis=1, keepdims=True))
    dyn_out[...] = dyn
    rate = sigmoid(jnp.sum(rows * row(router), axis=1, keepdims=True))
    ga = (rate * dyr[...].astype(F32) + dyn).astype(BF16)
    ga_out[...] = ga
    for weight, out in zip(w_parts, do_outs):
        out[...] = dot(ga, weight[...], NT).astype(BF16)


def delta_pair_body(where, *refs):
    attn_a, attn_b, xr, dyr, dyn, router = refs[4:10]
    upd_out, base_out, grad_router_out = refs[10:]
    step = pl.program_id(0)
    delta = either(step, attn_a[...], attn_b[...])
    for piece in refs[:4]:
        delta = delta + piece[...].astype(F32)
    rows = xr[...].astype(F32)
    grads = dyr[...].astype(F32)
    vec = row(router)
    rate = sigmoid(jnp.sum(rows * vec, axis=1, keepdims=True))
    upd_out[...] = (rows + rate * delta).astype(BF16)
    dlogit = jnp.sum(grads * delta, axis=1, keepdims=True) * rate * (1.0 - rate)
    base_out[...] = grads + dyn[...] + dlogit * vec
    collect(step, grad_router_out, fold(dlogit * rows))


def out_grad_body(where, *refs):
    ga, keep_out, give_out = refs[8:]
    half = keep_out.shape[1]
    grads = ga[...]
    for out, core in ((keep_out, where[CORE]), (give_out, 1 - where[CORE])):
        span = pl.ds(pl.multiple_of(core * half, half), half)
        for at, part in enumerate(STREAMS[0]):
            mixed = jnp.concatenate([refs[part][:, span], refs[4 + part][:, span]], axis=0)
            out[at] = dot(mixed, grads, TN).astype(BF16)


def back_pair_body(heads, stream, where, qkv, mask, lse, *refs):
    dmixed = refs[:4]
    w_qkv = refs[4]
    dqkv_out, send_out, keep_out = refs[-3:]
    step = pl.program_id(0)
    owners = STREAMS[stream]
    routed = mask.shape[1]
    logits, dprobs, norms, items = [], [], [], []
    for at in range(2):
        span = slice(at * routed, (at + 1) * routed)
        joint = qkv[span, :]
        allowed = mask[span, :].astype(F32) > 0.5
        grads = jnp.where(step == 0, dmixed[owners[at]][...], dmixed[owners[2 + at]][...])
        for head in range(heads):
            base = head * 3 * HD
            query = joint[:, base : base + HD]
            key = joint[:, base + HD : base + 2 * HD]
            value = joint[:, base + 2 * HD : base + 3 * HD]
            dmix = grads[:, head * HD : (head + 1) * HD]
            logits.append(jnp.where(allowed, dot(query, key, NT) * SCALE, -1e30))
            dprobs.append(dot(dmix, value, NT))
            norms.append(lse[span, head : head + 1])
            items.append((span, base, query, key, dmix))
    probs = jnp.exp(jnp.concatenate(logits, axis=0) - jnp.concatenate(norms, axis=0))
    dprobs = jnp.concatenate(dprobs, axis=0)
    spread = jnp.sum(probs * dprobs, axis=1, keepdims=True)
    dlogs = (probs * (dprobs - spread)).astype(BF16)
    probs = probs.astype(BF16)
    for at, (span, base, query, key, dmix) in enumerate(items):
        part = span.start // routed
        dlog = dlogs[at * routed : (at + 1) * routed]
        prob = probs[at * routed : (at + 1) * routed]
        dqkv_out[part, :, base : base + HD] = (dot(dlog, key) * SCALE).astype(BF16)
        dqkv_out[part, :, base + HD : base + 2 * HD] = (dot(dlog, query, TN) * SCALE).astype(BF16)
        dqkv_out[part, :, base + 2 * HD : base + 3 * HD] = dot(prob, dmix, TN).astype(BF16)
    low = dot(joined(dqkv_out[...]), w_qkv[...], NT).astype(BF16)

    @pl.when(step == 0)
    def _():
        send_out[0] = low[:routed]
        send_out[1] = low[routed:]

    @pl.when(step == 1)
    def _():
        keep_out[0] = low[:routed]
        keep_out[1] = low[routed:]


def last_pair_body(where, *refs):
    xr, base, gain, gain_two, router_part, score_a, score_b, out, gain_sum = refs[6:]
    step = pl.program_id(0)

    @pl.when(step < 2)
    def _():
        da1 = summed(step, refs[:6])
        rows = xr[...].astype(F32)
        inverse = lax.rsqrt(jnp.mean(rows * rows, axis=1, keepdims=True) + EPS)
        scaled = rows * inverse
        joint = da1 * scaled
        collect(step, gain_sum, fold(joint))
        vec = row(gain)
        dxn = inverse * (vec * da1 - scaled * jnp.mean(vec * joint, axis=1, keepdims=True))
        out[...] = (base[...] + dxn).astype(BF16)

    @pl.when(step == 2)
    def _():
        width = out.shape[1]
        scores = score_a[...] + score_b[...]
        scores = jnp.concatenate(
            [scores[0:1], scores[1:2] / 4, jnp.zeros((1, width - 256), F32)], axis=1
        )
        at = iota((16, width), 0)
        small = jnp.zeros((16, width), F32)
        lines = [gain_sum[...], gain_two[...], router_part[...]]
        lines = [jnp.sum(line, axis=0, keepdims=True) for line in lines] + [scores]
        for index, line in enumerate(lines):
            small = jnp.where(at % 8 == index, line, small)
        high = small.astype(BF16).astype(F32)
        out[:16, :] = jnp.where(at < 8, high, small - high).astype(BF16)


def place_body(starts, where, source, routes, *refs):
    rows, out = refs[: len(starts)], refs[-1]
    step = pl.program_id(0)
    line = routes[pl.ds(where[PUT + put_entry(starts, step)], 1), :]
    fresh = rows[0][...]
    for at, start in enumerate(starts):
        if at:
            fresh = jnp.where(step >= start[0], rows[at][...], fresh)
    chunk = min(256, source.shape[0])

    def place(at, carry):
        first = pl.multiple_of(at * chunk, chunk)
        hot = iota((chunk, line.shape[1]), 0) + first == line
        picked = jnp.where(hot, 1.0, 0.0)
        taken = jnp.sum(picked, axis=1, keepdims=True) > 0.5
        moved = dot(picked.astype(BF16), fresh)
        span = pl.ds(first, chunk)
        out[span, :] = jnp.where(taken, moved, source[span, :].astype(F32)).astype(BF16)
        return carry

    lax.fori_loop(0, source.shape[0] // chunk, place, 0)


def put_entry(starts, step):
    entry = starts[0][1] + step
    for first, place in starts[1:]:
        entry = jnp.where(step >= first, place + step - first, entry)
    return entry


def place_rows(table, source, routes, parts, target, name):
    seqs, routed = routes.shape
    length = source.shape[0] // seqs
    width = source.shape[1]
    starts, step = [], 0
    block = lambda i, w: (w[PUT + put_entry(starts, i)], 0)
    in_specs = [pl.BlockSpec((length, width), block), whole(routes.shape)]
    args = [table, source, routes]
    for rows, place in parts:
        per = rows.shape[0] // routed
        starts.append((step, place))
        in_specs.append(
            pl.BlockSpec(
                (routed, width),
                lambda i, w, first=step, top=per - 1: (jnp.clip(i - first, 0, top), 0),
            )
        )
        args.append(rows)
        step += per
    alias = None
    if target is not None:
        in_specs.append(pl.BlockSpec(memory_space=pl.ANY))
        alias = {len(args): 0}
        args.append(target)
    return call(
        functools.partial(place_body, tuple(starts)),
        (step,),
        in_specs,
        pl.BlockSpec((length, width), block),
        jax.ShapeDtypeStruct(source.shape, BF16),
        1,
        1,
        name,
        alias=alias,
    )(*args)


def halves_body(where, value, side, pair, corner, down_out, up_out):
    step = pl.program_id(0)
    for late, (own, other) in enumerate(((value, pair), (side, corner))):
        for core, outs in enumerate(((down_out, up_out), (up_out, down_out))):

            @pl.when((step // 2 == late) & (where[CORE] == core))
            def _(own=own, other=other, outs=outs):
                outs[0][...] = own[...].astype(F32)
                outs[1][...] = other[...].astype(F32)


def join_halves(table, pieces):
    rows, columns = pieces[0].shape
    block = (rows // 2, columns)
    early = pl.BlockSpec(block, lambda i, w: (jnp.minimum(i, 1), 0))
    late = pl.BlockSpec(block, lambda i, w: (jnp.maximum(i - 2, 0), 0))
    placed = pl.BlockSpec(block, lambda i, w: (2 * (w[BIT] ^ (i // 2)) + i % 2, 0))
    value, pair, side, corner = pieces
    return call(
        halves_body,
        (4,),
        [early, late, early, late],
        [placed, placed],
        [jax.ShapeDtypeStruct((2 * rows, columns), F32)] * 2,
        1,
        1,
        "join",
    )(table, value, side, pair, corner)


def tail_body(where, *refs):
    qkv_out, out_out = refs[-2:]
    for at in range(4):

        @pl.when(pl.program_id(0) == at)
        def _(at=at):
            qkv_out[...] = refs[at][...].astype(F32)
            if at < 2:
                out_out[...] = refs[4 + at][...].astype(F32)


def join_tail(table, pieces, outs):
    rows, columns = pieces[0].shape
    few, wide = outs[0].shape
    return call(
        tail_body,
        (4,),
        [whole((rows, columns))] * 4 + [whole((few, wide))] * 2,
        [
            pl.BlockSpec((rows, columns), lambda i, w: (w[QUARTER + i], 0)),
            pl.BlockSpec((few, wide), lambda i, w: (w[14 + jnp.minimum(i, 1)], 0)),
        ],
        [
            jax.ShapeDtypeStruct((4 * rows, columns), F32),
            jax.ShapeDtypeStruct((2 * few, wide), F32),
        ],
        1,
        1,
        "join",
    )(table, *pieces, *outs)


def after(value, *others):
    return lax.optimization_barrier((value, *others))[0]


def add(left, right):
    return (left.astype(F32) + right.astype(F32)).astype(BF16)


class Total:
    def __init__(self, give, keep, bit):
        self.keep, self.bit = keep, bit
        self.sent = swap(give, "dp", 1)

    def split(self, *others):
        got = after(self.sent, *others)
        rows = got.shape[0] // 2
        cut = lambda index: add(block_of(self.keep, index, rows), block_of(got, index, rows))
        far = cut(1 - self.bit)
        self.value = cut(self.bit)
        self.sent = swap(far, "dp", 2)
        return far

    def cross(self, *others):
        self.value = add(self.value, after(self.sent, *others))
        self.sent = swap(self.value, "dp", 4)
        return self.value

    def close(self, *others):
        self.value = add(self.value, after(self.sent, *others))
        self.sent = swap(self.value, "dp", 2)
        return self.value

    def share(self, *others):
        self.pair = swap(after(self.value, *others), "dp", 1)

    def back(self, *others):
        self.side = after(self.sent, *others)
        self.corner = swap(self.side, "dp", 1)
        return self.side

    def pieces(self):
        return [self.value, self.pair, self.side, self.corner]


OWNERS = (1, 3, 0, 2, 2, 3, 0, 1)
HALVES = (0, 0, 0, 0, 1, 1, 1, 1)
RANK, CORE, QUARTER, PUT, BIT = 8, 9, 10, 16, 24


def make_table(rank, core, bit):
    owners = jnp.array(OWNERS + (0,) * 8 + (0, 0, 1, 1, 2, 2, 3, 3, 0), jnp.int32)
    halves = jnp.array(HALVES + (0,) * 8 + (0, 1) * 4 + (0,), jnp.int32)
    at = jnp.arange(25, dtype=jnp.int32)
    table = 2 * (rank ^ owners) + halves
    quarter = at - QUARTER
    quarters = 2 * (core ^ (quarter % 2)) + (bit ^ (quarter // 2))
    table = jnp.where((at >= QUARTER) & (at < QUARTER + 4), quarters, table)
    table = jnp.where(at == 14, core, jnp.where(at == 15, 1 - core, table))
    table = jnp.where(at == BIT, bit, table)
    return jnp.where(at == RANK, rank, jnp.where(at == CORE, core, table)).astype(jnp.int32)


def paired(
    tokens, segments, routes, cotangent, gain_attn, gain_mlp, w_router, w_qkv, w_out, w_up, w_down
):
    seqs, length = segments.shape
    routed = routes.shape[1]
    width = tokens.shape[1]
    wide = w_out.shape[0]
    heads = wide // HD
    joint = w_qkv.shape[1]
    hidden = w_up.shape[1]
    rank = lax.axis_index("mp")
    core = lax.axis_index("dp") % 2
    bit = lax.axis_index("dp") // 2 % 2
    half_rows = 4 * routed
    pair = 2 * routed
    total_rows = 8 * routed
    sds = jax.ShapeDtypeStruct
    flat = lambda i, w: (i, 0)
    line = whole((width,))
    table = make_table(rank, core, bit)
    anywhere = pl.BlockSpec(memory_space=pl.ANY)
    partners = (1, 2, 3)

    def held(columns, dtype=BF16):
        return sds((2, 2, 2, routed, columns), dtype)

    def rowed(value):
        return value.reshape(total_rows, value.shape[-1])

    def by_owner(value):
        return value.reshape(2, 2, 2, routed, value.shape[-1])

    w_parts = [w_out] + [swap(w_out, "mp", j) for j in partners]

    fronts = []
    for stream in range(2):
        carried = fronts[0][:3] if fronts else []
        fronts.append(
            call(
                functools.partial(front_pair_body, heads, length // 4, 4 * stream),
                (2,),
                [
                    pl.BlockSpec((length, width), lambda i, w, s=4 * stream: (w[2 * i + s], 0)),
                    pl.BlockSpec((length, width), lambda i, w, s=4 * stream: (w[2 * i + 1 + s], 0)),
                    whole(routes.shape),
                    whole(segments.shape),
                    line,
                    line,
                    whole(w_qkv.shape),
                ]
                + [anywhere] * len(carried),
                [
                    owner_spec(stream, routed, width),
                    owner_spec(stream, routed, width // 2),
                    owner_spec(stream, routed, width // 2),
                    pl.BlockSpec((pair, joint), flat),
                    pl.BlockSpec((pair, routed), flat),
                    pl.BlockSpec((pair, 128), flat),
                    pl.BlockSpec((pair, wide), flat),
                    whole((8, 128)),
                ],
                [
                    held(width),
                    held(width // 2),
                    held(width // 2),
                    sds((half_rows, joint), BF16),
                    sds((half_rows, routed), BF16),
                    sds((half_rows, 128), F32),
                    sds((half_rows, wide), BF16),
                    sds((8, 128), F32),
                ],
                1,
                1,
                "front",
                alias={8 + at: at for at in range(len(carried))},
            )(
                after(table, fronts[0][6]) if fronts else table,
                tokens, tokens, routes, segments, gain_attn, w_router, w_qkv, *carried,
            )
        )
    xr, a1_give, a1_keep = fronts[1][:3]
    qkv, mask, lse, heads_out, score = [list(kind) for kind in zip(*[f[3:] for f in fronts])]
    xr_rows = rowed(xr)

    dyr, gm, dh = call(
        cot_pair_body,
        (4,),
        [
            pl.BlockSpec((length, width), lambda i, w: (w[PUT + 2 * i], 0)),
            pl.BlockSpec((length, width), lambda i, w: (w[PUT + 2 * i + 1], 0)),
            whole(routes.shape),
            pl.BlockSpec((pair, width), flat),
            line,
            whole(w_down.shape),
        ],
        [
            pl.BlockSpec((pair, width), flat),
            pl.BlockSpec((pair, width), flat),
            pl.BlockSpec((pair, hidden), flat),
        ],
        [
            sds((total_rows, width), BF16),
            sds((total_rows, width), BF16),
            sds((total_rows, hidden), F32),
        ],
        1,
        1,
        "cot",
    )(table, cotangent, cotangent, routes, xr_rows, w_router, w_down)

    w_parts = [w_out] + [after(weight, heads_out[1]) for weight in w_parts[1:]]
    mixed = []
    for stream in range(2):
        near, far = FIRST[stream], FIRST[1 - stream]
        rows = after(heads_out[1], *w_parts[1:]) if stream else heads_out[0]
        beside = swap(rows, "mp", near)
        across = swap(rows, "mp", far)
        came = after(beside, gm) if stream else after(beside, *w_parts[1:])
        corner = swap(came, "mp", far)
        parts = [heads_out[stream], None, None, corner]
        parts[near], parts[far] = came, across
        mixed.append(parts)

    middles = []
    for stream in range(2):
        near = FIRST[stream]
        specs = []
        for part in range(4):
            crossed = part in (near, 3)
            specs.append(
                pl.BlockSpec((pair, wide), (lambda i, w: (1 - i, 0)) if crossed else flat)
            )
        carried = middles[0][1:6] if middles else []
        middles.append(
            call(
                functools.partial(middle_pair_body, stream),
                (2,),
                specs
                + [whole(w_out.shape)] * 4
                + [
                    owner_spec(stream, routed, width),
                    owner_spec(stream, routed, hidden),
                    owner_spec(stream, routed, width),
                    line,
                    whole(w_up.shape),
                ]
                + [anywhere] * len(carried),
                [whole((routed, width))]
                + [owner_spec(stream, routed, width)] * 5
                + [whole((2, routed, width))] * 2,
                [sds((routed, width), F32)]
                + [held(width)] * 5
                + [sds((2, routed, width), BF16)] * 2,
                1,
                1,
                "middle",
                alias={14 + at: 1 + at for at in range(len(carried))},
            )(
                after(table, middles[0][7]) if middles else table,
                *mixed[stream], *w_parts, xr, by_owner(dh), by_owner(gm), gain_mlp, w_up, *carried,
            )
        )
    attn = [middles[0][0], middles[1][0]]
    left_give, left_keep, right_give, right_keep, hid = [rowed(v) for v in middles[1][1:6]]
    send, keep = [[m[at] for m in middles] for at in (6, 7)]

    first_a = after(swap(send[0], "mp", FIRST[0]), keep[1])
    ahead_a = add(keep[0][1], first_a[1])
    final_a = swap(ahead_a, "mp", FIRST[1])

    ffn_give = dot(after(left_give, ahead_a), right_give, TN).astype(BF16)
    mlp = call(
        mlp_body,
        (4,),
        [pl.BlockSpec((pair, hidden), flat), whole(w_down.shape)],
        [whole((pair, width))] * 4,
        [sds((pair, width), BF16)] * 4,
        1,
        1,
        "mlp",
    )(after(table, ffn_give), hid, w_down)
    first_b = after(swap(send[1], "mp", FIRST[1]), mlp[0])
    ahead_b = add(keep[1][1], first_b[1])
    final_b = swap(ahead_b, "mp", FIRST[0])
    ffn_keep = dot(after(left_keep, ahead_b), right_keep, TN).astype(BF16)
    ffn = Total(after(ffn_give, ahead_b), ffn_keep, bit)
    ffn_far = ffn.split(ffn_keep)
    mlp_all = [mlp[0], swap(after(mlp[1], ahead_b), "mp", 1), None, None]

    part = pl.BlockSpec((routed, width), flat)
    pieces = [
        pl.BlockSpec((1, routed, width), lambda i, w: (0, 0, 0)),
        pl.BlockSpec((1, routed, width), lambda i, w: (0, 0, 0)),
        whole((routed, width)),
    ] * 2
    rows_out = call(
        rows_pair_body,
        (2,),
        pieces + [whole((routed, width))] * 2 + [part, part, line, line] + [whole(w_out.shape)] * 4,
        [part, part, whole((8, width))] + [pl.BlockSpec((routed, wide), flat)] * 4,
        [sds((pair, width), F32), sds((pair, width), BF16), sds((8, width), F32)]
        + [sds((pair, wide), BF16)] * 4,
        1,
        1,
        "rows",
    )(
        after(table, ffn_far), keep[0], first_a, final_a, keep[1], first_b,
        final_b, *attn, xr_rows, dyr, gain_mlp, w_router, *w_parts,
    )
    dyn, ga, gain_two_part = rows_out[:3]
    dmix = [rows_out[3]] + [swap(rows_out[3 + j], "mp", j) for j in partners]

    out_specs = [
        pl.BlockSpec((routed, wide), lambda i, w, at=STREAMS[s].index(j): (at, 0))
        for s in (0, 1)
        for j in range(4)
    ]
    outs_keep, outs_give = call(
        out_grad_body,
        (1,),
        out_specs + [whole((pair, width))],
        [whole((4, wide // 2, width))] * 2,
        [sds((4, wide // 2, width), BF16)] * 2,
        1,
        1,
        "outs",
    )(after(table, ga), *mixed[0], *mixed[1], ga)
    outs_got = swap(outs_give, "dp", 1)
    dmix = [dmix[0]] + [after(value, outs_keep) for value in dmix[1:]]
    mlp_all[1] = after(mlp_all[1], *dmix[1:])
    mlp_all[2] = swap(after(mlp[2], mlp_all[1]), "mp", 2)
    mlp_all[3] = swap(after(mlp[3], mlp_all[1]), "mp", 3)
    ffn_now = ffn.cross(mlp_all[1])

    backs = []
    for stream in range(2):
        cut = pl.BlockSpec((routed, wide), lambda i, w, s=stream: (s, 0))
        carried = backs[0][:1] if backs else []
        backs.append(
            call(
                functools.partial(back_pair_body, heads, stream),
                (2,),
                [
                    pl.BlockSpec((pair, joint), flat),
                    pl.BlockSpec((pair, routed), flat),
                    pl.BlockSpec((pair, 128), flat),
                    cut,
                    cut,
                    cut,
                    cut,
                    whole(w_qkv.shape),
                ]
                + [anywhere] * len(carried),
                [
                    owner_spec(stream, routed, joint),
                    whole((2, routed, width)),
                    whole((2, routed, width)),
                ],
                [
                    held(joint),
                    sds((2, routed, width), BF16),
                    sds((2, routed, width), BF16),
                ],
                1,
                1,
                "back",
                alias={9: 0} if carried else None,
            )(
                after(table, backs[0][2]) if backs else after(table, ffn_now),
                qkv[stream], mask[stream], lse[stream], *dmix, w_qkv, *carried,
            )
        )
    dqkv = rowed(backs[1][0])
    back_send, back_keep = [[b[at] for b in backs] for at in (1, 2)]
    mlp_all[2] = after(mlp_all[2], back_keep[1])
    outs_got = after(outs_got, back_keep[1])
    qkv_give = dot(rowed(a1_give), dqkv, TN).astype(BF16)
    last_first_a = after(swap(back_send[0], "mp", FIRST[0]), qkv_give)
    last_ahead_a = add(back_keep[0][1], last_first_a[1])
    last_final_a = swap(last_ahead_a, "mp", FIRST[1])
    qkv_keep = dot(rowed(after(a1_keep, last_ahead_a)), dqkv, TN).astype(BF16)
    whole_qkv = Total(qkv_give, qkv_keep, bit)
    outs_x = add(after(outs_keep, qkv_keep)[:2], outs_got[:2])
    outs_sent = swap(outs_x, "mp", 1)
    mlp_all[3] = after(mlp_all[3], outs_x)

    upd, base, router_part = call(
        delta_pair_body,
        (2,),
        [part] * 4 + [whole((routed, width))] * 2 + [part] * 3 + [line],
        [part, part, whole((8, width))],
        [sds((pair, width), BF16), sds((pair, width), F32), sds((8, width), F32)],
        1,
        1,
        "delta",
    )(after(table, outs_x), *mlp_all, *attn, xr_rows, dyr, dyn, w_router)

    last_first_b = after(swap(back_send[1], "mp", FIRST[1]), base)
    last_ahead_b = add(back_keep[1][1], last_first_b[1])
    last_final_b = swap(last_ahead_b, "mp", FIRST[0])

    outs_sent = after(outs_sent, last_ahead_b)

    def outs_of(at, *more):
        value = outs_keep[2 + at].astype(F32) + outs_got[2 + at].astype(F32)
        for other in (outs_sent[at], *more):
            value = value + other.astype(F32)
        return value.astype(BF16)


    def put(source, parts, target, name, *others):
        return place_rows(after(table, *others), source, routes, parts, target, name)

    outs_ahead = outs_of(1)
    outs_final = swap(outs_ahead, "mp", 2)
    qkv_far = whole_qkv.split(outs_ahead)

    output = put(tokens, [(upd, 0)], None, "put_own", qkv_far)
    ffn_now = ffn.close(output)
    upd_all = [upd] + [swap(after(upd, output), "mp", j) for j in (1, 2)] + [None]
    out_half = outs_of(0, after(outs_final, ffn_now))
    last = call(
        last_pair_body,
        (3,),
        pieces
        + [pl.BlockSpec((routed, width), lambda i, w: (jnp.minimum(i, 1), 0))] * 2
        + [line]
        + [whole((8, width))] * 2
        + [whole((8, 128))] * 2,
        [part],
        [sds((pair + 16, width), BF16)],
        1,
        1,
        "last",
        scratch=[pltpu.VMEM((8, width), F32)],
    )(
        after(table, out_half), back_keep[0], last_first_a, last_final_a, back_keep[1],
        last_first_b, last_final_b, xr_rows, base, gain_attn, gain_two_part, router_part, *score,
    )[0]
    grads = put(cotangent, [(last, 0)], None, "put_own", last)
    qkv_now = whole_qkv.cross(grads)
    upd_all[1:3] = [after(value, qkv_now) for value in upd_all[1:3]]
    last_all = [last] + [swap(after(last, *upd_all[1:3]), "mp", j) for j in (1, 2)] + [None]
    upd_all[3] = swap(upd_all[1], "mp", 2)
    output = put(tokens, [(upd_all[1], 2), (upd_all[2], 4)], output, "put_out", grads)
    last_all[1:3] = [after(value, output) for value in last_all[1:3]]
    last_all[3] = swap(last_all[2], "mp", 1)
    out_sent = swap(after(out_half, *last_all[1:3]), "dp", 2)
    grads = put(cotangent, [(last_all[1], 2), (last_all[2], 4)], grads, "put_grad", qkv_now)
    upd_all[3] = after(upd_all[3], grads)
    output = put(tokens, [(upd_all[3], 6)], output, "put_out", grads)
    out_half = add(out_half, after(out_sent, output))
    out_sent = swap(out_half, "dp", 4)
    qkv_now = whole_qkv.close(out_half)
    ffn.share(qkv_now)
    last_all[3] = after(last_all[3], qkv_now)
    small = 0.0
    for rows in last_all:
        small = small + rows[pair : pair + 8].astype(F32) + rows[pair + 8 :].astype(F32)
    small_sent = swap(small, "dp", 2)
    grads = put(cotangent, [(last_all[3], 6)], grads, "put_grad", small)
    small = small + after(small_sent, grads)
    small_sent = swap(small, "dp", 4)
    side = ffn.back(small)
    ffn.pair = after(ffn.pair, side)
    whole_qkv.share(ffn.pair)
    grad_down, grad_up = join_halves(after(table, side), ffn.pieces())
    side = whole_qkv.back(grad_up)
    whole_qkv.pair = after(whole_qkv.pair, side)
    small = small + after(small_sent, whole_qkv.pair)
    small_sent = swap(small, "dp", 1)
    out_half = add(out_half, after(out_sent, small))
    out_sent = swap(out_half, "dp", 1)
    grad_qkv, grad_out = join_tail(
        after(table, out_half), whole_qkv.pieces(), [out_half, out_sent]
    )
    small = small + after(small_sent, grad_out)

    score_total = small[3, 0]
    routed_total = small[3, 128]
    token_count = seqs * length * lax.axis_size("dp")
    return (
        output,
        grads,
        small[0],
        small[1],
        small[2],
        grad_qkv,
        grad_out,
        grad_up,
        grad_down,
        routed_total / score_total,
        score_total / token_count,
    )


def shards(*arrays):
    tokens, segments, routes, w_out, w_up = (arrays[at] for at in (0, 1, 2, 8, 9))
    square = lax.axis_size("mp") == 4 and segments.shape[0] == 8 and lax.axis_size("dp") == 8
    square = square and w_up.shape[1] == tokens.shape[1] and tokens.shape[1] % 256 == 0
    if square and routes.shape[1] % 128 == 0 and w_out.shape[0] % 128 == 0:
        return paired(*arrays)
    return general(*arrays)


def solution(mesh):
    rows = P("dp", None)
    columns = P(None, "mp")
    lines = P("mp", None)
    in_specs = (rows, rows, rows, rows, P(), P(), P(), columns, lines, columns, lines)
    out_specs = (rows, rows, P(), P(), P(), columns, lines, columns, lines, P(), P())
    return jax.shard_map(shards, mesh=mesh, in_specs=in_specs, out_specs=out_specs, check_vma=False)
```

```python
import functools

import jax
import jax.numpy as jnp
from jax import lax
from jax.experimental import pallas as pl
from jax.experimental.pallas import tpu as pltpu
from jax.sharding import PartitionSpec as P

HD = 64
EPS = 1e-06
SCALE = HD ** (-0.5)
GELU_C = (2.0 / 3.141592653589793) ** 0.5
GELU_A = 0.044715
F32 = jnp.float32
BF16 = jnp.bfloat16


def dot(left, right, on=((1,), (0,))):
    return lax.dot_general(left, right, (on, ((), ())), preferred_element_type=F32)


NT = ((1,), (1,))
TN = ((0,), (0,))


def iota(shape, axis):
    return lax.broadcasted_iota(jnp.int32, shape, axis)


def sigmoid(value):
    return 1.0 / (1.0 + jnp.exp(-value))


LENGTHS = {
    "front": 5.2, "cot": 3.2, "middle": 5.5, "rows": 2.8, "outs": 3.9, "back": 1.0,
    "delta": 0.01, "mlp": 0.01, "last": 0.33, "put_own": 0.01, "put_out": 2.4, "put_grad": 2.4, "join": 1.5,
}
RATE = 4e9


def call(body, grid, in_specs, out_specs, out_shape, flops, nbytes, name, scratch=(), alias=None):
    if flops == 1:
        flops = LENGTHS[name] * grid[0] * RATE
        nbytes = 1
    return pl.pallas_call(
        body,
        grid_spec=pltpu.PrefetchScalarGridSpec(
            num_scalar_prefetch=1,
            grid=grid,
            in_specs=in_specs,
            out_specs=out_specs,
            scratch_shapes=list(scratch),
        ),
        out_shape=out_shape,
        cost_estimate=pl.CostEstimate(
            flops=int(flops), bytes_accessed=int(nbytes), transcendentals=0
        ),
        input_output_aliases=alias or {},
        name=name,
    )


def whole(shape):
    zeros = (0,) * len(shape)
    return pl.BlockSpec(shape, lambda *_: zeros)


def one_hot_rows(routes_row, length):
    routed = routes_row.shape[1]
    eye = iota((routed, routed), 0) == iota((routed, routed), 1)
    column = jnp.sum(jnp.where(eye, routes_row.astype(F32), 0.0), axis=1, keepdims=True)
    return iota((routed, length), 1) == column.astype(jnp.int32), eye


def head_mask(hot, eye, seg_line):
    seg_col = jnp.sum(jnp.where(hot, seg_line, 0.0), axis=1, keepdims=True)
    seg_row = jnp.sum(jnp.where(eye, seg_col, 0.0), axis=0, keepdims=True)
    routed = eye.shape[0]
    causal = iota((routed, routed), 0) >= iota((routed, routed), 1)
    return causal & (seg_col == seg_row)


def softmax_head(query, key, allowed):
    logits = jnp.where(allowed, dot(query, key, NT) * SCALE, -1e30)
    expon = jnp.exp(logits - jnp.max(logits, axis=1, keepdims=True))
    return expon / jnp.sum(expon, axis=1, keepdims=True)


def front_body(
    heads, slice_rows, where, tokens, routes, segments, gain, router, w_qkv,
    xr_out, a1_out, qkv_out, mask_out, mixed_out, score_out,
):
    step = pl.program_id(0)
    length = tokens.shape[0]
    hot, eye = one_hot_rows(routes[pl.ds(step, 1), :], length)
    seg_line = segments[pl.ds(step, 1), :].astype(F32)
    allowed = head_mask(hot, eye, seg_line)
    mask_out[...] = jnp.where(allowed, 1.0, 0.0).astype(BF16)
    rows = dot(jnp.where(hot, 1.0, 0.0).astype(BF16), tokens[...])
    xr_out[...] = rows.astype(BF16)
    vec = router[...].astype(F32)
    start = pl.multiple_of(where[0] * slice_rows, slice_rows)
    part = tokens[pl.ds(start, slice_rows), :].astype(F32)
    total = jnp.sum(sigmoid(jnp.sum(part * vec, axis=1, keepdims=True)), axis=0, keepdims=True)
    chosen = jnp.sum(sigmoid(jnp.sum(rows * vec, axis=1, keepdims=True)), axis=0, keepdims=True)

    @pl.when(step == 0)
    def _():
        score_out[...] = jnp.zeros_like(score_out)

    which = iota(score_out.shape, 0)
    score_out[...] += jnp.where(which == 0, total, jnp.where(which == 1, chosen, 0.0))
    inverse = lax.rsqrt(jnp.mean(rows * rows, axis=1, keepdims=True) + EPS)
    normed = (rows * inverse * gain[...].astype(F32)).astype(BF16)
    a1_out[...] = normed
    joint = dot(normed, w_qkv[...]).astype(BF16)
    qkv_out[...] = joint
    for head in range(heads):
        base = head * 3 * HD
        query = joint[:, base : base + HD]
        key = joint[:, base + HD : base + 2 * HD]
        value = joint[:, base + 2 * HD : base + 3 * HD]
        probs = softmax_head(query, key, allowed).astype(BF16)
        mixed_out[:, head * HD : (head + 1) * HD] = dot(probs, value).astype(BF16)


def cot_body(where, cotangent, routes, xr, router, w_down, dyr_out, gm_out, dh_out):
    step = pl.program_id(0)
    hot, _ = one_hot_rows(routes[pl.ds(step, 1), :], cotangent.shape[0])
    rows = dot(jnp.where(hot, 1.0, 0.0).astype(BF16), cotangent[...])
    dyr_out[...] = rows.astype(BF16)
    vec = router[...].astype(F32)
    rate = sigmoid(jnp.sum(xr[...].astype(F32) * vec, axis=1, keepdims=True))
    low = (rate * rows).astype(BF16)
    gm_out[...] = low
    dh_out[...] = dot(low, w_down[...], NT)


def middle_body(parts, table, *refs):
    mixed = refs[:parts]
    w_out, xr, dh, gain, w_up = refs[parts : parts + 5]
    attn_out, a2_out, hid_out, du_out, da2_out, gain_out = refs[parts + 5 :]
    attn = dot(mixed[0][...], w_out[0])
    for part in range(1, parts):
        attn = attn + dot(mixed[part][...], w_out[part])
    attn_out[...] = attn
    y = xr[...].astype(F32) + attn
    scaled = y * lax.rsqrt(jnp.mean(y * y, axis=1, keepdims=True) + EPS)
    a2 = (scaled * gain[...].astype(F32)).astype(BF16)
    a2_out[...] = a2
    u = dot(a2, w_up[...])
    square = u * u
    t = jnp.tanh(GELU_C * (u + GELU_A * (u * square)))
    hid_out[...] = (0.5 * u * (1.0 + t)).astype(BF16)
    slope = 0.5 * (1.0 + t) + (0.5 * GELU_C) * u * (1.0 - t * t) * (1.0 + 3.0 * GELU_A * square)
    du = (dh[...] * slope).astype(BF16)
    du_out[...] = du
    da2 = dot(du, w_up[...], NT)
    da2_out[0] = da2.astype(BF16)

    @pl.when(pl.program_id(0) == 0)
    def _():
        gain_out[...] = jnp.zeros_like(gain_out)

    gain_out[...] += jnp.sum((da2 * scaled).reshape(-1, 8, da2.shape[1]), axis=0)


def rows_body(parts, where, *refs):
    pieces = refs[:parts]
    attn, xr, dyr, gain, router, w_out = refs[parts : parts + 6]
    dyn_out, ga_out, do_out = refs[parts + 6 :]
    da2 = pieces[0][...].astype(F32)
    for piece in pieces[1:]:
        da2 = da2 + piece[...].astype(F32)
    rows = xr[...].astype(F32)
    y = rows + attn[...]
    inverse = lax.rsqrt(jnp.mean(y * y, axis=1, keepdims=True) + EPS)
    t = gain[...].astype(F32) * da2
    scaled = y * inverse
    dyn = inverse * (t - scaled * jnp.mean(t * scaled, axis=1, keepdims=True))
    dyn_out[...] = dyn
    rate = sigmoid(jnp.sum(rows * router[...].astype(F32), axis=1, keepdims=True))
    ga = (rate * dyr[...].astype(F32) + dyn).astype(BF16)
    ga_out[...] = ga
    for part in range(parts):
        do_out[part] = dot(ga, w_out[part], NT).astype(BF16)


def delta_body(parts, where, *refs):
    pieces = refs[:parts]
    attn, xr, dyr, dyn, router = refs[parts : parts + 5]
    upd_out, base_out, grad_router_out = refs[parts + 5 :]
    delta = attn[...]
    for piece in pieces:
        delta = delta + piece[...].astype(F32)
    rows = xr[...].astype(F32)
    grads = dyr[...].astype(F32)
    vec = router[...].astype(F32)
    rate = sigmoid(jnp.sum(rows * vec, axis=1, keepdims=True))
    upd_out[...] = (rows + rate * delta).astype(BF16)
    dlogit = jnp.sum(grads * delta, axis=1, keepdims=True) * rate * (1.0 - rate)
    base_out[...] = grads + dyn[...] + dlogit * vec

    @pl.when(pl.program_id(0) == 0)
    def _():
        grad_router_out[...] = jnp.zeros_like(grad_router_out)

    grad_router_out[...] += jnp.sum((dlogit * rows).reshape(-1, 8, rows.shape[1]), axis=0)


def back_body(heads, where, qkv, mask, dmixed, xr, gain, w_qkv, dqkv_out, da1_out, gain_out):
    joint = qkv[...]
    allowed = mask[...].astype(F32) > 0.5
    grads = dmixed[0]
    pieces = []
    for head in range(heads):
        base = head * 3 * HD
        query = joint[:, base : base + HD]
        key = joint[:, base + HD : base + 2 * HD]
        value = joint[:, base + 2 * HD : base + 3 * HD]
        dmix = grads[:, head * HD : (head + 1) * HD]
        probs = softmax_head(query, key, allowed)
        dprobs = dot(dmix, value, NT)
        spread = jnp.sum(probs * dprobs, axis=1, keepdims=True)
        dlog = (probs * (dprobs - spread)).astype(BF16)
        dquery = dot(dlog, key) * SCALE
        dkey = dot(dlog, query, TN) * SCALE
        dvalue = dot(probs.astype(BF16), dmix, TN)
        pieces += [dquery.astype(BF16), dkey.astype(BF16), dvalue.astype(BF16)]
    for at, piece in enumerate(pieces):
        dqkv_out[:, at * HD : (at + 1) * HD] = piece
    da1 = dot(dqkv_out[...], w_qkv[...], NT)
    da1_out[0] = da1.astype(BF16)
    rows = xr[...].astype(F32)
    scaled = rows * lax.rsqrt(jnp.mean(rows * rows, axis=1, keepdims=True) + EPS)

    @pl.when(pl.program_id(0) == 0)
    def _():
        gain_out[...] = jnp.zeros_like(gain_out)

    gain_out[...] += jnp.sum((da1 * scaled).reshape(-1, 8, da1.shape[1]), axis=0)


def last_body(parts, where, *refs):
    pieces = refs[:parts]
    xr, base, gain = refs[parts : parts + 3]
    (out,) = refs[parts + 3 :]
    da1 = pieces[0][...].astype(F32)
    for piece in pieces[1:]:
        da1 = da1 + piece[...].astype(F32)
    rows = xr[...].astype(F32)
    inverse = lax.rsqrt(jnp.mean(rows * rows, axis=1, keepdims=True) + EPS)
    t = gain[...].astype(F32) * da1
    scaled = rows * inverse
    dxn = inverse * (t - scaled * jnp.mean(t * scaled, axis=1, keepdims=True))
    out[...] = (base[...] + dxn).astype(BF16)


def put_body(where, source, routes, rows, *refs):
    out = refs[-1]
    length = source.shape[0]
    at = where[pl.program_id(0)]
    line = routes[pl.ds(at, 1), :]
    hot = iota((length, line.shape[1]), 0) == line
    picked = jnp.where(hot, 1.0, 0.0)
    taken = jnp.sum(picked, axis=1, keepdims=True) > 0.5
    moved = dot(picked.astype(BF16), rows[...])
    out[...] = jnp.where(taken, moved, source[...].astype(F32)).astype(BF16)


def put_rows(source, routes, rows, order, target, name):
    seqs, routed = routes.shape
    length = source.shape[0] // seqs
    width = source.shape[1]
    count = rows.shape[0] // routed
    in_specs = [
        pl.BlockSpec((length, width), lambda i, w: (w[i], 0)),
        whole(routes.shape),
        pl.BlockSpec((routed, width), lambda i, w: (i, 0)),
    ]
    args = [order, source, routes, rows]
    alias = None
    if target is not None:
        in_specs.append(pl.BlockSpec(memory_space=pl.ANY))
        args.append(target)
        alias = {4: 0}
    return call(
        put_body,
        (count,),
        in_specs,
        pl.BlockSpec((length, width), lambda i, w: (w[i], 0)),
        jax.ShapeDtypeStruct(source.shape, BF16),
        2 * count * length * routed * width,
        count * length * width * 4,
        name,
        alias=alias,
    )(*args)


def swap(value, axis, offset):
    size = lax.axis_size(axis)
    return lax.ppermute(value, axis, [(i, i ^ offset) for i in range(size)])


def block_of(value, index, rows):
    return lax.dynamic_slice_in_dim(value, index * rows, rows, 0)


def in_core_order(core, mine, other):
    return jnp.where(
        core == 0,
        jnp.concatenate([mine, other], axis=0),
        jnp.concatenate([other, mine], axis=0),
    )


def line_sum(value, depth):
    at = lax.axis_index("dp") // 2
    half = depth // 2

    def shift(array, pairs):
        return lax.ppermute(
            array, "dp", [(2 * a + c, 2 * b + c) for a, b in pairs for c in range(2)]
        )

    def mirrored(a, b):
        return [(a, b), (depth - 1 - a, depth - 1 - b)]

    for step in range(half - 1):
        got = shift(value, mirrored(step, step + 1))
        value = (value.astype(F32) + got.astype(F32)).astype(BF16)
    if depth > 1:
        got = shift(value, mirrored(half - 1, half))
        value = (value.astype(F32) + got.astype(F32)).astype(BF16)
    for step in reversed(range(half - 1)):
        got = shift(value, mirrored(step + 1, step))
        here = (at == step) | (at == depth - 1 - step)
        value = jnp.where(here, got, value)
    return value


def core_half(value, core):
    half = value.shape[0] // 2
    keep = block_of(value, core, half)
    give = block_of(value, 1 - core, half)
    got = swap(give.astype(BF16), "dp", 1)
    return (keep.astype(F32) + got.astype(F32)).astype(BF16)


def core_join(value, core):
    return in_core_order(core, value, swap(value, "dp", 1)).astype(F32)


def general(
    tokens, segments, routes, cotangent, gain_attn, gain_mlp, w_router, w_qkv, w_out, w_up, w_down
):
    seqs, length = segments.shape
    routed = routes.shape[1]
    width = tokens.shape[1]
    total = seqs * routed
    wide = w_out.shape[0]
    heads = wide // HD
    joint = w_qkv.shape[1]
    hidden = w_up.shape[1]
    parts = lax.axis_size("mp")
    depth = lax.axis_size("dp") // 2
    own = total // parts
    rank = lax.axis_index("mp")
    core = lax.axis_index("dp") % 2
    aligned = own % routed == 0
    per = own // routed if aligned else 1
    where = rank.reshape(1).astype(jnp.int32)
    gain_one = gain_attn.reshape(1, width)
    gain_two = gain_mlp.reshape(1, width)
    router = w_router.reshape(1, width)
    partners = list(range(1, parts))
    sds = jax.ShapeDtypeStruct

    share = block_of(w_out, core, wide // 2)
    mine = jnp.stack([swap(share, "mp", j) for j in partners])
    other = swap(mine, "dp", 1)
    w_all = jnp.where(
        core == 0,
        jnp.concatenate([mine, other], axis=1),
        jnp.concatenate([other, mine], axis=1),
    )
    w_all = jnp.concatenate([w_out[None], w_all], axis=0)

    xr, a1, qkv, mask, mixed, score = call(
        functools.partial(front_body, heads, length // parts),
        (seqs,),
        [
            pl.BlockSpec((length, width), lambda i, w: (i, 0)),
            whole(routes.shape),
            whole(segments.shape),
            whole((1, width)),
            whole((1, width)),
            whole(w_qkv.shape),
        ],
        [
            pl.BlockSpec((routed, width), lambda i, w: (i, 0)),
            pl.BlockSpec((routed, width), lambda i, w: (i, 0)),
            pl.BlockSpec((routed, joint), lambda i, w: (i, 0)),
            pl.BlockSpec((routed, routed), lambda i, w: (i, 0)),
            pl.BlockSpec((routed, wide), lambda i, w: (i, 0)),
            whole((8, 128)),
        ],
        [
            sds((total, width), BF16),
            sds((total, width), BF16),
            sds((total, joint), BF16),
            sds((total, routed), BF16),
            sds((total, wide), BF16),
            sds((8, 128), F32),
        ],
        2 * total * width * (length + joint) * 1.3,
        2 * seqs * length * width + 8 * total * width,
        "front",
    )(where, tokens, routes, segments, gain_one, router, w_qkv)

    mixed_all = [mixed] + [swap(mixed, "mp", j) for j in partners]

    dyr, gm, dh = call(
        cot_body,
        (seqs,),
        [
            pl.BlockSpec((length, width), lambda i, w: (i, 0)),
            whole(routes.shape),
            pl.BlockSpec((routed, width), lambda i, w: (i, 0)),
            whole((1, width)),
            whole(w_down.shape),
        ],
        [
            pl.BlockSpec((routed, width), lambda i, w: (i, 0)),
            pl.BlockSpec((routed, width), lambda i, w: (i, 0)),
            pl.BlockSpec((routed, hidden), lambda i, w: (i, 0)),
        ],
        [sds((total, width), BF16), sds((total, width), BF16), sds((total, hidden), F32)],
        2 * total * width * (length + hidden),
        2 * seqs * length * width + 6 * total * width + 4 * total * hidden,
        "cot",
    )(where, cotangent, routes, xr, router, w_down)

    order = partners[::-1] + [0]
    tile = min(own, 128)
    tiles = own // tile
    blocks = jnp.stack([rank ^ j for j in order])
    table = (blocks[:, None] * tiles + jnp.arange(tiles)[None, :]).reshape(-1).astype(jnp.int32)

    def by_row(i, t):
        return (t[i], 0)

    steps = parts * tiles
    attn, a2, hid, du, da2, gain_two_part = call(
        functools.partial(middle_body, parts),
        (steps,),
        [pl.BlockSpec((tile, wide), by_row)] * parts
        + [
            whole(w_all.shape),
            pl.BlockSpec((tile, width), by_row),
            pl.BlockSpec((tile, hidden), by_row),
            whole((1, width)),
            whole(w_up.shape),
        ],
        [
            pl.BlockSpec((tile, width), lambda i, t: (jnp.maximum(i - (steps - tiles), 0), 0)),
            pl.BlockSpec((tile, width), by_row),
            pl.BlockSpec((tile, hidden), by_row),
            pl.BlockSpec((tile, hidden), by_row),
            pl.BlockSpec((1, tile, width), lambda i, t: (i // tiles, i % tiles, 0)),
            whole((8, width)),
        ],
        [
            sds((own, width), F32),
            sds((total, width), BF16),
            sds((total, hidden), BF16),
            sds((total, hidden), BF16),
            sds((parts, own, width), BF16),
            sds((8, width), F32),
        ],
        2 * total * width * (parts * wide + 2 * hidden),
        total * (10 * width + 8 * hidden) + 2 * width * (hidden + parts * wide),
        "middle",
    )(table, *mixed_all, w_all, xr, dh, gain_two, w_up)

    da2_all = [da2[-1]] + [swap(da2[at], "mp", j) for at, j in enumerate(order[:-1])]

    mlp = dot(hid, w_down).astype(BF16)
    grad_up = dot(a2, du, TN).astype(BF16)
    grad_down = dot(hid, gm, TN).astype(BF16)
    mlp_all = [block_of(mlp, rank, own)] + [
        swap(block_of(mlp, rank ^ j, own), "mp", j) for j in partners
    ]

    own_tiles = lambda i, w: (w[0] * tiles + i, 0)
    flat = lambda i, w: (i, 0)
    row_block = pl.BlockSpec((tile, width), flat)
    own_block = pl.BlockSpec((tile, width), own_tiles)
    dyn, ga, dmix = call(
        functools.partial(rows_body, parts),
        (tiles,),
        [row_block] * parts
        + [row_block, own_block, own_block, whole((1, width)), whole((1, width)), whole(w_all.shape)],
        [row_block, row_block, pl.BlockSpec((parts, tile, wide), lambda i, w: (0, i, 0))],
        [sds((own, width), F32), sds((own, width), BF16), sds((parts, own, wide), BF16)],
        2 * own * width * parts * wide,
        own * width * 24 + 2 * width * width,
        "rows",
    )(where, *da2_all, attn, xr, dyr, gain_two, router, w_all)

    dmix_all = jnp.stack([dmix[0]] + [swap(dmix[j], "mp", j) for j in partners])

    upd, base, router_part = call(
        functools.partial(delta_body, parts),
        (tiles,),
        [row_block] * parts + [row_block, own_block, own_block, row_block, whole((1, width))],
        [row_block, row_block, whole((8, width))],
        [sds((own, width), BF16), sds((own, width), F32), sds((8, width), F32)],
        own * width * 20,
        own * width * 24,
        "delta",
    )(where, *mlp_all, attn, xr, dyr, dyn, router)
    upd_all = [upd] + [swap(upd, "mp", j) for j in partners]

    if aligned:
        by_owner = lambda i, w: ((i // per) ^ w[0], i % per, 0)
        da1_shape = (parts, own, width)
    else:
        dmix_all = dmix_all[jnp.arange(parts) ^ rank].reshape(1, total, wide)
        by_owner = lambda i, w: (0, i, 0)
        da1_shape = (1, total, width)
    dqkv, da1, gain_one_part = call(
        functools.partial(back_body, heads),
        (seqs,),
        [
            pl.BlockSpec((routed, joint), flat),
            pl.BlockSpec((routed, routed), flat),
            pl.BlockSpec((1, routed, wide), by_owner),
            pl.BlockSpec((routed, width), flat),
            whole((1, width)),
            whole(w_qkv.shape),
        ],
        [
            pl.BlockSpec((routed, joint), flat),
            pl.BlockSpec((1, routed, width), by_owner),
            whole((8, width)),
        ],
        [sds((total, joint), BF16), sds(da1_shape, BF16), sds((8, width), F32)],
        2 * total * width * joint * 1.5,
        total * (4 * joint + 6 * width) + 2 * width * joint,
        "back",
    )(where, qkv, mask, dmix_all, xr, gain_one, w_qkv)

    if aligned:
        da1_blocks = [da1[j] for j in range(parts)]
    else:
        da1_blocks = [block_of(da1[0], rank ^ j, own) for j in range(parts)]
    da1_all = [da1_blocks[0]] + [swap(da1_blocks[j], "mp", j) for j in partners]

    grad_qkv = dot(a1, dqkv, TN).astype(BF16)

    last = call(
        functools.partial(last_body, parts),
        (tiles,),
        [row_block] * parts + [own_block, row_block, whole((1, width))],
        row_block,
        sds((own, width), BF16),
        own * width * 20,
        own * width * 18,
        "last",
    )(where, *da1_all, xr, base, gain_one)
    last_all = [last] + [swap(last, "mp", j) for j in partners]

    def spread(source, rows_all, name):
        if not aligned:
            rows = jnp.stack(rows_all)[jnp.arange(parts) ^ rank].reshape(total, width)
            return put_rows(source, routes, rows, jnp.arange(seqs, dtype=jnp.int32), None, name)
        target = None
        for j, rows in enumerate(rows_all):
            seq = ((rank ^ j) * per + jnp.arange(per)).astype(jnp.int32)
            target = put_rows(source, routes, rows, seq, target, name)
        return target

    output = spread(tokens, upd_all, "put_out")
    grad_tokens = spread(cotangent, last_all, "put_grad")

    grad_up = core_join(line_sum(core_half(grad_up, core), depth), core)
    grad_down = core_join(line_sum(core_half(grad_down, core), depth), core)
    grad_qkv = core_join(line_sum(core_half(grad_qkv, core), depth), core)

    def out_part(j):
        rows = block_of(mixed_all[j], rank, own)
        return dot(rows, ga, TN).astype(BF16)

    outs = jnp.stack([out_part(j) for j in range(parts)], axis=1)
    outs = core_half(outs, core)
    half = outs[:, 0].astype(F32)
    for j in partners:
        half = half + swap(outs[:, j], "mp", j).astype(F32)
    grad_out = core_join(line_sum(half.astype(BF16), depth), core)

    lines = jnp.sum(
        jnp.stack([gain_one_part, gain_two_part, router_part]), axis=1
    )
    scores = jnp.concatenate(
        [score[0:1] / 1.0, score[1:2] / parts, jnp.zeros((6, 128), F32)], axis=0
    ).reshape(1, -1)
    scores = jnp.pad(scores, ((0, 0), (0, width - 1024))) if width > 1024 else scores[:, :width]
    small = jnp.concatenate([lines, scores, jnp.zeros((4, width), F32)], axis=0)
    bit = 1
    while bit < 2 * depth:
        small = small + swap(small, "dp", bit)
        bit *= 2
    bit = 1
    while bit < parts:
        small = small + swap(small, "mp", bit)
        bit *= 2
    score_total = small[3, 0]
    routed_total = small[3, 128]
    token_count = seqs * length * lax.axis_size("dp")
    return (
        output,
        grad_tokens,
        small[0],
        small[1],
        small[2],
        grad_qkv,
        grad_out,
        grad_up,
        grad_down,
        routed_total / score_total,
        score_total / token_count,
    )


STREAMS = ((1, 3, 0, 2), (2, 3, 0, 1))
FIRST = (1, 2)


def row(vector):
    return vector[...].astype(F32).reshape(1, -1)

def owner_spec(stream, rows, columns, slots=()):
    lead = tuple(slots)
    zeros = (0,) * len(lead)
    if stream == 0:
        return pl.BlockSpec(
            lead + (2, None, None, rows, columns), lambda i, w: zeros + (0, 1 - i, 0, 0, 0)
        )
    return pl.BlockSpec(
        lead + (None, 2, None, rows, columns), lambda i, w: zeros + (1 - i, 0, 1, 0, 0)
    )


def joined(value):
    return value.reshape(-1, value.shape[-1])


def parted(value):
    return value.reshape(2, -1, value.shape[-1])


def front_pair_body(heads, slice_rows, first, where, *refs):
    blocks = refs[:2]
    routes, segments, gain, router, w_qkv = refs[2:7]
    xr_out, give_out, keep_out, qkv_out, mask_out, lse_out, mixed_out, score_out = refs[-8:]
    step = pl.program_id(0)
    length, width = blocks[0].shape
    routed = routes.shape[1]
    vec = jnp.broadcast_to(row(router), (8, width)).astype(BF16)
    start = pl.multiple_of(where[RANK] * slice_rows, slice_rows)
    rows_all, allowed_all = [], []
    total = jnp.zeros((8, 1), F32)
    for at, tokens in enumerate(blocks):
        seq = where[first + 2 * step + at]
        hot, eye = one_hot_rows(routes[pl.ds(seq, 1), :], length)
        seg_line = segments[pl.ds(seq, 1), :].astype(F32)
        allowed = head_mask(hot, eye, seg_line)
        mask_out[at * routed : (at + 1) * routed, :] = jnp.where(allowed, 1.0, 0.0).astype(BF16)
        rows_all.append(dot(jnp.where(hot, 1.0, 0.0).astype(BF16), tokens[...]))
        allowed_all.append(allowed)
        scored = sigmoid(dot(vec, tokens[pl.ds(start, slice_rows), :], NT))
        total = total + jnp.sum(scored, axis=1, keepdims=True)
    rows = jnp.concatenate(rows_all, axis=0)
    low = rows.astype(BF16)
    xr_out[...] = parted(low)
    chosen = jnp.sum(sigmoid(dot(vec, low, NT)), axis=1, keepdims=True)

    @pl.when(step == 0)
    def _():
        score_out[...] = jnp.zeros_like(score_out)

    which = iota(score_out.shape, 0)
    score_out[...] += jnp.where(which == 0, total, jnp.where(which == 1, chosen, 0.0))
    inverse = lax.rsqrt(jnp.mean(rows * rows, axis=1, keepdims=True) + EPS)
    normed = (rows * inverse * row(gain)).astype(BF16)
    left, right = parted(normed[:, : width // 2]), parted(normed[:, width // 2 :])
    give_out[...] = jnp.where(where[CORE] == 0, right, left)
    keep_out[...] = jnp.where(where[CORE] == 0, left, right)
    joint = dot(normed, w_qkv[...]).astype(BF16)
    qkv_out[...] = joint
    logits = []
    for at in range(2):
        own = joint[at * routed : (at + 1) * routed]
        for head in range(heads):
            base = head * 3 * HD
            raw = dot(own[:, base : base + HD], own[:, base + HD : base + 2 * HD], NT)
            logits.append(jnp.where(allowed_all[at], raw * SCALE, -1e30))
    logits = jnp.concatenate(logits, axis=0)
    top = jnp.max(logits, axis=1, keepdims=True)
    expon = jnp.exp(logits - top)
    norm = jnp.sum(expon, axis=1, keepdims=True)
    sums = top + jnp.log(norm)
    probs = (expon * (1.0 / norm)).astype(BF16)
    for at in range(2):
        span = slice(at * routed, (at + 1) * routed)
        for head in range(heads):
            place = slice((at * heads + head) * routed, (at * heads + head + 1) * routed)
            base = head * 3 * HD
            value = joint[span, base + 2 * HD : base + 3 * HD]
            lse_out[span, head : head + 1] = sums[place]
            mixed_out[span, head * HD : (head + 1) * HD] = dot(probs[place], value).astype(BF16)


def cot_pair_body(where, *refs):
    blocks = refs[:2]
    routes, xr, router, w_down, dyr_out, gm_out, dh_out = refs[2:]
    step = pl.program_id(0)
    length = blocks[0].shape[0]
    picked = []
    for at, block in enumerate(blocks):
        hot, _ = one_hot_rows(routes[pl.ds(where[PUT + 2 * step + at], 1), :], length)
        picked.append(dot(jnp.where(hot, 1.0, 0.0).astype(BF16), block[...]))
    rows = jnp.concatenate(picked, axis=0)
    dyr_out[...] = rows.astype(BF16)
    rate = sigmoid(jnp.sum(xr[...].astype(F32) * row(router), axis=1, keepdims=True))
    low = (rate * rows).astype(BF16)
    gm_out[...] = low
    dh_out[...] = dot(low, w_down[...], NT)


def flip(value, swapped):
    half = value.shape[0] // 2
    if swapped:
        return jnp.concatenate([value[half:], value[:half]], axis=0)
    return value


def middle_pair_body(stream, where, *refs):
    mixed = refs[:4]
    w_parts = refs[4:8]
    xr, dh, gm, gain, w_up = refs[8:13]
    attn_out, left_give, left_keep, right_give, right_keep, hid_out, send_out, keep_out = refs[-8:]
    step = pl.program_id(0)
    plain = (0, FIRST[stream])
    attn = 0.0
    for part in range(4):
        attn = attn + dot(flip(mixed[part][...], part not in plain), w_parts[part][...])
    half = attn.shape[0] // 2
    attn_out[...] = attn[:half]
    y = joined(xr[...]).astype(F32) + attn
    scaled = y * lax.rsqrt(jnp.mean(y * y, axis=1, keepdims=True) + EPS)
    a2 = (scaled * row(gain)).astype(BF16)
    u = dot(a2, w_up[...])
    square = u * u
    t = jnp.tanh(u * (GELU_C + (GELU_C * GELU_A) * square))
    cdf = 0.5 + 0.5 * t
    hid = (u * cdf).astype(BF16)
    hid_out[...] = parted(hid)
    slope = cdf + (u * (1.0 - t * t)) * (0.5 * GELU_C + (1.5 * GELU_C * GELU_A) * square)
    du = (joined(dh[...]) * slope).astype(BF16)
    low = dot(du, w_up[...], NT).astype(BF16)
    first = where[CORE] == 0
    left_give[...] = parted(jnp.where(first, a2, hid))
    left_keep[...] = parted(jnp.where(first, hid, a2))
    down = joined(gm[...])
    right_give[...] = parted(jnp.where(first, du, down))
    right_keep[...] = parted(jnp.where(first, down, du))

    @pl.when(step == 0)
    def _():
        send_out[0] = low[:half]
        send_out[1] = low[half:]

    @pl.when(step == 1)
    def _():
        keep_out[0] = low[:half]
        keep_out[1] = low[half:]


def mlp_body(where, hid, w_down, *outs):
    value = dot(hid[...], w_down[...]).astype(BF16)
    for at, out in enumerate(outs):

        @pl.when(pl.program_id(0) == at)
        def _(out=out):
            out[...] = value


def either(step, left, right):
    return jnp.where(step == 0, left, right).astype(F32)


def summed(step, refs):
    keep, first, final = [
        either(step, refs[at][...], refs[3 + at][...]) for at in range(3)
    ]
    return joined(keep) + joined(first) + final


def fold(value):
    return jnp.sum(value.reshape(-1, 8, value.shape[1]), axis=0)


def collect(step, out, value):
    @pl.when(step == 0)
    def _():
        out[...] = jnp.zeros_like(out)

    out[...] += value


def rows_pair_body(where, *refs):
    step = pl.program_id(0)
    da2 = summed(step, refs[:6])
    attn_a, attn_b, xr, dyr, gain, router = refs[6:12]
    w_parts = refs[12:16]
    dyn_out, ga_out, gain_out, do_outs = refs[16], refs[17], refs[18], refs[19:]
    rows = xr[...].astype(F32)
    y = rows + either(step, attn_a[...], attn_b[...])
    inverse = lax.rsqrt(jnp.mean(y * y, axis=1, keepdims=True) + EPS)
    scaled = y * inverse
    joint = da2 * scaled
    collect(step, gain_out, fold(joint))
    vec = row(gain)
    dyn = inverse * (vec * da2 - scaled * jnp.mean(vec * joint, axis=1, keepdims=True))
    dyn_out[...] = dyn
    rate = sigmoid(jnp.sum(rows * row(router), axis=1, keepdims=True))
    ga = (rate * dyr[...].astype(F32) + dyn).astype(BF16)
    ga_out[...] = ga
    for weight, out in zip(w_parts, do_outs):
        out[...] = dot(ga, weight[...], NT).astype(BF16)


def delta_pair_body(where, *refs):
    attn_a, attn_b, xr, dyr, dyn, router = refs[4:10]
    upd_out, base_out, grad_router_out = refs[10:]
    step = pl.program_id(0)
    delta = either(step, attn_a[...], attn_b[...])
    for piece in refs[:4]:
        delta = delta + piece[...].astype(F32)
    rows = xr[...].astype(F32)
    grads = dyr[...].astype(F32)
    vec = row(router)
    rate = sigmoid(jnp.sum(rows * vec, axis=1, keepdims=True))
    upd_out[...] = (rows + rate * delta).astype(BF16)
    dlogit = jnp.sum(grads * delta, axis=1, keepdims=True) * rate * (1.0 - rate)
    base_out[...] = grads + dyn[...] + dlogit * vec
    collect(step, grad_router_out, fold(dlogit * rows))


def out_grad_body(where, *refs):
    ga, keep_out, give_out = refs[8:]
    half = keep_out.shape[1]
    grads = ga[...]
    for out, core in ((keep_out, where[CORE]), (give_out, 1 - where[CORE])):
        span = pl.ds(pl.multiple_of(core * half, half), half)
        for at, part in enumerate(STREAMS[0]):
            mixed = jnp.concatenate([refs[part][:, span], refs[4 + part][:, span]], axis=0)
            out[at] = dot(mixed, grads, TN).astype(BF16)


def back_pair_body(heads, stream, where, qkv, mask, lse, *refs):
    dmixed = refs[:4]
    w_qkv = refs[4]
    dqkv_out, send_out, keep_out = refs[-3:]
    step = pl.program_id(0)
    owners = STREAMS[stream]
    routed = mask.shape[1]
    logits, dprobs, norms, items = [], [], [], []
    for at in range(2):
        span = slice(at * routed, (at + 1) * routed)
        joint = qkv[span, :]
        allowed = mask[span, :].astype(F32) > 0.5
        grads = jnp.where(step == 0, dmixed[owners[at]][...], dmixed[owners[2 + at]][...])
        for head in range(heads):
            base = head * 3 * HD
            query = joint[:, base : base + HD]
            key = joint[:, base + HD : base + 2 * HD]
            value = joint[:, base + 2 * HD : base + 3 * HD]
            dmix = grads[:, head * HD : (head + 1) * HD]
            logits.append(jnp.where(allowed, dot(query, key, NT) * SCALE, -1e30))
            dprobs.append(dot(dmix, value, NT))
            norms.append(lse[span, head : head + 1])
            items.append((span, base, query, key, dmix))
    probs = jnp.exp(jnp.concatenate(logits, axis=0) - jnp.concatenate(norms, axis=0))
    dprobs = jnp.concatenate(dprobs, axis=0)
    spread = jnp.sum(probs * dprobs, axis=1, keepdims=True)
    dlogs = (probs * (dprobs - spread)).astype(BF16)
    probs = probs.astype(BF16)
    for at, (span, base, query, key, dmix) in enumerate(items):
        part = span.start // routed
        dlog = dlogs[at * routed : (at + 1) * routed]
        prob = probs[at * routed : (at + 1) * routed]
        dqkv_out[part, :, base : base + HD] = (dot(dlog, key) * SCALE).astype(BF16)
        dqkv_out[part, :, base + HD : base + 2 * HD] = (dot(dlog, query, TN) * SCALE).astype(BF16)
        dqkv_out[part, :, base + 2 * HD : base + 3 * HD] = dot(prob, dmix, TN).astype(BF16)
    low = dot(joined(dqkv_out[...]), w_qkv[...], NT).astype(BF16)

    @pl.when(step == 0)
    def _():
        send_out[0] = low[:routed]
        send_out[1] = low[routed:]

    @pl.when(step == 1)
    def _():
        keep_out[0] = low[:routed]
        keep_out[1] = low[routed:]


def last_pair_body(where, *refs):
    xr, base, gain, gain_two, router_part, score_a, score_b, out, gain_sum = refs[6:]
    step = pl.program_id(0)

    @pl.when(step < 2)
    def _():
        da1 = summed(step, refs[:6])
        rows = xr[...].astype(F32)
        inverse = lax.rsqrt(jnp.mean(rows * rows, axis=1, keepdims=True) + EPS)
        scaled = rows * inverse
        joint = da1 * scaled
        collect(step, gain_sum, fold(joint))
        vec = row(gain)
        dxn = inverse * (vec * da1 - scaled * jnp.mean(vec * joint, axis=1, keepdims=True))
        out[...] = (base[...] + dxn).astype(BF16)

    @pl.when(step == 2)
    def _():
        width = out.shape[1]
        scores = score_a[...] + score_b[...]
        scores = jnp.concatenate(
            [scores[0:1], scores[1:2] / 4, jnp.zeros((1, width - 256), F32)], axis=1
        )
        at = iota((16, width), 0)
        small = jnp.zeros((16, width), F32)
        lines = [gain_sum[...], gain_two[...], router_part[...]]
        lines = [jnp.sum(line, axis=0, keepdims=True) for line in lines] + [scores]
        for index, line in enumerate(lines):
            small = jnp.where(at % 8 == index, line, small)
        high = small.astype(BF16).astype(F32)
        out[:16, :] = jnp.where(at < 8, high, small - high).astype(BF16)


def place_body(starts, where, source, routes, *refs):
    rows, out = refs[: len(starts)], refs[-1]
    step = pl.program_id(0)
    line = routes[pl.ds(where[PUT + put_entry(starts, step)], 1), :]
    fresh = rows[0][...]
    for at, start in enumerate(starts):
        if at:
            fresh = jnp.where(step >= start[0], rows[at][...], fresh)
    chunk = min(256, source.shape[0])

    def place(at, carry):
        first = pl.multiple_of(at * chunk, chunk)
        hot = iota((chunk, line.shape[1]), 0) + first == line
        picked = jnp.where(hot, 1.0, 0.0)
        taken = jnp.sum(picked, axis=1, keepdims=True) > 0.5
        moved = dot(picked.astype(BF16), fresh)
        span = pl.ds(first, chunk)
        out[span, :] = jnp.where(taken, moved, source[span, :].astype(F32)).astype(BF16)
        return carry

    lax.fori_loop(0, source.shape[0] // chunk, place, 0)


def put_entry(starts, step):
    entry = starts[0][1] + step
    for first, place in starts[1:]:
        entry = jnp.where(step >= first, place + step - first, entry)
    return entry


def place_rows(table, source, routes, parts, target, name):
    seqs, routed = routes.shape
    length = source.shape[0] // seqs
    width = source.shape[1]
    starts, step = [], 0
    block = lambda i, w: (w[PUT + put_entry(starts, i)], 0)
    in_specs = [pl.BlockSpec((length, width), block), whole(routes.shape)]
    args = [table, source, routes]
    for rows, place in parts:
        per = rows.shape[0] // routed
        starts.append((step, place))
        in_specs.append(
            pl.BlockSpec(
                (routed, width),
                lambda i, w, first=step, top=per - 1: (jnp.clip(i - first, 0, top), 0),
            )
        )
        args.append(rows)
        step += per
    alias = None
    if target is not None:
        in_specs.append(pl.BlockSpec(memory_space=pl.ANY))
        alias = {len(args): 0}
        args.append(target)
    return call(
        functools.partial(place_body, tuple(starts)),
        (step,),
        in_specs,
        pl.BlockSpec((length, width), block),
        jax.ShapeDtypeStruct(source.shape, BF16),
        1,
        1,
        name,
        alias=alias,
    )(*args)


def halves_body(where, value, side, pair, corner, down_out, up_out):
    step = pl.program_id(0)
    for late, (own, other) in enumerate(((value, pair), (side, corner))):
        for core, outs in enumerate(((down_out, up_out), (up_out, down_out))):

            @pl.when((step // 2 == late) & (where[CORE] == core))
            def _(own=own, other=other, outs=outs):
                outs[0][...] = own[...].astype(F32)
                outs[1][...] = other[...].astype(F32)


def join_halves(table, pieces):
    rows, columns = pieces[0].shape
    block = (rows // 2, columns)
    early = pl.BlockSpec(block, lambda i, w: (jnp.minimum(i, 1), 0))
    late = pl.BlockSpec(block, lambda i, w: (jnp.maximum(i - 2, 0), 0))
    placed = pl.BlockSpec(block, lambda i, w: (2 * (w[BIT] ^ (i // 2)) + i % 2, 0))
    value, pair, side, corner = pieces
    return call(
        halves_body,
        (4,),
        [early, late, early, late],
        [placed, placed],
        [jax.ShapeDtypeStruct((2 * rows, columns), F32)] * 2,
        1,
        1,
        "join",
    )(table, value, side, pair, corner)


def tail_body(where, *refs):
    qkv_out, out_out = refs[-2:]
    for at in range(4):

        @pl.when(pl.program_id(0) == at)
        def _(at=at):
            qkv_out[...] = refs[at][...].astype(F32)
            if at < 2:
                out_out[...] = refs[4 + at][...].astype(F32)


def join_tail(table, pieces, outs):
    rows, columns = pieces[0].shape
    few, wide = outs[0].shape
    return call(
        tail_body,
        (4,),
        [whole((rows, columns))] * 4 + [whole((few, wide))] * 2,
        [
            pl.BlockSpec((rows, columns), lambda i, w: (w[QUARTER + i], 0)),
            pl.BlockSpec((few, wide), lambda i, w: (w[14 + jnp.minimum(i, 1)], 0)),
        ],
        [
            jax.ShapeDtypeStruct((4 * rows, columns), F32),
            jax.ShapeDtypeStruct((2 * few, wide), F32),
        ],
        1,
        1,
        "join",
    )(table, *pieces, *outs)


def after(value, *others):
    return lax.optimization_barrier((value, *others))[0]


def add(left, right):
    return (left.astype(F32) + right.astype(F32)).astype(BF16)


class Total:
    def __init__(self, give, keep, bit):
        self.keep, self.bit = keep, bit
        self.sent = swap(give, "dp", 1)

    def split(self, *others):
        got = after(self.sent, *others)
        rows = got.shape[0] // 2
        cut = lambda index: add(block_of(self.keep, index, rows), block_of(got, index, rows))
        far = cut(1 - self.bit)
        self.value = cut(self.bit)
        self.sent = swap(far, "dp", 2)
        return far

    def cross(self, *others):
        self.value = add(self.value, after(self.sent, *others))
        self.sent = swap(self.value, "dp", 4)
        return self.value

    def close(self, *others):
        self.value = add(self.value, after(self.sent, *others))
        self.sent = swap(self.value, "dp", 2)
        return self.value

    def share(self, *others):
        self.pair = swap(after(self.value, *others), "dp", 1)

    def back(self, *others):
        self.side = after(self.sent, *others)
        self.corner = swap(self.side, "dp", 1)
        return self.side

    def pieces(self):
        return [self.value, self.pair, self.side, self.corner]


OWNERS = (1, 3, 0, 2, 2, 3, 0, 1)
HALVES = (0, 0, 0, 0, 1, 1, 1, 1)
RANK, CORE, QUARTER, PUT, BIT = 8, 9, 10, 16, 24


def make_table(rank, core, bit):
    owners = jnp.array(OWNERS + (0,) * 8 + (0, 0, 1, 1, 2, 2, 3, 3, 0), jnp.int32)
    halves = jnp.array(HALVES + (0,) * 8 + (0, 1) * 4 + (0,), jnp.int32)
    at = jnp.arange(25, dtype=jnp.int32)
    table = 2 * (rank ^ owners) + halves
    quarter = at - QUARTER
    quarters = 2 * (core ^ (quarter % 2)) + (bit ^ (quarter // 2))
    table = jnp.where((at >= QUARTER) & (at < QUARTER + 4), quarters, table)
    table = jnp.where(at == 14, core, jnp.where(at == 15, 1 - core, table))
    table = jnp.where(at == BIT, bit, table)
    return jnp.where(at == RANK, rank, jnp.where(at == CORE, core, table)).astype(jnp.int32)


def paired(
    tokens, segments, routes, cotangent, gain_attn, gain_mlp, w_router, w_qkv, w_out, w_up, w_down
):
    seqs, length = segments.shape
    routed = routes.shape[1]
    width = tokens.shape[1]
    wide = w_out.shape[0]
    heads = wide // HD
    joint = w_qkv.shape[1]
    hidden = w_up.shape[1]
    rank = lax.axis_index("mp")
    core = lax.axis_index("dp") % 2
    bit = lax.axis_index("dp") // 2 % 2
    half_rows = 4 * routed
    pair = 2 * routed
    total_rows = 8 * routed
    sds = jax.ShapeDtypeStruct
    flat = lambda i, w: (i, 0)
    line = whole((width,))
    table = make_table(rank, core, bit)
    anywhere = pl.BlockSpec(memory_space=pl.ANY)
    partners = (1, 2, 3)

    def held(columns, dtype=BF16):
        return sds((2, 2, 2, routed, columns), dtype)

    def rowed(value):
        return value.reshape(total_rows, value.shape[-1])

    def by_owner(value):
        return value.reshape(2, 2, 2, routed, value.shape[-1])

    w_parts = [w_out] + [swap(w_out, "mp", j) for j in partners]

    fronts = []
    for stream in range(2):
        carried = fronts[0][:3] if fronts else []
        fronts.append(
            call(
                functools.partial(front_pair_body, heads, length // 4, 4 * stream),
                (2,),
                [
                    pl.BlockSpec((length, width), lambda i, w, s=4 * stream: (w[2 * i + s], 0)),
                    pl.BlockSpec((length, width), lambda i, w, s=4 * stream: (w[2 * i + 1 + s], 0)),
                    whole(routes.shape),
                    whole(segments.shape),
                    line,
                    line,
                    whole(w_qkv.shape),
                ]
                + [anywhere] * len(carried),
                [
                    owner_spec(stream, routed, width),
                    owner_spec(stream, routed, width // 2),
                    owner_spec(stream, routed, width // 2),
                    pl.BlockSpec((pair, joint), flat),
                    pl.BlockSpec((pair, routed), flat),
                    pl.BlockSpec((pair, 128), flat),
                    pl.BlockSpec((pair, wide), flat),
                    whole((8, 128)),
                ],
                [
                    held(width),
                    held(width // 2),
                    held(width // 2),
                    sds((half_rows, joint), BF16),
                    sds((half_rows, routed), BF16),
                    sds((half_rows, 128), F32),
                    sds((half_rows, wide), BF16),
                    sds((8, 128), F32),
                ],
                1,
                1,
                "front",
                alias={8 + at: at for at in range(len(carried))},
            )(
                after(table, fronts[0][6]) if fronts else table,
                tokens, tokens, routes, segments, gain_attn, w_router, w_qkv, *carried,
            )
        )
    xr, a1_give, a1_keep = fronts[1][:3]
    qkv, mask, lse, heads_out, score = [list(kind) for kind in zip(*[f[3:] for f in fronts])]
    xr_rows = rowed(xr)

    dyr, gm, dh = call(
        cot_pair_body,
        (4,),
        [
            pl.BlockSpec((length, width), lambda i, w: (w[PUT + 2 * i], 0)),
            pl.BlockSpec((length, width), lambda i, w: (w[PUT + 2 * i + 1], 0)),
            whole(routes.shape),
            pl.BlockSpec((pair, width), flat),
            line,
            whole(w_down.shape),
        ],
        [
            pl.BlockSpec((pair, width), flat),
            pl.BlockSpec((pair, width), flat),
            pl.BlockSpec((pair, hidden), flat),
        ],
        [
            sds((total_rows, width), BF16),
            sds((total_rows, width), BF16),
            sds((total_rows, hidden), F32),
        ],
        1,
        1,
        "cot",
    )(table, cotangent, cotangent, routes, xr_rows, w_router, w_down)

    w_parts = [w_out] + [after(weight, heads_out[1]) for weight in w_parts[1:]]
    mixed = []
    for stream in range(2):
        near, far = FIRST[stream], FIRST[1 - stream]
        rows = after(heads_out[1], *w_parts[1:]) if stream else heads_out[0]
        beside = swap(rows, "mp", near)
        across = swap(rows, "mp", far)
        came = after(beside, gm) if stream else after(beside, *w_parts[1:])
        corner = swap(came, "mp", far)
        parts = [heads_out[stream], None, None, corner]
        parts[near], parts[far] = came, across
        mixed.append(parts)

    middles = []
    for stream in range(2):
        near = FIRST[stream]
        specs = []
        for part in range(4):
            crossed = part in (near, 3)
            specs.append(
                pl.BlockSpec((pair, wide), (lambda i, w: (1 - i, 0)) if crossed else flat)
            )
        carried = middles[0][1:6] if middles else []
        middles.append(
            call(
                functools.partial(middle_pair_body, stream),
                (2,),
                specs
                + [whole(w_out.shape)] * 4
                + [
                    owner_spec(stream, routed, width),
                    owner_spec(stream, routed, hidden),
                    owner_spec(stream, routed, width),
                    line,
                    whole(w_up.shape),
                ]
                + [anywhere] * len(carried),
                [whole((routed, width))]
                + [owner_spec(stream, routed, width)] * 5
                + [whole((2, routed, width))] * 2,
                [sds((routed, width), F32)]
                + [held(width)] * 5
                + [sds((2, routed, width), BF16)] * 2,
                1,
                1,
                "middle",
                alias={14 + at: 1 + at for at in range(len(carried))},
            )(
                after(table, middles[0][7]) if middles else table,
                *mixed[stream], *w_parts, xr, by_owner(dh), by_owner(gm), gain_mlp, w_up, *carried,
            )
        )
    attn = [middles[0][0], middles[1][0]]
    left_give, left_keep, right_give, right_keep, hid = [rowed(v) for v in middles[1][1:6]]
    send, keep = [[m[at] for m in middles] for at in (6, 7)]

    first_a = after(swap(send[0], "mp", FIRST[0]), keep[1])
    ahead_a = add(keep[0][1], first_a[1])
    final_a = swap(ahead_a, "mp", FIRST[1])

    ffn_give = dot(after(left_give, ahead_a), right_give, TN).astype(BF16)
    mlp = call(
        mlp_body,
        (4,),
        [pl.BlockSpec((pair, hidden), flat), whole(w_down.shape)],
        [whole((pair, width))] * 4,
        [sds((pair, width), BF16)] * 4,
        1,
        1,
        "mlp",
    )(after(table, ffn_give), hid, w_down)
    first_b = after(swap(send[1], "mp", FIRST[1]), mlp[0])
    ahead_b = add(keep[1][1], first_b[1])
    final_b = swap(ahead_b, "mp", FIRST[0])
    ffn_keep = dot(after(left_keep, ahead_b), right_keep, TN).astype(BF16)
    ffn = Total(after(ffn_give, ahead_b), ffn_keep, bit)
    ffn_far = ffn.split(ffn_keep)
    mlp_all = [mlp[0], swap(after(mlp[1], ahead_b), "mp", 1), None, None]

    part = pl.BlockSpec((routed, width), flat)
    pieces = [
        pl.BlockSpec((1, routed, width), lambda i, w: (0, 0, 0)),
        pl.BlockSpec((1, routed, width), lambda i, w: (0, 0, 0)),
        whole((routed, width)),
    ] * 2
    rows_out = call(
        rows_pair_body,
        (2,),
        pieces + [whole((routed, width))] * 2 + [part, part, line, line] + [whole(w_out.shape)] * 4,
        [part, part, whole((8, width))] + [pl.BlockSpec((routed, wide), flat)] * 4,
        [sds((pair, width), F32), sds((pair, width), BF16), sds((8, width), F32)]
        + [sds((pair, wide), BF16)] * 4,
        1,
        1,
        "rows",
    )(
        after(table, ffn_far), keep[0], first_a, final_a, keep[1], first_b,
        final_b, *attn, xr_rows, dyr, gain_mlp, w_router, *w_parts,
    )
    dyn, ga, gain_two_part = rows_out[:3]
    dmix = [rows_out[3]] + [swap(rows_out[3 + j], "mp", j) for j in partners]

    out_specs = [
        pl.BlockSpec((routed, wide), lambda i, w, at=STREAMS[s].index(j): (at, 0))
        for s in (0, 1)
        for j in range(4)
    ]
    outs_keep, outs_give = call(
        out_grad_body,
        (1,),
        out_specs + [whole((pair, width))],
        [whole((4, wide // 2, width))] * 2,
        [sds((4, wide // 2, width), BF16)] * 2,
        1,
        1,
        "outs",
    )(after(table, ga), *mixed[0], *mixed[1], ga)
    outs_got = swap(outs_give, "dp", 1)
    dmix = [dmix[0]] + [after(value, outs_keep) for value in dmix[1:]]
    mlp_all[1] = after(mlp_all[1], *dmix[1:])
    mlp_all[2] = swap(after(mlp[2], mlp_all[1]), "mp", 2)
    mlp_all[3] = swap(after(mlp[3], mlp_all[1]), "mp", 3)
    ffn_now = ffn.cross(mlp_all[1])

    backs = []
    for stream in range(2):
        cut = pl.BlockSpec((routed, wide), lambda i, w, s=stream: (s, 0))
        carried = backs[0][:1] if backs else []
        backs.append(
            call(
                functools.partial(back_pair_body, heads, stream),
                (2,),
                [
                    pl.BlockSpec((pair, joint), flat),
                    pl.BlockSpec((pair, routed), flat),
                    pl.BlockSpec((pair, 128), flat),
                    cut,
                    cut,
                    cut,
                    cut,
                    whole(w_qkv.shape),
                ]
                + [anywhere] * len(carried),
                [
                    owner_spec(stream, routed, joint),
                    whole((2, routed, width)),
                    whole((2, routed, width)),
                ],
                [
                    held(joint),
                    sds((2, routed, width), BF16),
                    sds((2, routed, width), BF16),
                ],
                1,
                1,
                "back",
                alias={9: 0} if carried else None,
            )(
                after(table, backs[0][2]) if backs else after(table, ffn_now),
                qkv[stream], mask[stream], lse[stream], *dmix, w_qkv, *carried,
            )
        )
    dqkv = rowed(backs[1][0])
    back_send, back_keep = [[b[at] for b in backs] for at in (1, 2)]
    mlp_all[2] = after(mlp_all[2], back_keep[1])
    outs_got = after(outs_got, back_keep[1])
    qkv_give = dot(rowed(a1_give), dqkv, TN).astype(BF16)
    last_first_a = after(swap(back_send[0], "mp", FIRST[0]), qkv_give)
    last_ahead_a = add(back_keep[0][1], last_first_a[1])
    last_final_a = swap(last_ahead_a, "mp", FIRST[1])
    qkv_keep = dot(rowed(after(a1_keep, last_ahead_a)), dqkv, TN).astype(BF16)
    whole_qkv = Total(qkv_give, qkv_keep, bit)
    outs_x = add(after(outs_keep, qkv_keep)[:2], outs_got[:2])
    outs_sent = swap(outs_x, "mp", 1)
    mlp_all[3] = after(mlp_all[3], outs_x)

    upd, base, router_part = call(
        delta_pair_body,
        (2,),
        [part] * 4 + [whole((routed, width))] * 2 + [part] * 3 + [line],
        [part, part, whole((8, width))],
        [sds((pair, width), BF16), sds((pair, width), F32), sds((8, width), F32)],
        1,
        1,
        "delta",
    )(after(table, outs_x), *mlp_all, *attn, xr_rows, dyr, dyn, w_router)

    last_first_b = after(swap(back_send[1], "mp", FIRST[1]), base)
    last_ahead_b = add(back_keep[1][1], last_first_b[1])
    last_final_b = swap(last_ahead_b, "mp", FIRST[0])

    outs_sent = after(outs_sent, last_ahead_b)

    def outs_of(at, *more):
        value = outs_keep[2 + at].astype(F32) + outs_got[2 + at].astype(F32)
        for other in (outs_sent[at], *more):
            value = value + other.astype(F32)
        return value.astype(BF16)


    def put(source, parts, target, name, *others):
        return place_rows(after(table, *others), source, routes, parts, target, name)

    outs_ahead = outs_of(1)
    outs_final = swap(outs_ahead, "mp", 2)
    qkv_far = whole_qkv.split(outs_ahead)

    output = put(tokens, [(upd, 0)], None, "put_own", qkv_far)
    ffn_now = ffn.close(output)
    upd_all = [upd] + [swap(after(upd, output), "mp", j) for j in (1, 2)] + [None]
    out_half = outs_of(0, after(outs_final, ffn_now))
    last = call(
        last_pair_body,
        (3,),
        pieces
        + [pl.BlockSpec((routed, width), lambda i, w: (jnp.minimum(i, 1), 0))] * 2
        + [line]
        + [whole((8, width))] * 2
        + [whole((8, 128))] * 2,
        [part],
        [sds((pair + 16, width), BF16)],
        1,
        1,
        "last",
        scratch=[pltpu.VMEM((8, width), F32)],
    )(
        after(table, out_half), back_keep[0], last_first_a, last_final_a, back_keep[1],
        last_first_b, last_final_b, xr_rows, base, gain_attn, gain_two_part, router_part, *score,
    )[0]
    grads = put(cotangent, [(last, 0)], None, "put_own", last)
    qkv_now = whole_qkv.cross(grads)
    upd_all[1:3] = [after(value, qkv_now) for value in upd_all[1:3]]
    last_all = [last] + [swap(after(last, *upd_all[1:3]), "mp", j) for j in (1, 2)] + [None]
    upd_all[3] = swap(upd_all[1], "mp", 2)
    output = put(tokens, [(upd_all[1], 2), (upd_all[2], 4)], output, "put_out", grads)
    last_all[1:3] = [after(value, output) for value in last_all[1:3]]
    last_all[3] = swap(last_all[2], "mp", 1)
    out_sent = swap(after(out_half, *last_all[1:3]), "dp", 2)
    grads = put(cotangent, [(last_all[1], 2), (last_all[2], 4)], grads, "put_grad", qkv_now)
    upd_all[3] = after(upd_all[3], grads)
    output = put(tokens, [(upd_all[3], 6)], output, "put_out", grads)
    out_half = add(out_half, after(out_sent, output))
    out_sent = swap(out_half, "dp", 4)
    qkv_now = whole_qkv.close(out_half)
    ffn.share(qkv_now)
    last_all[3] = after(last_all[3], qkv_now)
    small = 0.0
    for rows in last_all:
        small = small + rows[pair : pair + 8].astype(F32) + rows[pair + 8 :].astype(F32)
    small_sent = swap(small, "dp", 2)
    grads = put(cotangent, [(last_all[3], 6)], grads, "put_grad", small)
    small = small + after(small_sent, grads)
    small_sent = swap(small, "dp", 4)
    side = ffn.back(small)
    ffn.pair = after(ffn.pair, side)
    whole_qkv.share(ffn.pair)
    grad_down, grad_up = join_halves(after(table, side), ffn.pieces())
    side = whole_qkv.back(grad_up)
    whole_qkv.pair = after(whole_qkv.pair, side)
    small = small + after(small_sent, whole_qkv.pair)
    small_sent = swap(small, "dp", 1)
    out_half = add(out_half, after(out_sent, small))
    out_sent = swap(out_half, "dp", 1)
    grad_qkv, grad_out = join_tail(
        after(table, out_half), whole_qkv.pieces(), [out_half, out_sent]
    )
    small = small + after(small_sent, grad_out)

    score_total = small[3, 0]
    routed_total = small[3, 128]
    token_count = seqs * length * lax.axis_size("dp")
    return (
        output,
        grads,
        small[0],
        small[1],
        small[2],
        grad_qkv,
        grad_out,
        grad_up,
        grad_down,
        routed_total / score_total,
        score_total / token_count,
    )


def shards(*arrays):
    tokens, segments, routes, w_out, w_up = (arrays[at] for at in (0, 1, 2, 8, 9))
    square = lax.axis_size("mp") == 4 and segments.shape[0] == 8 and lax.axis_size("dp") == 8
    square = square and w_up.shape[1] == tokens.shape[1] and tokens.shape[1] % 256 == 0
    if square and routes.shape[1] % 128 == 0 and w_out.shape[0] % 128 == 0:
        return paired(*arrays)
    return general(*arrays)


def solution(mesh):
    rows = P("dp", None)
    columns = P(None, "mp")
    lines = P("mp", None)
    in_specs = (rows, rows, rows, rows, P(), P(), P(), columns, lines, columns, lines)
    out_specs = (rows, rows, P(), P(), P(), columns, lines, columns, lines, P(), P())
    return jax.shard_map(shards, mesh=mesh, in_specs=in_specs, out_specs=out_specs, check_vma=False)
```
